128 devices in a mesh: gx: 32 (over x, y, core), gy: 4 (over z).
Axes of the slice: x: 4, y: 4, z: 4, core: 2. Of those that a mesh axis runs over, the one named last changes fastest.
Arguments:
- populations: float32 [19, 128, 128, 256], P(None, 'gx', 'gy'), may hold values from 0.6 to 1.4
- relax_rates: float32 [19], replicated, may hold values from 0.8 to 1.9
- velocity: float32 [3, 65536], P(None, ('gx', 'gy')), may hold values from -0.2 to 0.2
- velocity_change: float32 [3, 65536], P(None, ('gx', 'gy')), may hold values from -0.16 to 0.16
- fractions: float32 [27, 65536], P(None, ('gx', 'gy')), may hold values from 0.05 to 0.5
- anchor: int32 [65536], P(('gx', 'gy')), may hold values from 8449 to 24318, as said below
- destination: int32 [65536], P(('gx', 'gy')), may hold values from 0 to 9, as said below
Outputs:
- advanced: float32 [19, 128, 128, 256], P(None, 'gx', 'gy')
The draws below stay inside these ranges and needn't reach their ends.
Inputs may be any that keep to these rules, and one draw needn't show every extreme that they name: `destination`: empty rows (9) carry no particle. Every brick sends exactly 4 particles to each of its 8 neighbouring bricks that lie inside the grid across the bed (gy index within 0 to 3; along gx the neighbours wrap around); the rest of the occupied rows stay (4); brick rows at gy index q hold 512 // 2^q occupied rows. Each anchor lies at least one cell inside its destination brick along x, y and z, so that the whole correlation cube lies in that brick.
All inputs are finite; a program needn't handle non-finite values.
Results may differ from the reference program's by a relative error of at most 0.0001.
Values sent between devices are 32-bit elements; how exact they have to be, the bound alone decides.
A program may use at most 128 MiB of HBM per device.

```python
import math
import jax
import jax.numpy as jnp
import numpy as np
from jax import lax

CX = 4
CY = 32
CZ = 256
PSLOT = 512
CAP = 4
STEPS = 2
NX = 128
NY = 128
NZ = 256
BANDS = 4
PROWS = 65536
N_GX = 32
N_GY = 4


def draw_anchor(key, part):
    key_x, key_y, key_z = jax.random.split(key, 3)
    along_x = jax.random.randint(key_x, (PROWS,), 1, CX - 1)
    along_y = jax.random.randint(key_y, (PROWS,), 1, CY - 1)
    along_z = jax.random.randint(key_z, (PROWS,), 1, CZ - 1)
    return ((along_x * CY + along_y) * CZ + along_z).astype(jnp.int32)


def draw_destination(key, part):
    group_codes = jnp.array([0, 1, 2, 3, 5, 6, 7, 8], jnp.int32)
    position = jnp.arange(PSLOT, dtype=jnp.int32)

    def one_block(block_key, device):
        level = device % BANDS
        live_rows = jnp.right_shift(jnp.int32(PSLOT), level)
        group = jnp.minimum(position // CAP, 7)
        code_value = group_codes[group]
        across = code_value % 3 - 1
        valid = (position < 8 * CAP) & (level + across >= 0) & (level + across < BANDS)
        labels = jnp.where(valid, code_value, jnp.where(position < live_rows, 4, 9)).astype(jnp.int32)
        order = jax.random.permutation(block_key, PSLOT)
        return labels[order]
    block_count = PROWS // PSLOT
    block_keys = jax.random.split(key, block_count)
    blocks = jax.vmap(one_block)(block_keys, jnp.arange(block_count, dtype=jnp.int32))
    return blocks.reshape(-1).astype(jnp.int32)


def shard_levels(own_key, dims, shards, smallest, largest):
    def one(dim, shards_of):
        heights = jax.random.uniform(jax.random.fold_in(jax.random.fold_in(own_key, 6), dim), (shards_of,), jnp.float32, smallest / len(shards), largest / len(shards))
        return jnp.repeat(jnp.exp(heights), dims[dim] // shards_of).reshape((-1,) + (1,) * (len(dims) - dim - 1))

    factor_of = one(*shards[0])
    for cut in shards[1:]:
        factor_of = factor_of * one(*cut)
    return factor_of


def noise(key, extent, spread, limit, cuts=(), held_as=jnp.bfloat16):
    result = spread * jax.random.normal(key, extent, jnp.float32)
    if cuts:
        result = result * shard_levels(key, extent, cuts, -0.22, 0.18)
    return jnp.clip(result, -limit, limit).astype(held_as)


def setup_inputs(seed: int = 0) -> dict:
    key_list = jax.random.split(jax.random.key(seed), 8)
    return {
        "populations": jnp.clip(0.6 + 0.79999995 * jax.random.uniform(key_list[0], (19, NX, NY, NZ), jnp.float32) ** shard_levels(key_list[0], (19, NX, NY, NZ), ((1, 32), (2, 4)), -0.2, 0.2), 0.6, 1.4),
        "relax_rates": jnp.clip(jnp.exp(jax.random.uniform(key_list[1], (19,), jnp.float32, math.log(0.8), math.log(1.9))), 0.8, 1.9),
        "velocity": noise(key_list[2], (3, PROWS), 0.05, 0.2, ((1, 128),), jnp.float32),
        "velocity_change": noise(key_list[3], (3, PROWS), 0.04, 0.16, ((1, 128),), jnp.float32),
        "fractions": jnp.clip(0.05 + 0.45 * jax.random.uniform(key_list[4], (27, PROWS), jnp.float32) ** shard_levels(key_list[4], (27, PROWS), ((1, 128),), -0.2, 0.2), 0.05, 0.5),
        "anchor": draw_anchor(jax.random.fold_in(key_list[7], 71), 0),
        "destination": draw_destination(jax.random.fold_in(key_list[7], 71), 0),
    }


def lattice():
    vectors = [[0, 0, 0]]
    for axis_one in range(3):
        for orient in (1, -1):
            vector_one = [0, 0, 0]
            vector_one[axis_one] = orient
            vectors.append(vector_one)
    for axis_one, axis_two in ((0, 1), (0, 2), (1, 2)):
        for orient in (1, -1):
            for second in (1, -1):
                vector_one = [0, 0, 0]
                vector_one[axis_one] = orient
                vector_one[axis_two] = second
                vectors.append(vector_one)
    integral = np.array(vectors)
    speeds = integral * 1.0
    length = (speeds ** 2).sum(axis=1)
    weights = np.where(length == 0, 1.0 / 3.0, np.where(length == 1, 1.0 / 18.0, 1.0 / 36.0))
    opposite = np.array([vectors.index([0 - component for component in vector_one]) for vector_one in vectors])
    along_x, along_y, along_z = (speeds[:, 0], speeds[:, 1], speeds[:, 2])
    rows_list = [np.ones(19), along_x, along_y, along_z, length, 3 * along_x ** 2 - length, along_y ** 2 - along_z ** 2, along_x * along_y, along_y * along_z, along_x * along_z, along_x * length, along_y * length, along_z * length, along_x * (along_y ** 2 - along_z ** 2), along_y * (along_z ** 2 - along_x ** 2), along_z * (along_x ** 2 - along_y ** 2), length ** 2, (3 * along_x ** 2 - length) * length, (along_y ** 2 - along_z ** 2) * length]
    basis_rows = []
    for candidate in rows_list:
        for earlier in basis_rows:
            candidate = candidate - np.dot(candidate, earlier) * earlier
        basis_rows.append(candidate / np.sqrt(np.dot(candidate, candidate)))
    basis = np.array(basis_rows)
    return (speeds, weights, opposite, basis, integral)

def tables():
    speeds, weights, opposite, basis, integral = lattice()
    lattice_vel = jnp.asarray(speeds, jnp.float32)
    moment_rows = jnp.asarray(np.concatenate([weights[None, :], (weights[:, None] * speeds).T], axis=0), jnp.float32)
    to_moments = jnp.asarray(basis * weights[None, :], jnp.float32)
    from_moments = jnp.asarray(basis.T / weights[:, None], jnp.float32)
    return (lattice_vel, moment_rows, to_moments, from_moments, opposite, integral)

def equilibrium(density, flow, lattice_vel):
    projected = jnp.dot(lattice_vel, flow, precision=lax.Precision.HIGHEST)
    speed_sq = lax.optimization_barrier(jnp.sum(flow * flow, axis=0))
    return density[None, :] * (1.0 + 3.0 * projected + 4.5 * projected * projected - 1.5 * speed_sq[None, :])

def collide(states, solid_part, solid_flow, relax_rates, packed):
    lattice_vel, moment_rows, to_moments, from_moments, opposite = packed
    moments = jnp.dot(moment_rows, states, precision=lax.Precision.HIGHEST)
    density = moments[0]
    flow = moments[1:] / density[None, :]
    fluid_eq = equilibrium(density, flow, lattice_vel)
    solid_eq = equilibrium(density, solid_flow, lattice_vel)
    off_eq = states - fluid_eq
    projected = jnp.dot(to_moments, off_eq, precision=lax.Precision.HIGHEST)
    relaxed = jnp.dot(from_moments, relax_rates[:, None] * projected, precision=lax.Precision.HIGHEST)
    bounce = states[opposite] - fluid_eq[opposite] - (states - solid_eq)
    return states - (1.0 - solid_part)[None, :] * relaxed + solid_part[None, :] * bounce

def reference(populations, relax_rates, velocity, velocity_change, fractions, anchor, destination):
    lattice_vel, moment_rows, to_moments, from_moments, opposite, speeds = tables()
    packed = (lattice_vel, moment_rows, to_moments, from_moments, opposite)
    new_velocity = velocity + velocity_change
    owner = jnp.arange(PROWS, dtype=jnp.int32) // PSLOT
    owner_x = owner // N_GY
    owner_y = owner % N_GY
    target_x = (owner_x + destination // 3 - 1) % N_GX
    target_y = owner_y + destination % 3 - 1
    keep = (destination == 4) | (destination < 9) & (destination != 4)
    centre_x = target_x * CX + anchor // (CY * CZ)
    centre_y = target_y * CY + anchor // CZ % CY
    centre_z = anchor % CZ
    cube = jnp.arange(27, dtype=jnp.int32)[:, None]
    flat = ((centre_x[None, :] + cube // 9 - 1) * NY + centre_y[None, :] + cube // 3 % 3 - 1) * NZ + centre_z[None, :] + cube % 3 - 1
    cells = NX * NY * NZ
    flat = jnp.clip(flat, 0, cells - 1).reshape(-1)
    shares = jnp.where(keep[None, :], fractions, jnp.float32(0.0))
    solid_sum = jnp.zeros((cells,), jnp.float32).at[flat].add(shares.reshape(-1))
    momentum = jnp.zeros((3, cells), jnp.float32).at[:, flat].add((shares[None, :, :] * new_velocity[:, None, :]).reshape(3, -1))
    solid = jnp.minimum(solid_sum, 1.0)
    solid_velocity = momentum / (solid_sum + 1e-06)[None, :]
    solid_slabs = solid.reshape(NX, NY * NZ)
    velocity_slabs = jnp.moveaxis(solid_velocity.reshape(3, NX, NY * NZ), 1, 0)
    coord_y = jnp.arange(NY, dtype=jnp.int32)[None, :, None]
    states = populations
    for sweep_number in range(STEPS):
        slabs = jnp.moveaxis(states, 1, 0).reshape(NX, 19, NY * NZ)
        post = lax.map(lambda slab_args: collide(slab_args[0], slab_args[1], slab_args[2], relax_rates, packed), (slabs, solid_slabs, velocity_slabs))
        post = jnp.moveaxis(post.reshape(NX, 19, NY, NZ), 0, 1)
        read = []
        for number in range(19):
            shift_x, shift_y, shift_z = (int(speeds[number, 0]), int(speeds[number, 1]), int(speeds[number, 2]))
            pulled = jnp.roll(post[number], (shift_x, shift_y, shift_z), (0, 1, 2))
            if shift_y == 1:
                pulled = jnp.where(coord_y == 0, post[opposite[number]], pulled)
            elif shift_y == -1:
                pulled = jnp.where(coord_y == NY - 1, post[opposite[number]], pulled)
            read.append(pulled)
        states = jnp.stack(read, axis=0)
    return states
```

```python
import functools

import jax
import jax.numpy as jnp
import numpy as np
from jax import lax
from jax.experimental import pallas as pl
from jax.experimental.pallas import tpu as pltpu
from jax.sharding import PartitionSpec as P

CAP = 4
MESH = pl.DeviceIdType.MESH
F32 = jnp.float32
BF16 = jnp.bfloat16
AXIS_PAIRS = ((0, 1), (0, 2), (1, 2))
SIDES = ((-1, -1), (-1, 0), (-1, 1), (0, -1), (0, 1), (1, -1), (1, 0), (1, 1))
PAD = 8


def lattice():
    vectors = [(0, 0, 0)]
    for axis_one in range(3):
        for orient in (1, -1):
            vector_one = [0, 0, 0]
            vector_one[axis_one] = orient
            vectors.append(tuple(vector_one))
    for axis_one, axis_two in AXIS_PAIRS:
        for orient in (1, -1):
            for second in (1, -1):
                vector_one = [0, 0, 0]
                vector_one[axis_one] = orient
                vector_one[axis_two] = second
                vectors.append(tuple(vector_one))
    return vectors


VEL = lattice()
INDEX = {vector: number for number, vector in enumerate(VEL)}
OPP = [INDEX[tuple(-part for part in vector)] for vector in VEL]
PLACES = (
    [number for number in range(19) if VEL[number][0] == 1]
    + [number for number in range(19) if VEL[number][0] == -1]
    + [number for number in range(19) if VEL[number][0] == 0]
)
SLOT = {number: place for place, number in enumerate(PLACES)}
UP = [number for number in range(19) if VEL[number][1] == 1]
DOWN = [number for number in range(19) if VEL[number][1] == -1]


def relaxation_terms():
    speeds = np.array(VEL) * 1.0
    length = (speeds**2).sum(axis=1)
    weights = np.where(length == 0, 1.0 / 3.0, np.where(length == 1, 1.0 / 18.0, 1.0 / 36.0))
    along_x, along_y, along_z = (speeds[:, 0], speeds[:, 1], speeds[:, 2])
    rows_list = [
        np.ones(19),
        along_x,
        along_y,
        along_z,
        length,
        3 * along_x**2 - length,
        along_y**2 - along_z**2,
        along_x * along_y,
        along_y * along_z,
        along_x * along_z,
        along_x * length,
        along_y * length,
        along_z * length,
        along_x * (along_y**2 - along_z**2),
        along_y * (along_z**2 - along_x**2),
        along_z * (along_x**2 - along_y**2),
        length**2,
        (3 * along_x**2 - length) * length,
        (along_y**2 - along_z**2) * length,
    ]
    basis_rows = []
    for candidate in rows_list:
        for earlier in basis_rows:
            candidate = candidate - np.dot(candidate, earlier) * earlier
        basis_rows.append(candidate / np.sqrt(np.dot(candidate, candidate)))
    basis = np.array(basis_rows)

    means = np.zeros((19, 19))
    means[0, 0] = 1.0
    for number, vector in enumerate(VEL):
        used = [axis for axis in range(3) if vector[axis]]
        if len(used) == 1:
            axis = used[0]
            means[1 + axis, number] = 0.5
            means[7 + axis, number] = 0.5 * vector[axis]
        elif len(used) == 2:
            pair = AXIS_PAIRS.index(tuple(used))
            one, two = vector[used[0]], vector[used[1]]
            means[4 + pair, number] = 0.25
            means[10 + 2 * pair, number] = 0.25 * one
            means[11 + 2 * pair, number] = 0.25 * two
            means[16 + pair, number] = 0.25 * one * two
    combine = np.zeros((19, 19))
    entries = [
        {0: 1},
        {1: 1, 2: 1, 3: 1},
        {4: 1, 5: 1, 6: 1},
        {1: 2, 2: -1, 3: -1},
        {4: 1, 5: 1, 6: -2},
        {2: 1, 3: -1},
        {4: 1, 5: -1},
        {7: 1},
        {10: 1, 12: 1},
        {10: 1, 12: -1},
        {8: 1},
        {11: 1, 14: 1},
        {11: 1, 14: -1},
        {9: 1},
        {13: 1, 15: 1},
        {13: 1, 15: -1},
        {16: 1},
        {17: 1},
        {18: 1},
    ]
    for row_number, entry in enumerate(entries):
        for column, factor in entry.items():
            combine[row_number, column] = factor
    scale = np.array(
        [1, 1 / 3, 1 / 3, 1 / 6, 1 / 6, 0.5, 0.5]
        + [1, 0.5, 0.5] * 3
        + [1, 1, 1]
    )
    to_symmetric = combine @ means
    back = np.linalg.inv(to_symmetric)
    terms = {}
    for rate in range(19):
        part = (
            scale[:, None]
            * to_symmetric
            @ np.diag(1.0 / weights)
            @ np.outer(basis[rate], basis[rate])
            @ np.diag(weights)
            @ back
        )
        for row_number in range(19):
            for column in range(19):
                if abs(part[row_number, column]) > 1e-9:
                    terms.setdefault((row_number, column), []).append(
                        (rate, float(part[row_number, column]))
                    )
    return terms


TERMS = relaxation_terms()
ENTRY = {where: number for number, where in enumerate(sorted(TERMS))}


def to_means(value):
    mean = [None] * 19
    mean[0] = value[0]
    for axis in range(3):
        ahead, behind = value[1 + 2 * axis], value[2 + 2 * axis]
        mean[1 + axis] = 0.5 * (ahead + behind)
        mean[7 + axis] = 0.5 * (ahead - behind)
    for pair in range(3):
        pp, pm, mp, mm = value[7 + 4 * pair : 11 + 4 * pair]
        even_one, odd_one = (pp + mm), (pp - mm)
        even_two, odd_two = (pm + mp), (pm - mp)
        mean[4 + pair] = 0.25 * (even_one + even_two)
        mean[16 + pair] = 0.25 * (even_one - even_two)
        mean[10 + 2 * pair] = 0.25 * (odd_one + odd_two)
        mean[11 + 2 * pair] = 0.25 * (odd_one - odd_two)
    return mean


def from_means(mean):
    value = [None] * 19
    value[0] = mean[0]
    for axis in range(3):
        value[1 + 2 * axis] = mean[1 + axis] + mean[7 + axis]
        value[2 + 2 * axis] = mean[1 + axis] - mean[7 + axis]
    for pair in range(3):
        even_one = mean[4 + pair] + mean[16 + pair]
        even_two = mean[4 + pair] - mean[16 + pair]
        odd_one = mean[10 + 2 * pair] + mean[11 + 2 * pair]
        odd_two = mean[10 + 2 * pair] - mean[11 + 2 * pair]
        value[7 + 4 * pair] = even_one + odd_one
        value[8 + 4 * pair] = even_two + odd_two
        value[9 + 4 * pair] = even_two - odd_two
        value[10 + 4 * pair] = even_one - odd_one
    return value


def equilibrium_means(density, impulse, triple):
    half = [0.5 * part for part in triple]
    square = [impulse[axis] * half[axis] for axis in range(3)]
    rest = density - (square[0] + square[1] + square[2]) * (1.0 / 3.0)
    axes = [rest + square[axis] for axis in range(3)]
    mean = [rest] + axes
    mean += [axes[one] + square[two] for one, two in AXIS_PAIRS]
    mean += list(impulse)
    for one, two in AXIS_PAIRS:
        mean += [impulse[one], impulse[two]]
    mean += [impulse[one] * triple[two] for one, two in AXIS_PAIRS]
    return mean


def relax_means(off, coefficient):
    plus = [None] * 19
    plus[0] = off[0]
    pair_sum = off[2] + off[3]
    plus[1] = off[1] + pair_sum
    plus[3] = off[1] + off[1] - pair_sum
    plus[5] = off[2] - off[3]
    pair_sum = off[4] + off[5]
    plus[2] = pair_sum + off[6]
    plus[4] = pair_sum - (off[6] + off[6])
    plus[6] = off[4] - off[5]
    for axis, (one, two) in enumerate(((10, 12), (11, 14), (13, 15))):
        plus[7 + 3 * axis] = off[7 + axis]
        plus[8 + 3 * axis] = off[one] + off[two]
        plus[9 + 3 * axis] = off[one] - off[two]
    plus[16:19] = off[16:19]
    made = []
    for row_number in range(19):
        total = None
        for column in range(19):
            if (row_number, column) in ENTRY:
                term = coefficient(ENTRY[row_number, column]) * plus[column]
                total = term if total is None else total + term
        made.append(total)
    out = [None] * 19
    out[0] = made[0]
    lower = made[1] - made[3]
    out[1] = made[1] + (made[3] + made[3])
    out[2] = lower + made[5]
    out[3] = lower - made[5]
    upper = made[2] + made[4]
    out[4] = upper + made[6]
    out[5] = upper - made[6]
    out[6] = made[2] - (made[4] + made[4])
    for axis, (one, two) in enumerate(((10, 12), (11, 14), (13, 15))):
        out[7 + axis] = made[7 + 3 * axis]
        out[one] = made[8 + 3 * axis] + made[9 + 3 * axis]
        out[two] = made[8 + 3 * axis] - made[9 + 3 * axis]
    out[16:19] = made[16:19]
    return out


def collide(value, solid, solid_triple, coefficient):
    mean = to_means(value)
    ninth, third = 1.0 / 9.0, 1.0 / 3.0
    density = mean[0] * third + (
        (mean[1] + mean[2]) + (mean[3] + mean[4]) + (mean[5] + mean[6])
    ) * ninth
    impulse = [
        (mean[7 + axis] + (mean[one] + mean[two])) * third
        for axis, (one, two) in enumerate(((10, 12), (11, 14), (13, 15)))
    ]
    inverse = 1.0 / density
    triple = [part * inverse for part in impulse]
    fluid = equilibrium_means(density, impulse, triple)
    wall = equilibrium_means(density, [density * part for part in solid_triple], solid_triple)
    off = [mean[number] - fluid[number] for number in range(19)]
    relaxed = relax_means(off, coefficient)
    fluid_part = 1.0 - solid
    post = []
    for number in range(19):
        odd = 7 <= number < 16
        bounced = wall[number] - off[number] if odd else wall[number] + off[number]
        post.append(fluid_part * (mean[number] - relaxed[number]) + solid * bounced)
    return from_means(post)


def main_kernel(
    sizes, rates, velocity, change, fractions, anchor, destination, populations, sent2,
    start, sent1, coef, payload, outbox, inbox, values, spread, across, solids,
    rows_out, rows_in, ends_out, ends_in,
    load_sem, mail_send, mail_recv, halo_send, halo_recv,
):
    size_x, size_y, size_z, table = sizes
    tiles = size_y // 8
    me_x, me_y = lax.axis_index("gx"), lax.axis_index("gy")
    count_x, count_y = lax.axis_size("gx"), lax.axis_size("gy")

    def there(side):
        return side[1] == 0 or (me_y < count_y - 1 if side[1] > 0 else me_y > 0)

    def device(side):
        return (lax.rem(me_x + side[0] + count_x, count_x), me_y + side[1])

    def when_there(side, act):
        if side[1] == 0:
            act()
        else:
            pl.when(there(side))(act)

    load = pltpu.make_async_copy(populations, start, load_sem)
    load.start()
    inbox[...] = jnp.zeros_like(inbox)

    barrier = pltpu.get_barrier_semaphore()
    for side in SIDES:
        def greet(side=side):
            pl.semaphore_signal(barrier, inc=1, device_id=device(side), device_id_type=MESH)
        when_there(side, greet)

    place = anchor[...]
    place_x = lax.shift_right_logical(place, 13)
    place_y = lax.bitwise_and(lax.shift_right_logical(place, 8), 31)
    place_z = lax.bitwise_and(place, 255)
    moved = velocity[...] + change[...]
    payload[...] = jnp.zeros_like(payload)
    payload[0:3, :] = moved
    payload[3:4, :] = place_x.astype(F32)
    payload[4:5, :] = place_y.astype(F32)
    payload[5:6, :] = place_z.astype(F32)
    for plane in range(3):
        payload[8 + 16 * plane : 17 + 16 * plane, :] = fractions[9 * plane : 9 * plane + 9, :]
    code = destination[...]
    row = lax.broadcasted_iota(jnp.int32, (64, table), 0)
    group = lax.shift_right_logical(row, 3)
    wanted = group + jnp.where(group >= 4, 1, 0)
    matches = jnp.broadcast_to(code, (64, table)) == wanted
    chosen = jnp.where(matches, 1.0, 0.0)
    earlier = jnp.where(
        lax.broadcasted_iota(jnp.int32, (table, table), 0)
        <= lax.broadcasted_iota(jnp.int32, (table, table), 1),
        1.0,
        0.0,
    ).astype(BF16)
    ranks = jnp.dot(chosen.astype(BF16), earlier, preferred_element_type=F32)
    rank_of_row = (lax.bitwise_and(row, 7) + 1).astype(F32)
    picked = jnp.where(ranks == rank_of_row, chosen, 0.0).astype(BF16)
    whole = payload[...]
    high = whole.astype(BF16)
    rest = whole - high.astype(F32)
    middle = rest.astype(BF16)
    low = (rest - middle.astype(F32)).astype(BF16)
    contract = (((1,), (1,)), ((), ()))
    packed = lax.dot_general(picked, high, contract, preferred_element_type=F32)
    packed += lax.dot_general(picked, middle, contract, preferred_element_type=F32)
    packed += lax.dot_general(picked, low, contract, preferred_element_type=F32)
    outbox[...] = jnp.zeros_like(outbox)
    for number in range(8):
        outbox[number, :, 0:56] = packed[8 * number : 8 * number + 8, :]

    inside = jnp.logical_and(me_y > 0, me_y < count_y - 1)
    pl.when(inside)(lambda: pl.semaphore_wait(barrier, 8))
    pl.when(jnp.logical_not(inside))(lambda: pl.semaphore_wait(barrier, 5))

    def mail(number):
        return pltpu.make_async_remote_copy(
            src_ref=outbox.at[number],
            dst_ref=inbox.at[number],
            send_sem=mail_send.at[number],
            recv_sem=mail_recv.at[number],
            device_id=device(SIDES[number]),
            device_id_type=MESH,
        )

    for number, side in enumerate(SIDES):
        when_there(side, lambda number=number: mail(number).start())

    for where, number in ENTRY.items():
        total = None
        for rate, factor in TERMS[where]:
            term = rates[rate] * factor
            total = term if total is None else total + term
        coef[number] = jnp.full((8, 128), total, F32)

    def deposit(many, at_x, at_y, at_z, speeds, planes):
        first = at_x == 1.0
        second = at_x == 2.0
        for x in range(size_x):
            near = jnp.where(first, planes[x], 0.0) if x < 3 else jnp.zeros_like(planes[0])
            if x >= 1:
                near = jnp.where(second, planes[x - 1], near)
            for c in range(4):
                part = near if c == 0 else near * speeds[c - 1]
                upper = part.astype(BF16).astype(F32)
                values[0, c, x, 0:9, 0:many] = upper
                values[1, c, x, 0:9, 0:many] = part - upper
        along_y = lax.broadcasted_iota(jnp.int32, (size_y, many), 0).astype(F32)
        ones_y = [
            jnp.where(along_y == at_y + (dy - 1.0), 1.0, 0.0).astype(BF16) for dy in range(3)
        ]
        along_z = lax.broadcasted_iota(jnp.int32, (size_z, many), 0).astype(F32)
        for dz in range(3):
            across[:, dz * many : dz * many + many] = jnp.where(
                along_z == at_z + (dz - 1.0), 1.0, 0.0
            ).astype(BF16)
            for s in range(2):
                for c in range(4):
                    for x in range(size_x):
                        total = None
                        for dy in range(3):
                            line = values[s, c, x, 3 * dy + dz : 3 * dy + dz + 1, 0:many]
                            line = jnp.broadcast_to(line, (size_y, many)).astype(BF16)
                            term = ones_y[dy] * line
                            total = term if total is None else total + term
                        base = ((s * 4 + c) * size_x + x) * size_y
                        spread[base : base + size_y, dz * many : dz * many + many] = total
        both = lax.dot_general(
            spread[:, 0 : 3 * many], across[:, 0 : 3 * many], contract, preferred_element_type=F32
        )
        half = 4 * size_x * size_y
        return both[0:half] + both[half:]

    staying = code == 4
    planes = [
        jnp.where(staying, payload[8 + 16 * plane : 17 + 16 * plane, :], 0.0) for plane in range(3)
    ]
    solids[...] = deposit(
        table,
        payload[3:4, :],
        payload[4:5, :],
        payload[5:6, :],
        [payload[axis : axis + 1, :] for axis in range(3)],
        planes,
    )

    for number, side in enumerate(SIDES):
        back = (-side[0], -side[1])
        when_there(back, lambda number=number: mail(number).wait_recv())
    came = jnp.concatenate([inbox[...].reshape(64, 128), jnp.zeros((64, 128), F32)], axis=0).T
    solids[...] += deposit(
        128,
        came[3:4, :],
        came[4:5, :],
        came[5:6, :],
        [came[axis : axis + 1, :] for axis in range(3)],
        [came[8 + 16 * plane : 17 + 16 * plane, :] for plane in range(3)],
    )

    lane = lax.broadcasted_iota(jnp.int32, (8, 128), 1)
    plane_rows = size_x * size_y

    def rolled(halves, shift):
        turned = [pltpu.roll(half, shift % 128, 1) for half in halves]
        edge = lane == (0 if shift == 1 else 127)
        return [jnp.where(edge, turned[1 - h], turned[h]) for h in range(2)]

    def chunk(step, x, tile):
        posts = []
        for h in range(2):
            at = pl.ds(pl.multiple_of(x * size_y + tile * 8, 8), 8)
            lanes = slice(128 * h, 128 * h + 128)
            whole_rows = [
                pl.ds(pl.multiple_of(c * plane_rows + x * size_y + tile * 8, 8), 8)
                for c in range(4)
            ]
            fields = [solids[whole_rows[c], lanes] for c in range(4)]
            if step == 0:
                value = [
                    start[number, x, pl.ds(pl.multiple_of(tile * 8, 8), 8), lanes]
                    for number in range(19)
                ]
                inverse = 3.0 / (fields[0] + 1e-06)
                solid = jnp.minimum(fields[0], 1.0)
                triple = [fields[1 + axis] * inverse for axis in range(3)]
                solids[whole_rows[0], lanes] = solid
                for axis in range(3):
                    solids[whole_rows[1 + axis], lanes] = triple[axis]
            else:
                value = [
                    sent1[
                        SLOT[number],
                        x + (1 - VEL[number][0]),
                        h,
                        pl.ds(tile * 8 + (PAD - VEL[number][1]), 8),
                        :,
                    ]
                    for number in range(19)
                ]
                solid, triple = fields[0], fields[1:]
            posts.append(collide(value, solid, triple, lambda number: coef[number]))
        out = sent1 if step == 0 else sent2
        rows = pl.ds(pl.multiple_of(tile * 8 + PAD, 8), 8)
        for number in range(19):
            halves = [posts[0][number], posts[1][number]]
            if VEL[number][2]:
                halves = rolled(halves, VEL[number][2])
            for h in range(2):
                out[SLOT[number], x + 1, h, rows, :] = halves[h]

    def sweep(step, places):
        def body(turn, carry):
            chunk(step, *places(turn))
            return carry

        return body

    outer = lambda turn: ((turn // tiles) * (size_x - 1), turn % tiles)
    rims = lambda turn: (1 + turn // 2, (turn % 2) * (tiles - 1))
    inner = lambda turn: (1 + turn // (tiles - 2), 1 + turn % (tiles - 2))

    def side_of(kind, number):
        if kind == "x":
            return ((1, 0), (-1, 0))[number]
        if kind == "y":
            return ((0, 1), (0, -1))[number]
        return ((1, 1), (-1, 1), (1, -1), (-1, -1))[number]

    def halo(step, kind, number):
        out = sent1 if step == 0 else sent2
        side = side_of(kind, number)
        if kind == "x":
            rows = pl.ds(PAD, size_y)
            source = out.at[pl.ds(5 * number, 5), size_x if number == 0 else 1, :, rows, :]
            target = out.at[pl.ds(5 * number, 5), 0 if number == 0 else size_x + 1, :, rows, :]
            sem = number
        elif kind == "y":
            source, target = rows_out.at[step, number], rows_in.at[step, number]
            sem = 2 + number
        else:
            source, target = ends_out.at[step, number], ends_in.at[step, number]
            sem = 4 + number
        return pltpu.make_async_remote_copy(
            src_ref=source,
            dst_ref=target,
            send_sem=halo_send.at[step, sem],
            recv_sem=halo_recv.at[step, sem],
            device_id=device(side),
            device_id_type=MESH,
        )

    HALOS = [("x", 0), ("x", 1), ("y", 0), ("y", 1)] + [("e", number) for number in range(4)]

    def begin(step, kinds):
        for kind, number in HALOS:
            if kind in kinds:
                when_there(
                    side_of(kind, number),
                    lambda kind=kind, number=number: halo(step, kind, number).start(),
                )

    def arrive(step, kinds):
        for kind, number in HALOS:
            if kind in kinds:
                side = side_of(kind, number)
                when_there(
                    (-side[0], -side[1]),
                    lambda kind=kind, number=number: halo(step, kind, number).wait_recv(),
                )

    def stage_rows(step):
        out = sent1 if step == 0 else sent2
        for number, (kinds, row) in enumerate(((UP, PAD + size_y - 1), (DOWN, PAD))):
            for order, one in enumerate(kinds):
                for x in range(size_x):
                    for h in range(2):
                        at = (order * size_x + x) * 2 + h
                        rows_out[step, number, at : at + 1, :] = out[
                            SLOT[one], x + 1, h, row : row + 1, :
                        ]
        for number, (side_x, side_y) in enumerate(((1, 1), (-1, 1), (1, -1), (-1, -1))):
            one = INDEX[side_x, side_y, 0]
            row = PAD + size_y - 1 if side_y == 1 else PAD
            x = size_x if side_x == 1 else 1
            for h in range(2):
                ends_out[step, number, h : h + 1, :] = out[SLOT[one], x, h, row : row + 1, :]

    def fill_rows(step):
        out = sent1 if step == 0 else sent2
        for number, (kinds, sign) in enumerate(((UP, 1), (DOWN, -1))):
            to_row = PAD - 1 if sign == 1 else PAD + size_y
            own_tile = PAD if sign == 1 else PAD + size_y - 8
            own_row = 0 if sign == 1 else 7

            def from_neighbour(number=number, kinds=kinds, to_row=to_row):
                for order, one in enumerate(kinds):
                    for x in range(size_x):
                        for h in range(2):
                            at = (order * size_x + x) * 2 + h
                            out[SLOT[one], x + 1, h, to_row : to_row + 1, :] = rows_in[
                                step, number, at : at + 1, :
                            ]

            def from_wall(kinds=kinds, to_row=to_row, own_tile=own_tile, own_row=own_row):
                for one in kinds:
                    for x in range(size_x):
                        halves = [
                            out[SLOT[OPP[one]], x + 1, h, own_tile : own_tile + 8, :]
                            for h in range(2)
                        ]
                        if VEL[one][2]:
                            halves = rolled(halves, VEL[one][2])
                        for h in range(2):
                            out[SLOT[one], x + 1 - VEL[one][0], h, to_row : to_row + 1, :] = (
                                halves[h][own_row : own_row + 1, :]
                            )

            wall = me_y == 0 if sign == 1 else me_y == count_y - 1
            pl.when(wall)(from_wall)
            pl.when(jnp.logical_not(wall))(from_neighbour)

    def fill_ends(step):
        out = sent1 if step == 0 else sent2
        for number, (side_x, side_y) in enumerate(((1, 1), (-1, 1), (1, -1), (-1, -1))):
            one = INDEX[side_x, side_y, 0]
            to_row = PAD - 1 if side_y == 1 else PAD + size_y
            to_x = 0 if side_x == 1 else size_x + 1

            def copy_in(number=number, one=one, to_row=to_row, to_x=to_x):
                for h in range(2):
                    out[SLOT[one], to_x, h, to_row : to_row + 1, :] = ends_in[
                        step, number, h : h + 1, :
                    ]

            when_there((-side_x, -side_y), copy_in)

    load.wait()
    lax.fori_loop(0, 2 * tiles, sweep(0, outer), 0)
    begin(0, "x")
    lax.fori_loop(0, 4, sweep(0, rims), 0)
    stage_rows(0)
    begin(0, "ye")
    lax.fori_loop(0, 2 * (tiles - 2), sweep(0, inner), 0)
    lax.fori_loop(0, 2 * (tiles - 2), sweep(1, inner), 0)
    arrive(0, "y")
    fill_rows(0)
    lax.fori_loop(0, 4, sweep(1, rims), 0)
    arrive(0, "xe")
    fill_ends(0)
    lax.fori_loop(0, 2 * tiles, sweep(1, outer), 0)
    begin(1, "x")
    stage_rows(1)
    begin(1, "ye")
    arrive(1, "ye")
    fill_rows(1)
    fill_ends(1)
    arrive(1, "x")
    for number, side in enumerate(SIDES):
        when_there(side, lambda number=number: mail(number).wait_send())
    for step in range(2):
        for kind, number in HALOS:
            when_there(
                side_of(kind, number),
                lambda step=step, kind=kind, number=number: halo(step, kind, number).wait_send(),
            )


def last_kernel(sizes, sent, out, stage, sems):
    size_x, size_y, size_z = sizes
    copies = []
    for x in range(size_x):
        for number in range(19):
            for h in range(2):
                low = PAD - VEL[number][1]
                stage[number, x, :, 128 * h : 128 * h + 128] = sent[
                    SLOT[number], x + 1 - VEL[number][0], h, low : low + size_y, :
                ]
        copies.append(pltpu.make_async_copy(stage.at[:, x], out.at[:, x], sems.at[x]))
        copies[-1].start()
    for copy in copies:
        copy.wait()


def local(populations, relax_rates, velocity, velocity_change, fractions, anchor, destination):
    size_x, size_y, size_z = populations.shape[1:]
    table = anchor.shape[0]
    padded = (19, size_x + 2, 2, size_y + 2 * PAD, 128)
    vmem = pl.BlockSpec(memory_space=pltpu.VMEM)
    rows = 5 * size_x * 2
    sent = pl.pallas_call(
        functools.partial(main_kernel, (size_x, size_y, size_z, table)),
        out_shape=pltpu.VMEM(padded, F32),
        in_specs=[pl.BlockSpec(memory_space=pltpu.SMEM)]
        + [vmem] * 5
        + [pl.BlockSpec(memory_space=pl.ANY)],
        out_specs=vmem,
        scratch_shapes=[
            pltpu.VMEM((19, size_x, size_y, size_z), F32),
            pltpu.VMEM(padded, F32),
            pltpu.VMEM((len(ENTRY), 8, 128), F32),
            pltpu.VMEM((56, table), F32),
            pltpu.VMEM((8, 8, 128), F32),
            pltpu.VMEM((8, 8, 128), F32),
            pltpu.VMEM((2, 4, size_x, 16, table), F32),
            pltpu.VMEM((8 * size_x * size_y, 3 * table), BF16),
            pltpu.VMEM((size_z, 3 * table), BF16),
            pltpu.VMEM((4 * size_x * size_y, size_z), F32),
            pltpu.VMEM((2, 2, rows, 128), F32),
            pltpu.VMEM((2, 2, rows, 128), F32),
            pltpu.VMEM((2, 4, 2, 128), F32),
            pltpu.VMEM((2, 4, 2, 128), F32),
            pltpu.SemaphoreType.DMA,
            pltpu.SemaphoreType.DMA((8,)),
            pltpu.SemaphoreType.DMA((8,)),
            pltpu.SemaphoreType.DMA((2, 8)),
            pltpu.SemaphoreType.DMA((2, 8)),
        ],
        compiler_params=pltpu.CompilerParams(
            collective_id=0, has_side_effects=True, vmem_limit_bytes=48 * 1024 * 1024
        ),
    )(
        relax_rates,
        velocity,
        velocity_change,
        fractions,
        anchor.reshape(1, table),
        destination.reshape(1, table),
        populations,
    )
    return pl.pallas_call(
        functools.partial(last_kernel, (size_x, size_y, size_z)),
        out_shape=jax.ShapeDtypeStruct(populations.shape, F32),
        in_specs=[vmem],
        out_specs=pl.BlockSpec(memory_space=pl.ANY),
        scratch_shapes=[
            pltpu.VMEM((19, size_x, size_y, size_z), F32),
            pltpu.SemaphoreType.DMA((size_x,)),
        ],
        compiler_params=pltpu.CompilerParams(vmem_limit_bytes=24 * 1024 * 1024),
    )(sent)


def solution(mesh):
    placed = (
        P(None, "gx", "gy", None),
        P(),
        P(None, ("gx", "gy")),
        P(None, ("gx", "gy")),
        P(None, ("gx", "gy")),
        P(("gx", "gy")),
        P(("gx", "gy")),
    )
    return jax.shard_map(
        local, mesh=mesh, in_specs=placed, out_specs=P(None, "gx", "gy", None), check_vma=False
    )
```

```python
import functools

import jax
import jax.numpy as jnp
import numpy as np
from jax import lax
from jax.experimental import pallas as pl
from jax.experimental.pallas import tpu as pltpu
from jax.sharding import PartitionSpec as P

CAP = 4
MESH = pl.DeviceIdType.MESH
F32 = jnp.float32
BF16 = jnp.bfloat16
AXIS_PAIRS = ((0, 1), (0, 2), (1, 2))
SIDES = ((-1, -1), (-1, 0), (-1, 1), (0, -1), (0, 1), (1, -1), (1, 0), (1, 1))
PAD = 8


def lattice():
    vectors = [(0, 0, 0)]
    for axis_one in range(3):
        for orient in (1, -1):
            vector_one = [0, 0, 0]
            vector_one[axis_one] = orient
            vectors.append(tuple(vector_one))
    for axis_one, axis_two in AXIS_PAIRS:
        for orient in (1, -1):
            for second in (1, -1):
                vector_one = [0, 0, 0]
                vector_one[axis_one] = orient
                vector_one[axis_two] = second
                vectors.append(tuple(vector_one))
    return vectors


VEL = lattice()
INDEX = {vector: number for number, vector in enumerate(VEL)}
OPP = [INDEX[tuple(-part for part in vector)] for vector in VEL]
PLACES = (
    [number for number in range(19) if VEL[number][0] == 1]
    + [number for number in range(19) if VEL[number][0] == -1]
    + [number for number in range(19) if VEL[number][0] == 0]
)
SLOT = {number: place for place, number in enumerate(PLACES)}
UP = [number for number in range(19) if VEL[number][1] == 1]
DOWN = [number for number in range(19) if VEL[number][1] == -1]


def relaxation_terms():
    speeds = np.array(VEL) * 1.0
    length = (speeds**2).sum(axis=1)
    weights = np.where(length == 0, 1.0 / 3.0, np.where(length == 1, 1.0 / 18.0, 1.0 / 36.0))
    along_x, along_y, along_z = (speeds[:, 0], speeds[:, 1], speeds[:, 2])
    rows_list = [
        np.ones(19),
        along_x,
        along_y,
        along_z,
        length,
        3 * along_x**2 - length,
        along_y**2 - along_z**2,
        along_x * along_y,
        along_y * along_z,
        along_x * along_z,
        along_x * length,
        along_y * length,
        along_z * length,
        along_x * (along_y**2 - along_z**2),
        along_y * (along_z**2 - along_x**2),
        along_z * (along_x**2 - along_y**2),
        length**2,
        (3 * along_x**2 - length) * length,
        (along_y**2 - along_z**2) * length,
    ]
    basis_rows = []
    for candidate in rows_list:
        for earlier in basis_rows:
            candidate = candidate - np.dot(candidate, earlier) * earlier
        basis_rows.append(candidate / np.sqrt(np.dot(candidate, candidate)))
    basis = np.array(basis_rows)

    means = np.zeros((19, 19))
    means[0, 0] = 1.0
    for number, vector in enumerate(VEL):
        used = [axis for axis in range(3) if vector[axis]]
        if len(used) == 1:
            axis = used[0]
            means[1 + axis, number] = 0.5
            means[7 + axis, number] = 0.5 * vector[axis]
        elif len(used) == 2:
            pair = AXIS_PAIRS.index(tuple(used))
            one, two = vector[used[0]], vector[used[1]]
            means[4 + pair, number] = 0.25
            means[10 + 2 * pair, number] = 0.25 * one
            means[11 + 2 * pair, number] = 0.25 * two
            means[16 + pair, number] = 0.25 * one * two
    combine = np.zeros((19, 19))
    entries = [
        {0: 1},
        {1: 1, 2: 1, 3: 1},
        {4: 1, 5: 1, 6: 1},
        {1: 2, 2: -1, 3: -1},
        {4: 1, 5: 1, 6: -2},
        {2: 1, 3: -1},
        {4: 1, 5: -1},
        {7: 1},
        {10: 1, 12: 1},
        {10: 1, 12: -1},
        {8: 1},
        {11: 1, 14: 1},
        {11: 1, 14: -1},
        {9: 1},
        {13: 1, 15: 1},
        {13: 1, 15: -1},
        {16: 1},
        {17: 1},
        {18: 1},
    ]
    for row_number, entry in enumerate(entries):
        for column, factor in entry.items():
            combine[row_number, column] = factor
    scale = np.array(
        [1, 1 / 3, 1 / 3, 1 / 6, 1 / 6, 0.5, 0.5]
        + [1, 0.5, 0.5] * 3
        + [1, 1, 1]
    )
    to_symmetric = combine @ means
    back = np.linalg.inv(to_symmetric)
    terms = {}
    for rate in range(19):
        part = (
            scale[:, None]
            * to_symmetric
            @ np.diag(1.0 / weights)
            @ np.outer(basis[rate], basis[rate])
            @ np.diag(weights)
            @ back
        )
        for row_number in range(19):
            for column in range(19):
                if abs(part[row_number, column]) > 1e-9:
                    terms.setdefault((row_number, column), []).append(
                        (rate, float(part[row_number, column]))
                    )
    return terms


TERMS = relaxation_terms()
ENTRY = {where: number for number, where in enumerate(sorted(TERMS))}


def to_means(value):
    mean = [None] * 19
    mean[0] = value[0]
    for axis in range(3):
        ahead, behind = value[1 + 2 * axis], value[2 + 2 * axis]
        mean[1 + axis] = 0.5 * (ahead + behind)
        mean[7 + axis] = 0.5 * (ahead - behind)
    for pair in range(3):
        pp, pm, mp, mm = value[7 + 4 * pair : 11 + 4 * pair]
        even_one, odd_one = (pp + mm), (pp - mm)
        even_two, odd_two = (pm + mp), (pm - mp)
        mean[4 + pair] = 0.25 * (even_one + even_two)
        mean[16 + pair] = 0.25 * (even_one - even_two)
        mean[10 + 2 * pair] = 0.25 * (odd_one + odd_two)
        mean[11 + 2 * pair] = 0.25 * (odd_one - odd_two)
    return mean


def from_means(mean):
    value = [None] * 19
    value[0] = mean[0]
    for axis in range(3):
        value[1 + 2 * axis] = mean[1 + axis] + mean[7 + axis]
        value[2 + 2 * axis] = mean[1 + axis] - mean[7 + axis]
    for pair in range(3):
        even_one = mean[4 + pair] + mean[16 + pair]
        even_two = mean[4 + pair] - mean[16 + pair]
        odd_one = mean[10 + 2 * pair] + mean[11 + 2 * pair]
        odd_two = mean[10 + 2 * pair] - mean[11 + 2 * pair]
        value[7 + 4 * pair] = even_one + odd_one
        value[8 + 4 * pair] = even_two + odd_two
        value[9 + 4 * pair] = even_two - odd_two
        value[10 + 4 * pair] = even_one - odd_one
    return value


def equilibrium_means(density, impulse, triple):
    half = [0.5 * part for part in triple]
    square = [impulse[axis] * half[axis] for axis in range(3)]
    rest = density - (square[0] + square[1] + square[2]) * (1.0 / 3.0)
    axes = [rest + square[axis] for axis in range(3)]
    mean = [rest] + axes
    mean += [axes[one] + square[two] for one, two in AXIS_PAIRS]
    mean += list(impulse)
    for one, two in AXIS_PAIRS:
        mean += [impulse[one], impulse[two]]
    mean += [impulse[one] * triple[two] for one, two in AXIS_PAIRS]
    return mean


def relax_means(off, coefficient):
    plus = [None] * 19
    plus[0] = off[0]
    pair_sum = off[2] + off[3]
    plus[1] = off[1] + pair_sum
    plus[3] = off[1] + off[1] - pair_sum
    plus[5] = off[2] - off[3]
    pair_sum = off[4] + off[5]
    plus[2] = pair_sum + off[6]
    plus[4] = pair_sum - (off[6] + off[6])
    plus[6] = off[4] - off[5]
    for axis, (one, two) in enumerate(((10, 12), (11, 14), (13, 15))):
        plus[7 + 3 * axis] = off[7 + axis]
        plus[8 + 3 * axis] = off[one] + off[two]
        plus[9 + 3 * axis] = off[one] - off[two]
    plus[16:19] = off[16:19]
    made = []
    for row_number in range(19):
        total = None
        for column in range(19):
            if (row_number, column) in ENTRY:
                term = coefficient(ENTRY[row_number, column]) * plus[column]
                total = term if total is None else total + term
        made.append(total)
    out = [None] * 19
    out[0] = made[0]
    lower = made[1] - made[3]
    out[1] = made[1] + (made[3] + made[3])
    out[2] = lower + made[5]
    out[3] = lower - made[5]
    upper = made[2] + made[4]
    out[4] = upper + made[6]
    out[5] = upper - made[6]
    out[6] = made[2] - (made[4] + made[4])
    for axis, (one, two) in enumerate(((10, 12), (11, 14), (13, 15))):
        out[7 + axis] = made[7 + 3 * axis]
        out[one] = made[8 + 3 * axis] + made[9 + 3 * axis]
        out[two] = made[8 + 3 * axis] - made[9 + 3 * axis]
    out[16:19] = made[16:19]
    return out


def collide(value, solid, solid_triple, coefficient):
    mean = to_means(value)
    ninth, third = 1.0 / 9.0, 1.0 / 3.0
    density = mean[0] * third + (
        (mean[1] + mean[2]) + (mean[3] + mean[4]) + (mean[5] + mean[6])
    ) * ninth
    impulse = [
        (mean[7 + axis] + (mean[one] + mean[two])) * third
        for axis, (one, two) in enumerate(((10, 12), (11, 14), (13, 15)))
    ]
    inverse = 1.0 / density
    triple = [part * inverse for part in impulse]
    fluid = equilibrium_means(density, impulse, triple)
    wall = equilibrium_means(density, [density * part for part in solid_triple], solid_triple)
    off = [mean[number] - fluid[number] for number in range(19)]
    relaxed = relax_means(off, coefficient)
    fluid_part = 1.0 - solid
    post = []
    for number in range(19):
        odd = 7 <= number < 16
        bounced = wall[number] - off[number] if odd else wall[number] + off[number]
        post.append(fluid_part * (mean[number] - relaxed[number]) + solid * bounced)
    return from_means(post)


def main_kernel(
    sizes, rates_hbm, velocity_hbm, change_hbm, fractions_hbm, anchor_hbm, destination_hbm,
    populations, result,
    rates, velocity, change, fractions, anchor, destination,
    start, sent1, sent2, coef, payload, outbox, inbox, values, spread, across, solids,
    rows_out, rows_in, ends_out, ends_in,
    fetch_sem, load_sem, mail_send, mail_recv, halo_send, halo_recv,
):
    size_x, size_y, size_z, table = sizes
    tiles = size_y // 8
    me_x, me_y = lax.axis_index("gx"), lax.axis_index("gy")
    count_x, count_y = lax.axis_size("gx"), lax.axis_size("gy")

    def there(side):
        return side[1] == 0 or (me_y < count_y - 1 if side[1] > 0 else me_y > 0)

    def device(side):
        return (lax.rem(me_x + side[0] + count_x, count_x), me_y + side[1])

    def when_there(side, act):
        if side[1] == 0:
            act()
        else:
            pl.when(there(side))(act)

    fetches = [
        pltpu.make_async_copy(source, target, fetch_sem.at[number])
        for number, (source, target) in enumerate(
            (
                (destination_hbm, destination),
                (anchor_hbm, anchor),
                (velocity_hbm, velocity),
                (change_hbm, change),
                (fractions_hbm, fractions),
                (rates_hbm, rates),
            )
        )
    ]
    for fetch in fetches:
        fetch.start()
    load = pltpu.make_async_copy(populations, start, load_sem)
    load.start()
    inbox[...] = jnp.zeros_like(inbox)

    barrier = pltpu.get_barrier_semaphore()
    for side in SIDES:
        def greet(side=side):
            pl.semaphore_signal(barrier, inc=1, device_id=device(side), device_id_type=MESH)
        when_there(side, greet)

    payload[...] = jnp.zeros_like(payload)
    outbox[...] = jnp.zeros_like(outbox)
    for fetch in fetches:
        fetch.wait()
    place = anchor[...]
    place_x = lax.shift_right_logical(place, 13)
    place_y = lax.bitwise_and(lax.shift_right_logical(place, 8), 31)
    place_z = lax.bitwise_and(place, 255)
    moved = velocity[...] + change[...]
    payload[0:3, :] = moved
    payload[3:4, :] = place_x.astype(F32)
    payload[4:5, :] = place_y.astype(F32)
    payload[5:6, :] = place_z.astype(F32)
    for plane in range(3):
        payload[8 + 16 * plane : 17 + 16 * plane, :] = fractions[9 * plane : 9 * plane + 9, :]
    code = destination[...]
    row = lax.broadcasted_iota(jnp.int32, (64, table), 0)
    group = lax.shift_right_logical(row, 3)
    wanted = group + jnp.where(group >= 4, 1, 0)
    matches = jnp.broadcast_to(code, (64, table)) == wanted
    chosen = jnp.where(matches, 1.0, 0.0)
    earlier = jnp.where(
        lax.broadcasted_iota(jnp.int32, (table, table), 0)
        <= lax.broadcasted_iota(jnp.int32, (table, table), 1),
        1.0,
        0.0,
    ).astype(BF16)
    ranks = jnp.dot(chosen.astype(BF16), earlier, preferred_element_type=F32)
    rank_of_row = (lax.bitwise_and(row, 7) + 1).astype(F32)
    picked = jnp.where(ranks == rank_of_row, chosen, 0.0).astype(BF16)
    whole = payload[...]
    high = whole.astype(BF16)
    rest = whole - high.astype(F32)
    middle = rest.astype(BF16)
    low = (rest - middle.astype(F32)).astype(BF16)
    contract = (((1,), (1,)), ((), ()))
    packed = lax.dot_general(picked, high, contract, preferred_element_type=F32)
    packed += lax.dot_general(picked, middle, contract, preferred_element_type=F32)
    packed += lax.dot_general(picked, low, contract, preferred_element_type=F32)
    for number in range(8):
        outbox[number, :, 0:56] = packed[8 * number : 8 * number + 8, :]

    inside = jnp.logical_and(me_y > 0, me_y < count_y - 1)
    pl.when(inside)(lambda: pl.semaphore_wait(barrier, 8))
    pl.when(jnp.logical_not(inside))(lambda: pl.semaphore_wait(barrier, 5))

    def mail(number):
        return pltpu.make_async_remote_copy(
            src_ref=outbox.at[number],
            dst_ref=inbox.at[number],
            send_sem=mail_send.at[number],
            recv_sem=mail_recv.at[number],
            device_id=device(SIDES[number]),
            device_id_type=MESH,
        )

    for number, side in enumerate(SIDES):
        when_there(side, lambda number=number: mail(number).start())

    for where, number in ENTRY.items():
        total = None
        for rate, factor in TERMS[where]:
            term = rates[rate] * factor
            total = term if total is None else total + term
        coef[number] = jnp.full((8, 128), total, F32)

    def deposit(many, at_x, at_y, at_z, speeds, planes):
        first = at_x == 1.0
        second = at_x == 2.0
        for x in range(size_x):
            near = jnp.where(first, planes[x], 0.0) if x < 3 else jnp.zeros_like(planes[0])
            if x >= 1:
                near = jnp.where(second, planes[x - 1], near)
            for c in range(4):
                part = near if c == 0 else near * speeds[c - 1]
                upper = part.astype(BF16).astype(F32)
                values[0, c, x, 0:9, 0:many] = upper
                values[1, c, x, 0:9, 0:many] = part - upper
        along_y = lax.broadcasted_iota(jnp.int32, (size_y, many), 0).astype(F32)
        ones_y = [
            jnp.where(along_y == at_y + (dy - 1.0), 1.0, 0.0).astype(BF16) for dy in range(3)
        ]
        along_z = lax.broadcasted_iota(jnp.int32, (size_z, many), 0).astype(F32)
        for dz in range(3):
            across[:, dz * many : dz * many + many] = jnp.where(
                along_z == at_z + (dz - 1.0), 1.0, 0.0
            ).astype(BF16)
            for s in range(2):
                for c in range(4):
                    for x in range(size_x):
                        total = None
                        for dy in range(3):
                            line = values[s, c, x, 3 * dy + dz : 3 * dy + dz + 1, 0:many]
                            line = jnp.broadcast_to(line, (size_y, many)).astype(BF16)
                            term = ones_y[dy] * line
                            total = term if total is None else total + term
                        base = ((s * 4 + c) * size_x + x) * size_y
                        spread[base : base + size_y, dz * many : dz * many + many] = total
        both = lax.dot_general(
            spread[:, 0 : 3 * many], across[:, 0 : 3 * many], contract, preferred_element_type=F32
        )
        half = 4 * size_x * size_y
        return both[0:half] + both[half:]

    staying = code == 4
    planes = [
        jnp.where(staying, payload[8 + 16 * plane : 17 + 16 * plane, :], 0.0) for plane in range(3)
    ]
    solids[...] = deposit(
        table,
        payload[3:4, :],
        payload[4:5, :],
        payload[5:6, :],
        [payload[axis : axis + 1, :] for axis in range(3)],
        planes,
    )

    for number, side in enumerate(SIDES):
        back = (-side[0], -side[1])
        when_there(back, lambda number=number: mail(number).wait_recv())
    came = jnp.concatenate([inbox[...].reshape(64, 128), jnp.zeros((64, 128), F32)], axis=0).T
    solids[...] += deposit(
        128,
        came[3:4, :],
        came[4:5, :],
        came[5:6, :],
        [came[axis : axis + 1, :] for axis in range(3)],
        [came[8 + 16 * plane : 17 + 16 * plane, :] for plane in range(3)],
    )

    lane = lax.broadcasted_iota(jnp.int32, (8, 128), 1)
    plane_rows = size_x * size_y

    def rolled(halves, shift):
        turned = [pltpu.roll(half, shift % 128, 1) for half in halves]
        edge = lane == (0 if shift == 1 else 127)
        return [jnp.where(edge, turned[1 - h], turned[h]) for h in range(2)]

    def chunk(step, x, tile):
        posts = []
        for h in range(2):
            at = pl.ds(pl.multiple_of(x * size_y + tile * 8, 8), 8)
            lanes = slice(128 * h, 128 * h + 128)
            whole_rows = [
                pl.ds(pl.multiple_of(c * plane_rows + x * size_y + tile * 8, 8), 8)
                for c in range(4)
            ]
            fields = [solids[whole_rows[c], lanes] for c in range(4)]
            if step == 0:
                value = [
                    start[number, x, pl.ds(pl.multiple_of(tile * 8, 8), 8), lanes]
                    for number in range(19)
                ]
                inverse = 3.0 / (fields[0] + 1e-06)
                solid = jnp.minimum(fields[0], 1.0)
                triple = [fields[1 + axis] * inverse for axis in range(3)]
                solids[whole_rows[0], lanes] = solid
                for axis in range(3):
                    solids[whole_rows[1 + axis], lanes] = triple[axis]
            else:
                value = [
                    sent1[
                        SLOT[number],
                        x + (1 - VEL[number][0]),
                        h,
                        pl.ds(tile * 8 + (PAD - VEL[number][1]), 8),
                        :,
                    ]
                    for number in range(19)
                ]
                solid, triple = fields[0], fields[1:]
            posts.append(collide(value, solid, triple, lambda number: coef[number]))
        out = sent1 if step == 0 else sent2
        rows = pl.ds(pl.multiple_of(tile * 8 + PAD, 8), 8)
        for number in range(19):
            halves = [posts[0][number], posts[1][number]]
            if VEL[number][2]:
                halves = rolled(halves, VEL[number][2])
            for h in range(2):
                out[SLOT[number], x + 1, h, rows, :] = halves[h]

    def sweep(step, places):
        def body(turn, carry):
            chunk(step, *places(turn))
            return carry

        return body

    rims = lambda turn: (1 + turn // 2, (turn % 2) * (tiles - 1))
    inner = lambda turn: (1 + turn // (tiles - 2), 1 + turn % (tiles - 2))

    def side_of(kind, number):
        if kind == "x":
            return ((1, 0), (-1, 0))[number]
        if kind == "y":
            return ((0, 1), (0, -1))[number]
        return ((1, 1), (-1, 1), (1, -1), (-1, -1))[number]

    def halo(step, kind, number, piece=0):
        out = sent1 if step == 0 else sent2
        side = side_of(kind, number)
        if kind == "x":
            rows = pl.ds(pl.multiple_of(PAD + 8 * piece, 8), 8)
            source = out.at[pl.ds(5 * number, 5), size_x if number == 0 else 1, :, rows, :]
            target = out.at[pl.ds(5 * number, 5), 0 if number == 0 else size_x + 1, :, rows, :]
            sem = 6 + number * tiles + piece
        elif kind == "y":
            source, target = rows_out.at[step, number], rows_in.at[step, number]
            sem = number
        else:
            source, target = ends_out.at[step, number], ends_in.at[step, number]
            sem = 2 + number
        return pltpu.make_async_remote_copy(
            src_ref=source,
            dst_ref=target,
            send_sem=halo_send.at[step, sem],
            recv_sem=halo_recv.at[step, sem],
            device_id=device(side),
            device_id_type=MESH,
        )

    HALOS = [("y", 0), ("y", 1)] + [("e", number) for number in range(4)]

    def begin(step):
        for kind, number in HALOS:
            when_there(
                side_of(kind, number),
                lambda kind=kind, number=number: halo(step, kind, number).start(),
            )

    def arrive(step):
        for kind, number in HALOS:
            side = side_of(kind, number)
            when_there(
                (-side[0], -side[1]),
                lambda kind=kind, number=number: halo(step, kind, number).wait_recv(),
            )

    def face_begin(step, piece):
        for number in range(2):
            halo(step, "x", number, piece).start()

    def face_arrive(step, piece):
        for number in range(2):
            halo(step, "x", number, piece).wait_recv()

    def stage_rows(step):
        out = sent1 if step == 0 else sent2
        for number, (kinds, row) in enumerate(((UP, PAD + size_y - 1), (DOWN, PAD))):
            for order, one in enumerate(kinds):
                for x in range(size_x):
                    for h in range(2):
                        at = (order * size_x + x) * 2 + h
                        rows_out[step, number, at : at + 1, :] = out[
                            SLOT[one], x + 1, h, row : row + 1, :
                        ]
        for number, (side_x, side_y) in enumerate(((1, 1), (-1, 1), (1, -1), (-1, -1))):
            one = INDEX[side_x, side_y, 0]
            row = PAD + size_y - 1 if side_y == 1 else PAD
            x = size_x if side_x == 1 else 1
            for h in range(2):
                ends_out[step, number, h : h + 1, :] = out[SLOT[one], x, h, row : row + 1, :]

    def fill_rows(step):
        out = sent1 if step == 0 else sent2
        for number, (kinds, sign) in enumerate(((UP, 1), (DOWN, -1))):
            to_row = PAD - 1 if sign == 1 else PAD + size_y
            own_tile = PAD if sign == 1 else PAD + size_y - 8
            own_row = 0 if sign == 1 else 7

            def from_neighbour(number=number, kinds=kinds, to_row=to_row):
                for order, one in enumerate(kinds):
                    for x in range(size_x):
                        for h in range(2):
                            at = (order * size_x + x) * 2 + h
                            out[SLOT[one], x + 1, h, to_row : to_row + 1, :] = rows_in[
                                step, number, at : at + 1, :
                            ]

            def from_wall(kinds=kinds, to_row=to_row, own_tile=own_tile, own_row=own_row):
                for one in kinds:
                    for x in range(size_x):
                        halves = [
                            out[SLOT[OPP[one]], x + 1, h, own_tile : own_tile + 8, :]
                            for h in range(2)
                        ]
                        if VEL[one][2]:
                            halves = rolled(halves, VEL[one][2])
                        for h in range(2):
                            out[SLOT[one], x + 1 - VEL[one][0], h, to_row : to_row + 1, :] = (
                                halves[h][own_row : own_row + 1, :]
                            )

            wall = me_y == 0 if sign == 1 else me_y == count_y - 1
            pl.when(wall)(from_wall)
            pl.when(jnp.logical_not(wall))(from_neighbour)

    def fill_ends(step):
        out = sent1 if step == 0 else sent2
        for number, (side_x, side_y) in enumerate(((1, 1), (-1, 1), (1, -1), (-1, -1))):
            one = INDEX[side_x, side_y, 0]
            to_row = PAD - 1 if side_y == 1 else PAD + size_y
            to_x = 0 if side_x == 1 else size_x + 1

            def copy_in(number=number, one=one, to_row=to_row, to_x=to_x):
                for h in range(2):
                    out[SLOT[one], to_x, h, to_row : to_row + 1, :] = ends_in[
                        step, number, h : h + 1, :
                    ]

            when_there((-side_x, -side_y), copy_in)

    def final(number, x, tiles_of):
        for h in range(2):
            for tile in tiles_of:
                result[number, x, 8 * tile : 8 * tile + 8, 128 * h : 128 * h + 128] = sent2[
                    SLOT[number],
                    x + 1 - VEL[number][0],
                    h,
                    8 * tile + PAD - VEL[number][1] : 8 * tile + PAD - VEL[number][1] + 8,
                    :,
                ]

    def finish(early):
        for number in range(19):
            for x in range(size_x):
                from_x = 0 <= x - VEL[number][0] < size_x
                ready = [
                    tile
                    for tile in range(tiles)
                    if from_x
                    and not (VEL[number][1] == 1 and tile == 0)
                    and not (VEL[number][1] == -1 and tile == tiles - 1)
                ]
                final(number, x, ready if early else [t for t in range(tiles) if t not in ready])

    def edges(step, tile):
        chunk(step, size_x - 1, tile)
        chunk(step, 0, tile)
        face_begin(step, tile)

    load.wait()

    @pl.loop(0, tiles)
    def _(turn):
        edges(0, turn)

    lax.fori_loop(0, 4, sweep(0, rims), 0)
    stage_rows(0)
    begin(0)
    lax.fori_loop(0, 2 * (tiles - 2), sweep(0, inner), 0)
    lax.fori_loop(0, 2 * (tiles - 2), sweep(1, inner), 0)
    face_arrive(0, 0)
    face_arrive(0, 1)

    @pl.loop(1, tiles - 1)
    def _(turn):
        face_arrive(0, turn + 1)
        edges(1, turn)

    arrive(0)
    fill_rows(0)
    fill_ends(0)

    @pl.loop(0, 2)
    def _(turn):
        edges(1, turn * (tiles - 1))

    lax.fori_loop(0, 4, sweep(1, rims), 0)
    stage_rows(1)
    begin(1)
    finish(True)
    for piece in range(tiles):
        face_arrive(1, piece)
    arrive(1)
    fill_rows(1)
    fill_ends(1)
    finish(False)
    for number, side in enumerate(SIDES):
        when_there(side, lambda number=number: mail(number).wait_send())
    for step in range(2):
        for kind, number in HALOS:
            when_there(
                side_of(kind, number),
                lambda step=step, kind=kind, number=number: halo(step, kind, number).wait_send(),
            )
        for number in range(2):
            for piece in range(tiles):
                halo(step, "x", number, piece).wait_send()


def local(populations, relax_rates, velocity, velocity_change, fractions, anchor, destination):
    size_x, size_y, size_z = populations.shape[1:]
    table = anchor.shape[0]
    padded = (19, size_x + 2, 2, size_y + 2 * PAD, 128)
    hbm = pl.BlockSpec(memory_space=pltpu.HBM)
    rows = 5 * size_x * 2
    halos = 6 + 2 * (size_y // 8)
    return pl.pallas_call(
        functools.partial(main_kernel, (size_x, size_y, size_z, table)),
        out_shape=pltpu.VMEM(populations.shape, F32),
        in_specs=[hbm] * 7,
        out_specs=pl.BlockSpec(memory_space=pltpu.VMEM),
        scratch_shapes=[
            pltpu.SMEM((19,), F32),
            pltpu.VMEM((3, table), F32),
            pltpu.VMEM((3, table), F32),
            pltpu.VMEM((27, table), F32),
            pltpu.VMEM((1, table), jnp.int32),
            pltpu.VMEM((1, table), jnp.int32),
            pltpu.VMEM((19, size_x, size_y, size_z), F32),
            pltpu.VMEM(padded, F32),
            pltpu.VMEM(padded, F32),
            pltpu.VMEM((len(ENTRY), 8, 128), F32),
            pltpu.VMEM((56, table), F32),
            pltpu.VMEM((8, 8, 128), F32),
            pltpu.VMEM((8, 8, 128), F32),
            pltpu.VMEM((2, 4, size_x, 16, table), F32),
            pltpu.VMEM((8 * size_x * size_y, 3 * table), BF16),
            pltpu.VMEM((size_z, 3 * table), BF16),
            pltpu.VMEM((4 * size_x * size_y, size_z), F32),
            pltpu.VMEM((2, 2, rows, 128), F32),
            pltpu.VMEM((2, 2, rows, 128), F32),
            pltpu.VMEM((2, 4, 2, 128), F32),
            pltpu.VMEM((2, 4, 2, 128), F32),
            pltpu.SemaphoreType.DMA((6,)),
            pltpu.SemaphoreType.DMA,
            pltpu.SemaphoreType.DMA((8,)),
            pltpu.SemaphoreType.DMA((8,)),
            pltpu.SemaphoreType.DMA((2, halos)),
            pltpu.SemaphoreType.DMA((2, halos)),
        ],
        compiler_params=pltpu.CompilerParams(
            collective_id=0, has_side_effects=True, vmem_limit_bytes=48 * 1024 * 1024
        ),
    )(
        *(
            pltpu.with_memory_space_constraint(operand, pltpu.HBM)
            for operand in (
                relax_rates,
                velocity,
                velocity_change,
                fractions,
                anchor.reshape(1, table),
                destination.reshape(1, table),
                populations,
            )
        )
    )


def solution(mesh):
    placed = (
        P(None, "gx", "gy", None),
        P(),
        P(None, ("gx", "gy")),
        P(None, ("gx", "gy")),
        P(None, ("gx", "gy")),
        P(("gx", "gy")),
        P(("gx", "gy")),
    )
    return jax.shard_map(
        local, mesh=mesh, in_specs=placed, out_specs=P(None, "gx", "gy", None), check_vma=False
    )
```

```python
import functools

import jax
import jax.numpy as jnp
import numpy as np
from jax import lax
from jax.experimental import pallas as pl
from jax.experimental.pallas import tpu as pltpu
from jax.sharding import PartitionSpec as P

CAP = 4
MESH = pl.DeviceIdType.MESH
F32 = jnp.float32
BF16 = jnp.bfloat16
AXIS_PAIRS = ((0, 1), (0, 2), (1, 2))
SIDES = ((-1, -1), (-1, 0), (-1, 1), (0, -1), (0, 1), (1, -1), (1, 0), (1, 1))
PAD = 8


def lattice():
    vectors = [(0, 0, 0)]
    for axis_one in range(3):
        for orient in (1, -1):
            vector_one = [0, 0, 0]
            vector_one[axis_one] = orient
            vectors.append(tuple(vector_one))
    for axis_one, axis_two in AXIS_PAIRS:
        for orient in (1, -1):
            for second in (1, -1):
                vector_one = [0, 0, 0]
                vector_one[axis_one] = orient
                vector_one[axis_two] = second
                vectors.append(tuple(vector_one))
    return vectors


VEL = lattice()
INDEX = {vector: number for number, vector in enumerate(VEL)}
OPP = [INDEX[tuple(-part for part in vector)] for vector in VEL]
PLACES = (
    [number for number in range(19) if VEL[number][0] == 1]
    + [number for number in range(19) if VEL[number][0] == -1]
    + [number for number in range(19) if VEL[number][0] == 0]
)
SLOT = {number: place for place, number in enumerate(PLACES)}
UP = [number for number in range(19) if VEL[number][1] == 1]
DOWN = [number for number in range(19) if VEL[number][1] == -1]


def relaxation_terms():
    speeds = np.array(VEL) * 1.0
    length = (speeds**2).sum(axis=1)
    weights = np.where(length == 0, 1.0 / 3.0, np.where(length == 1, 1.0 / 18.0, 1.0 / 36.0))
    along_x, along_y, along_z = (speeds[:, 0], speeds[:, 1], speeds[:, 2])
    rows_list = [
        np.ones(19),
        along_x,
        along_y,
        along_z,
        length,
        3 * along_x**2 - length,
        along_y**2 - along_z**2,
        along_x * along_y,
        along_y * along_z,
        along_x * along_z,
        along_x * length,
        along_y * length,
        along_z * length,
        along_x * (along_y**2 - along_z**2),
        along_y * (along_z**2 - along_x**2),
        along_z * (along_x**2 - along_y**2),
        length**2,
        (3 * along_x**2 - length) * length,
        (along_y**2 - along_z**2) * length,
    ]
    basis_rows = []
    for candidate in rows_list:
        for earlier in basis_rows:
            candidate = candidate - np.dot(candidate, earlier) * earlier
        basis_rows.append(candidate / np.sqrt(np.dot(candidate, candidate)))
    basis = np.array(basis_rows)

    means = np.zeros((19, 19))
    means[0, 0] = 1.0
    for number, vector in enumerate(VEL):
        used = [axis for axis in range(3) if vector[axis]]
        if len(used) == 1:
            axis = used[0]
            means[1 + axis, number] = 0.5
            means[7 + axis, number] = 0.5 * vector[axis]
        elif len(used) == 2:
            pair = AXIS_PAIRS.index(tuple(used))
            one, two = vector[used[0]], vector[used[1]]
            means[4 + pair, number] = 0.25
            means[10 + 2 * pair, number] = 0.25 * one
            means[11 + 2 * pair, number] = 0.25 * two
            means[16 + pair, number] = 0.25 * one * two
    combine = np.zeros((19, 19))
    entries = [
        {0: 1},
        {1: 1, 2: 1, 3: 1},
        {4: 1, 5: 1, 6: 1},
        {1: 2, 2: -1, 3: -1},
        {4: 1, 5: 1, 6: -2},
        {2: 1, 3: -1},
        {4: 1, 5: -1},
        {7: 1},
        {10: 1, 12: 1},
        {10: 1, 12: -1},
        {8: 1},
        {11: 1, 14: 1},
        {11: 1, 14: -1},
        {9: 1},
        {13: 1, 15: 1},
        {13: 1, 15: -1},
        {16: 1},
        {17: 1},
        {18: 1},
    ]
    for row_number, entry in enumerate(entries):
        for column, factor in entry.items():
            combine[row_number, column] = factor
    scale = np.array(
        [1, 1 / 3, 1 / 3, 1 / 6, 1 / 6, 0.5, 0.5]
        + [1, 0.5, 0.5] * 3
        + [1, 1, 1]
    )
    to_symmetric = combine @ means
    back = np.linalg.inv(to_symmetric)
    terms = {}
    for rate in range(19):
        part = (
            scale[:, None]
            * to_symmetric
            @ np.diag(1.0 / weights)
            @ np.outer(basis[rate], basis[rate])
            @ np.diag(weights)
            @ back
        )
        for row_number in range(19):
            for column in range(19):
                if abs(part[row_number, column]) > 1e-9:
                    terms.setdefault((row_number, column), []).append(
                        (rate, float(part[row_number, column]))
                    )
    return terms


TERMS = relaxation_terms()
ENTRY = {where: number for number, where in enumerate(sorted(TERMS))}


def to_means(value):
    mean = [None] * 19
    mean[0] = value[0]
    for axis in range(3):
        ahead, behind = value[1 + 2 * axis], value[2 + 2 * axis]
        mean[1 + axis] = 0.5 * (ahead + behind)
        mean[7 + axis] = 0.5 * (ahead - behind)
    for pair in range(3):
        pp, pm, mp, mm = value[7 + 4 * pair : 11 + 4 * pair]
        even_one, odd_one = (pp + mm), (pp - mm)
        even_two, odd_two = (pm + mp), (pm - mp)
        mean[4 + pair] = 0.25 * (even_one + even_two)
        mean[16 + pair] = 0.25 * (even_one - even_two)
        mean[10 + 2 * pair] = 0.25 * (odd_one + odd_two)
        mean[11 + 2 * pair] = 0.25 * (odd_one - odd_two)
    return mean


def from_means(mean):
    value = [None] * 19
    value[0] = mean[0]
    for axis in range(3):
        value[1 + 2 * axis] = mean[1 + axis] + mean[7 + axis]
        value[2 + 2 * axis] = mean[1 + axis] - mean[7 + axis]
    for pair in range(3):
        even_one = mean[4 + pair] + mean[16 + pair]
        even_two = mean[4 + pair] - mean[16 + pair]
        odd_one = mean[10 + 2 * pair] + mean[11 + 2 * pair]
        odd_two = mean[10 + 2 * pair] - mean[11 + 2 * pair]
        value[7 + 4 * pair] = even_one + odd_one
        value[8 + 4 * pair] = even_two + odd_two
        value[9 + 4 * pair] = even_two - odd_two
        value[10 + 4 * pair] = even_one - odd_one
    return value


def equilibrium_means(density, impulse, triple):
    half = [0.5 * part for part in triple]
    square = [impulse[axis] * half[axis] for axis in range(3)]
    rest = density - (square[0] + square[1] + square[2]) * (1.0 / 3.0)
    axes = [rest + square[axis] for axis in range(3)]
    mean = [rest] + axes
    mean += [axes[one] + square[two] for one, two in AXIS_PAIRS]
    mean += list(impulse)
    for one, two in AXIS_PAIRS:
        mean += [impulse[one], impulse[two]]
    mean += [impulse[one] * triple[two] for one, two in AXIS_PAIRS]
    return mean


def relax_means(off, coefficient):
    plus = [None] * 19
    plus[0] = off[0]
    pair_sum = off[2] + off[3]
    plus[1] = off[1] + pair_sum
    plus[3] = off[1] + off[1] - pair_sum
    plus[5] = off[2] - off[3]
    pair_sum = off[4] + off[5]
    plus[2] = pair_sum + off[6]
    plus[4] = pair_sum - (off[6] + off[6])
    plus[6] = off[4] - off[5]
    for axis, (one, two) in enumerate(((10, 12), (11, 14), (13, 15))):
        plus[7 + 3 * axis] = off[7 + axis]
        plus[8 + 3 * axis] = off[one] + off[two]
        plus[9 + 3 * axis] = off[one] - off[two]
    plus[16:19] = off[16:19]
    made = []
    for row_number in range(19):
        total = None
        for column in range(19):
            if (row_number, column) in ENTRY:
                term = coefficient(ENTRY[row_number, column]) * plus[column]
                total = term if total is None else total + term
        made.append(total)
    out = [None] * 19
    out[0] = made[0]
    lower = made[1] - made[3]
    out[1] = made[1] + (made[3] + made[3])
    out[2] = lower + made[5]
    out[3] = lower - made[5]
    upper = made[2] + made[4]
    out[4] = upper + made[6]
    out[5] = upper - made[6]
    out[6] = made[2] - (made[4] + made[4])
    for axis, (one, two) in enumerate(((10, 12), (11, 14), (13, 15))):
        out[7 + axis] = made[7 + 3 * axis]
        out[one] = made[8 + 3 * axis] + made[9 + 3 * axis]
        out[two] = made[8 + 3 * axis] - made[9 + 3 * axis]
    out[16:19] = made[16:19]
    return out


def fluid_part(value, coefficient):
    mean = to_means(value)
    ninth, third = 1.0 / 9.0, 1.0 / 3.0
    density = mean[0] * third + (
        (mean[1] + mean[2]) + (mean[3] + mean[4]) + (mean[5] + mean[6])
    ) * ninth
    impulse = [
        (mean[7 + axis] + (mean[one] + mean[two])) * third
        for axis, (one, two) in enumerate(((10, 12), (11, 14), (13, 15)))
    ]
    inverse = 1.0 / density
    triple = [part * inverse for part in impulse]
    fluid = equilibrium_means(density, impulse, triple)
    off = [mean[number] - fluid[number] for number in range(19)]
    relaxed = relax_means(off, coefficient)
    return density, [mean[number] - relaxed[number] for number in range(19)], off


def solid_part(density, kept, off, solid, solid_triple):
    wall = equilibrium_means(density, [density * part for part in solid_triple], solid_triple)
    share = 1.0 - solid
    post = []
    for number in range(19):
        odd = 7 <= number < 16
        bounced = wall[number] - off[number] if odd else wall[number] + off[number]
        post.append(share * kept[number] + solid * bounced)
    return from_means(post)


def main_kernel(
    sizes, rates_hbm, velocity_hbm, change_hbm, fractions_hbm, anchor_hbm, destination_hbm,
    populations, result,
    rates, velocity, change, fractions, anchor, destination,
    start, ahead, sent1, sent2, coef, payload, outbox, inbox, values, spread, across, solids,
    rows_out, rows_in, ends_out, ends_in,
    fetch_sem, load_sem, mail_send, mail_recv, halo_send, halo_recv,
):
    size_x, size_y, size_z, table = sizes
    tiles = size_y // 8
    me_x, me_y = lax.axis_index("gx"), lax.axis_index("gy")
    count_x, count_y = lax.axis_size("gx"), lax.axis_size("gy")

    def there(side):
        return side[1] == 0 or (me_y < count_y - 1 if side[1] > 0 else me_y > 0)

    def device(side):
        return (lax.rem(me_x + side[0] + count_x, count_x), me_y + side[1])

    def when_there(side, act):
        if side[1] == 0:
            act()
        else:
            pl.when(there(side))(act)

    inbox[...] = jnp.zeros_like(inbox)
    barrier = pltpu.get_barrier_semaphore()
    def far(side):
        return -2 * abs(side[0]) - abs(side[1])

    for side in sorted(SIDES, key=far):
        def greet(side=side):
            pl.semaphore_signal(barrier, inc=1, device_id=device(side), device_id_type=MESH)
        when_there(side, greet)

    fetches = [
        pltpu.make_async_copy(source, target, fetch_sem.at[number])
        for number, (source, target) in enumerate(
            (
                (destination_hbm, destination),
                (anchor_hbm, anchor),
                (velocity_hbm, velocity),
                (change_hbm, change),
                (fractions_hbm, fractions),
                (rates_hbm, rates),
            )
        )
    ]
    for fetch in fetches:
        fetch.start()
    load = pltpu.make_async_copy(populations, start, load_sem)
    load.start()

    payload[...] = jnp.zeros_like(payload)
    outbox[...] = jnp.zeros_like(outbox)
    for fetch in fetches:
        fetch.wait()
    place = anchor[...]
    place_x = lax.shift_right_logical(place, 13)
    place_y = lax.bitwise_and(lax.shift_right_logical(place, 8), 31)
    place_z = lax.bitwise_and(place, 255)
    moved = velocity[...] + change[...]
    payload[0:3, :] = moved
    payload[3:4, :] = place_x.astype(F32)
    payload[4:5, :] = place_y.astype(F32)
    payload[5:6, :] = place_z.astype(F32)
    for plane in range(3):
        payload[8 + 16 * plane : 17 + 16 * plane, :] = fractions[9 * plane : 9 * plane + 9, :]
    code = destination[...]
    row = lax.broadcasted_iota(jnp.int32, (64, table), 0)
    group = lax.shift_right_logical(row, 3)
    wanted = group + jnp.where(group >= 4, 1, 0)
    matches = jnp.broadcast_to(code, (64, table)) == wanted
    chosen = jnp.where(matches, 1.0, 0.0)
    earlier = jnp.where(
        lax.broadcasted_iota(jnp.int32, (table, table), 0)
        <= lax.broadcasted_iota(jnp.int32, (table, table), 1),
        1.0,
        0.0,
    ).astype(BF16)
    ranks = jnp.dot(chosen.astype(BF16), earlier, preferred_element_type=F32)
    rank_of_row = (lax.bitwise_and(row, 7) + 1).astype(F32)
    picked = jnp.where(ranks == rank_of_row, chosen, 0.0).astype(BF16)
    whole = payload[...]
    high = whole.astype(BF16)
    rest = whole - high.astype(F32)
    middle = rest.astype(BF16)
    low = (rest - middle.astype(F32)).astype(BF16)
    contract = (((1,), (1,)), ((), ()))
    packed = lax.dot_general(picked, high, contract, preferred_element_type=F32)
    packed += lax.dot_general(picked, middle, contract, preferred_element_type=F32)
    packed += lax.dot_general(picked, low, contract, preferred_element_type=F32)
    for number in range(8):
        outbox[number, :, 0:56] = packed[8 * number : 8 * number + 8, :]

    inside = jnp.logical_and(me_y > 0, me_y < count_y - 1)
    pl.when(inside)(lambda: pl.semaphore_wait(barrier, 8))
    pl.when(jnp.logical_not(inside))(lambda: pl.semaphore_wait(barrier, 5))

    def mail(number):
        return pltpu.make_async_remote_copy(
            src_ref=outbox.at[number],
            dst_ref=inbox.at[number],
            send_sem=mail_send.at[number],
            recv_sem=mail_recv.at[number],
            device_id=device(SIDES[number]),
            device_id_type=MESH,
        )

    for number in sorted(range(8), key=lambda number: far(SIDES[number])):
        when_there(SIDES[number], lambda number=number: mail(number).start())

    for where, number in ENTRY.items():
        total = None
        for rate, factor in TERMS[where]:
            term = rates[rate] * factor
            total = term if total is None else total + term
        coef[number] = jnp.full((8, 128), total, F32)

    def deposit(many, at_x, at_y, at_z, speeds, planes, twice):
        left = lax.broadcasted_iota(jnp.int32, (1, many), 1) < many // 2
        first = at_x == 1.0
        second = at_x == 2.0
        for x in range(size_x):
            near = jnp.where(first, planes[x], 0.0) if x < 3 else jnp.zeros_like(planes[0])
            if x >= 1:
                near = jnp.where(second, planes[x - 1], near)
            for c in range(4):
                part = near if c == 0 else near * speeds[c - 1]
                upper = part.astype(BF16).astype(F32)
                if twice:
                    values[0, c, x, 0:9, 0:many] = jnp.where(left, upper, part - upper)
                else:
                    values[0, c, x, 0:9, 0:many] = upper
                    values[1, c, x, 0:9, 0:many] = part - upper
        along_y = lax.broadcasted_iota(jnp.int32, (size_y, many), 0).astype(F32)
        ones_y = [
            jnp.where(along_y == at_y + (dy - 1.0), 1.0, 0.0).astype(BF16) for dy in range(3)
        ]
        along_z = lax.broadcasted_iota(jnp.int32, (size_z, many), 0).astype(F32)
        for dz in range(3):
            across[:, dz * many : dz * many + many] = jnp.where(
                along_z == at_z + (dz - 1.0), 1.0, 0.0
            ).astype(BF16)
            for s in range(1 if twice else 2):
                for c in range(4):
                    for x in range(size_x):
                        total = None
                        for dy in range(3):
                            line = values[s, c, x, 3 * dy + dz : 3 * dy + dz + 1, 0:many]
                            line = jnp.broadcast_to(line, (size_y, many)).astype(BF16)
                            term = ones_y[dy] * line
                            total = term if total is None else total + term
                        base = ((s * 4 + c) * size_x + x) * size_y
                        spread[base : base + size_y, dz * many : dz * many + many] = total
        half = 4 * size_x * size_y
        both = lax.dot_general(
            spread[0 : half if twice else 2 * half, 0 : 3 * many],
            across[:, 0 : 3 * many],
            contract,
            preferred_element_type=F32,
        )
        return both if twice else both[0:half] + both[half:]

    staying = code == 4
    planes = [
        jnp.where(staying, payload[8 + 16 * plane : 17 + 16 * plane, :], 0.0) for plane in range(3)
    ]
    solids[...] = deposit(
        table,
        payload[3:4, :],
        payload[4:5, :],
        payload[5:6, :],
        [payload[axis : axis + 1, :] for axis in range(3)],
        planes,
        False,
    )

    load.wait()

    @pl.loop(0, size_x * tiles)
    def _(turn):
        x, tile = turn // tiles, turn % tiles
        rows = pl.ds(pl.multiple_of(tile * 8, 8), 8)
        for h in range(2):
            lanes = slice(128 * h, 128 * h + 128)
            density, kept, off = fluid_part(
                [start[number, x, rows, lanes] for number in range(19)], lambda number: coef[number]
            )
            ahead[38, x, h, rows, :] = density
            for number in range(19):
                ahead[number, x, h, rows, :] = kept[number]
                ahead[19 + number, x, h, rows, :] = off[number]

    for number, side in enumerate(SIDES):
        back = (-side[0], -side[1])
        when_there(back, lambda number=number: mail(number).wait_recv())
    letters = inbox[...].reshape(64, 128)
    came = jnp.concatenate([letters, letters], axis=0).T
    solids[...] += deposit(
        128,
        came[3:4, :],
        came[4:5, :],
        came[5:6, :],
        [came[axis : axis + 1, :] for axis in range(3)],
        [came[8 + 16 * plane : 17 + 16 * plane, :] for plane in range(3)],
        True,
    )

    lane = lax.broadcasted_iota(jnp.int32, (8, 128), 1)
    plane_rows = size_x * size_y

    def rolled(halves, shift):
        turned = [pltpu.roll(half, shift % 128, 1) for half in halves]
        edge = lane == (0 if shift == 1 else 127)
        return [jnp.where(edge, turned[1 - h], turned[h]) for h in range(2)]

    def chunk(step, x, tile):
        posts = []
        for h in range(2):
            lanes = slice(128 * h, 128 * h + 128)
            whole_rows = [
                pl.ds(pl.multiple_of(c * plane_rows + x * size_y + tile * 8, 8), 8)
                for c in range(4)
            ]
            fields = [solids[whole_rows[c], lanes] for c in range(4)]
            if step == 0:
                own = pl.ds(pl.multiple_of(tile * 8, 8), 8)
                parts = [ahead[number, x, h, own, :] for number in range(39)]
                density, kept, off = parts[38], parts[0:19], parts[19:38]
                inverse = 3.0 / (fields[0] + 1e-06)
                solid = jnp.minimum(fields[0], 1.0)
                triple = [fields[1 + axis] * inverse for axis in range(3)]
                solids[whole_rows[0], lanes] = solid
                for axis in range(3):
                    solids[whole_rows[1 + axis], lanes] = triple[axis]
            else:
                value = [
                    sent1[
                        SLOT[number],
                        x + (1 - VEL[number][0]),
                        h,
                        pl.ds(tile * 8 + (PAD - VEL[number][1]), 8),
                        :,
                    ]
                    for number in range(19)
                ]
                solid, triple = fields[0], fields[1:]
                density, kept, off = fluid_part(value, lambda number: coef[number])
            posts.append(solid_part(density, kept, off, solid, triple))
        out = sent1 if step == 0 else sent2
        rows = pl.ds(pl.multiple_of(tile * 8 + PAD, 8), 8)
        for number in range(19):
            halves = [posts[0][number], posts[1][number]]
            if VEL[number][2]:
                halves = rolled(halves, VEL[number][2])
            for h in range(2):
                out[SLOT[number], x + 1, h, rows, :] = halves[h]

    def sweep(step, places):
        def body(turn, carry):
            chunk(step, *places(turn))
            return carry

        return body

    rims = lambda turn: (1 + turn // 2, (turn % 2) * (tiles - 1))
    inner = lambda turn: (1 + turn // (tiles - 2), 1 + turn % (tiles - 2))

    def side_of(kind, number):
        if kind == "x":
            return ((1, 0), (-1, 0))[number]
        if kind == "y":
            return ((0, 1), (0, -1))[number]
        return ((1, 1), (-1, 1), (1, -1), (-1, -1))[number]

    def halo(step, kind, number, piece=0):
        out = sent1 if step == 0 else sent2
        side = side_of(kind, number)
        if kind == "x":
            rows = pl.ds(pl.multiple_of(PAD + 8 * piece, 8), 8)
            source = out.at[pl.ds(5 * number, 5), size_x if number == 0 else 1, :, rows, :]
            target = out.at[pl.ds(5 * number, 5), 0 if number == 0 else size_x + 1, :, rows, :]
            sem = 6 + number * tiles + piece
        elif kind == "y":
            source, target = rows_out.at[step, number], rows_in.at[step, number]
            sem = number
        else:
            source, target = ends_out.at[step, number], ends_in.at[step, number]
            sem = 2 + number
        return pltpu.make_async_remote_copy(
            src_ref=source,
            dst_ref=target,
            send_sem=halo_send.at[step, sem],
            recv_sem=halo_recv.at[step, sem],
            device_id=device(side),
            device_id_type=MESH,
        )

    ROWS = [("y", 0), ("y", 1)]
    ENDS = [("e", number) for number in range(4)]
    ENDS_UP, ENDS_DOWN = ENDS[:2], ENDS[2:]

    def begin(step, halos):
        for kind, number in halos:
            when_there(
                side_of(kind, number),
                lambda kind=kind, number=number: halo(step, kind, number).start(),
            )

    def arrive(step, halos):
        for kind, number in halos:
            side = side_of(kind, number)
            when_there(
                (-side[0], -side[1]),
                lambda kind=kind, number=number: halo(step, kind, number).wait_recv(),
            )

    def face_begin(step, piece):
        for number in range(2):
            halo(step, "x", number, piece).start()

    def face_arrive(step, piece):
        for number in range(2):
            halo(step, "x", number, piece).wait_recv()

    def stage_rows(step):
        out = sent1 if step == 0 else sent2
        for number, (kinds, row) in enumerate(((UP, PAD + size_y - 1), (DOWN, PAD))):
            for order, one in enumerate(kinds):
                for x in range(size_x):
                    for h in range(2):
                        at = (order * size_x + x) * 2 + h
                        rows_out[step, number, at : at + 1, :] = out[
                            SLOT[one], x + 1, h, row : row + 1, :
                        ]

    def stage_ends(step, halos):
        out = sent1 if step == 0 else sent2
        for kind, number in halos:
            side_x, side_y = side_of(kind, number)
            one = INDEX[side_x, side_y, 0]
            row = PAD + size_y - 1 if side_y == 1 else PAD
            x = size_x if side_x == 1 else 1
            for h in range(2):
                ends_out[step, number, h : h + 1, :] = out[SLOT[one], x, h, row : row + 1, :]

    def fill_rows(step):
        out = sent1 if step == 0 else sent2
        for number, (kinds, sign) in enumerate(((UP, 1), (DOWN, -1))):
            to_row = PAD - 1 if sign == 1 else PAD + size_y
            own_tile = PAD if sign == 1 else PAD + size_y - 8
            own_row = 0 if sign == 1 else 7

            def from_neighbour(number=number, kinds=kinds, to_row=to_row):
                for order, one in enumerate(kinds):
                    for x in range(size_x):
                        for h in range(2):
                            at = (order * size_x + x) * 2 + h
                            out[SLOT[one], x + 1, h, to_row : to_row + 1, :] = rows_in[
                                step, number, at : at + 1, :
                            ]

            def from_wall(kinds=kinds, to_row=to_row, own_tile=own_tile, own_row=own_row):
                for one in kinds:
                    for x in range(size_x):
                        halves = [
                            out[SLOT[OPP[one]], x + 1, h, own_tile : own_tile + 8, :]
                            for h in range(2)
                        ]
                        if VEL[one][2]:
                            halves = rolled(halves, VEL[one][2])
                        for h in range(2):
                            out[SLOT[one], x + 1 - VEL[one][0], h, to_row : to_row + 1, :] = (
                                halves[h][own_row : own_row + 1, :]
                            )

            wall = me_y == 0 if sign == 1 else me_y == count_y - 1
            pl.when(wall)(from_wall)
            pl.when(jnp.logical_not(wall))(from_neighbour)

    def fill_ends(step):
        out = sent1 if step == 0 else sent2
        for number, (side_x, side_y) in enumerate(((1, 1), (-1, 1), (1, -1), (-1, -1))):
            one = INDEX[side_x, side_y, 0]
            to_row = PAD - 1 if side_y == 1 else PAD + size_y
            to_x = 0 if side_x == 1 else size_x + 1

            def copy_in(number=number, one=one, to_row=to_row, to_x=to_x):
                for h in range(2):
                    out[SLOT[one], to_x, h, to_row : to_row + 1, :] = ends_in[
                        step, number, h : h + 1, :
                    ]

            when_there((-side_x, -side_y), copy_in)

    def final(number, x, tiles_of):
        for h in range(2):
            for tile in tiles_of:
                result[number, x, 8 * tile : 8 * tile + 8, 128 * h : 128 * h + 128] = sent2[
                    SLOT[number],
                    x + 1 - VEL[number][0],
                    h,
                    8 * tile + PAD - VEL[number][1] : 8 * tile + PAD - VEL[number][1] + 8,
                    :,
                ]

    def finish(early):
        for number in range(19):
            for x in range(size_x):
                from_x = 0 <= x - VEL[number][0] < size_x
                ready = [
                    tile
                    for tile in range(tiles)
                    if from_x
                    and not (VEL[number][1] == 1 and tile == 0)
                    and not (VEL[number][1] == -1 and tile == tiles - 1)
                ]
                final(number, x, ready if early else [t for t in range(tiles) if t not in ready])

    def edges(step, tile, halos=()):
        chunk(step, size_x - 1, tile)
        chunk(step, 0, tile)
        stage_ends(step, halos)
        begin(step, halos)
        face_begin(step, tile)

    edges(0, 0, ENDS_DOWN)
    edges(0, tiles - 1, ENDS_UP)

    @pl.loop(1, tiles - 1)
    def _(turn):
        edges(0, turn)

    lax.fori_loop(0, 4, sweep(0, rims), 0)
    stage_rows(0)
    begin(0, ROWS)
    lax.fori_loop(0, 2 * (tiles - 2), sweep(0, inner), 0)
    lax.fori_loop(0, 2 * (tiles - 2), sweep(1, inner), 0)
    arrive(0, ROWS)
    fill_rows(0)
    lax.fori_loop(0, 4, sweep(1, rims), 0)
    arrive(0, ENDS)
    fill_ends(0)
    face_arrive(0, 0)
    face_arrive(0, 1)
    edges(1, 0, ENDS_DOWN)
    for piece in range(2, tiles):
        face_arrive(0, piece)
    edges(1, tiles - 1, ENDS_UP)
    stage_rows(1)
    begin(1, ROWS)

    @pl.loop(1, tiles - 1)
    def _(turn):
        edges(1, turn)

    finish(True)
    arrive(1, ROWS)
    fill_rows(1)
    for piece in range(tiles):
        face_arrive(1, piece)
    arrive(1, ENDS)
    fill_ends(1)
    finish(False)
    for number, side in enumerate(SIDES):
        when_there(side, lambda number=number: mail(number).wait_send())
    for step in range(2):
        for kind, number in ROWS + ENDS:
            when_there(
                side_of(kind, number),
                lambda step=step, kind=kind, number=number: halo(step, kind, number).wait_send(),
            )
        for number in range(2):
            for piece in range(tiles):
                halo(step, "x", number, piece).wait_send()


def local(populations, relax_rates, velocity, velocity_change, fractions, anchor, destination):
    size_x, size_y, size_z = populations.shape[1:]
    table = anchor.shape[0]
    padded = (19, size_x + 2, 2, size_y + 2 * PAD, 128)
    hbm = pl.BlockSpec(memory_space=pltpu.HBM)
    rows = 5 * size_x * 2
    halos = 6 + 2 * (size_y // 8)
    return pl.pallas_call(
        functools.partial(main_kernel, (size_x, size_y, size_z, table)),
        out_shape=pltpu.VMEM(populations.shape, F32),
        in_specs=[hbm] * 7,
        out_specs=pl.BlockSpec(memory_space=pltpu.VMEM),
        scratch_shapes=[
            pltpu.SMEM((19,), F32),
            pltpu.VMEM((3, table), F32),
            pltpu.VMEM((3, table), F32),
            pltpu.VMEM((27, table), F32),
            pltpu.VMEM((1, table), jnp.int32),
            pltpu.VMEM((1, table), jnp.int32),
            pltpu.VMEM((19, size_x, size_y, size_z), F32),
            pltpu.VMEM((39, size_x, 2, size_y, 128), F32),
            pltpu.VMEM(padded, F32),
            pltpu.VMEM(padded, F32),
            pltpu.VMEM((len(ENTRY), 8, 128), F32),
            pltpu.VMEM((56, table), F32),
            pltpu.VMEM((8, 8, 128), F32),
            pltpu.VMEM((8, 8, 128), F32),
            pltpu.VMEM((2, 4, size_x, 16, table), F32),
            pltpu.VMEM((8 * size_x * size_y, 3 * table), BF16),
            pltpu.VMEM((size_z, 3 * table), BF16),
            pltpu.VMEM((4 * size_x * size_y, size_z), F32),
            pltpu.VMEM((2, 2, rows, 128), F32),
            pltpu.VMEM((2, 2, rows, 128), F32),
            pltpu.VMEM((2, 4, 2, 128), F32),
            pltpu.VMEM((2, 4, 2, 128), F32),
            pltpu.SemaphoreType.DMA((6,)),
            pltpu.SemaphoreType.DMA,
            pltpu.SemaphoreType.DMA((8,)),
            pltpu.SemaphoreType.DMA((8,)),
            pltpu.SemaphoreType.DMA((2, halos)),
            pltpu.SemaphoreType.DMA((2, halos)),
        ],
        compiler_params=pltpu.CompilerParams(
            collective_id=0, has_side_effects=True, vmem_limit_bytes=48 * 1024 * 1024
        ),
    )(
        *(
            pltpu.with_memory_space_constraint(operand, pltpu.HBM)
            for operand in (
                relax_rates,
                velocity,
                velocity_change,
                fractions,
                anchor.reshape(1, table),
                destination.reshape(1, table),
                populations,
            )
        )
    )


def solution(mesh):
    placed = (
        P(None, "gx", "gy", None),
        P(),
        P(None, ("gx", "gy")),
        P(None, ("gx", "gy")),
        P(None, ("gx", "gy")),
        P(("gx", "gy")),
        P(("gx", "gy")),
    )
    return jax.shard_map(
        local, mesh=mesh, in_specs=placed, out_specs=P(None, "gx", "gy", None), check_vma=False
    )
```

```python
import functools

import jax
import jax.numpy as jnp
import numpy as np
from jax import lax
from jax.experimental import pallas as pl
from jax.experimental.pallas import tpu as pltpu
from jax.sharding import PartitionSpec as P

CAP = 4
MESH = pl.DeviceIdType.MESH
F32 = jnp.float32
BF16 = jnp.bfloat16
AXIS_PAIRS = ((0, 1), (0, 2), (1, 2))
SIDES = ((-1, -1), (-1, 0), (-1, 1), (0, -1), (0, 1), (1, -1), (1, 0), (1, 1))
PAD = 8


def lattice():
    vectors = [(0, 0, 0)]
    for axis_one in range(3):
        for orient in (1, -1):
            vector_one = [0, 0, 0]
            vector_one[axis_one] = orient
            vectors.append(tuple(vector_one))
    for axis_one, axis_two in AXIS_PAIRS:
        for orient in (1, -1):
            for second in (1, -1):
                vector_one = [0, 0, 0]
                vector_one[axis_one] = orient
                vector_one[axis_two] = second
                vectors.append(tuple(vector_one))
    return vectors


VEL = lattice()
INDEX = {vector: number for number, vector in enumerate(VEL)}
OPP = [INDEX[tuple(-part for part in vector)] for vector in VEL]
PLACES = (
    [number for number in range(19) if VEL[number][0] == 1]
    + [number for number in range(19) if VEL[number][0] == -1]
    + [number for number in range(19) if VEL[number][0] == 0]
)
SLOT = {number: place for place, number in enumerate(PLACES)}
UP = [number for number in range(19) if VEL[number][1] == 1]
DOWN = [number for number in range(19) if VEL[number][1] == -1]


def relaxation_terms():
    speeds = np.array(VEL) * 1.0
    length = (speeds**2).sum(axis=1)
    weights = np.where(length == 0, 1.0 / 3.0, np.where(length == 1, 1.0 / 18.0, 1.0 / 36.0))
    along_x, along_y, along_z = (speeds[:, 0], speeds[:, 1], speeds[:, 2])
    rows_list = [
        np.ones(19),
        along_x,
        along_y,
        along_z,
        length,
        3 * along_x**2 - length,
        along_y**2 - along_z**2,
        along_x * along_y,
        along_y * along_z,
        along_x * along_z,
        along_x * length,
        along_y * length,
        along_z * length,
        along_x * (along_y**2 - along_z**2),
        along_y * (along_z**2 - along_x**2),
        along_z * (along_x**2 - along_y**2),
        length**2,
        (3 * along_x**2 - length) * length,
        (along_y**2 - along_z**2) * length,
    ]
    basis_rows = []
    for candidate in rows_list:
        for earlier in basis_rows:
            candidate = candidate - np.dot(candidate, earlier) * earlier
        basis_rows.append(candidate / np.sqrt(np.dot(candidate, candidate)))
    basis = np.array(basis_rows)

    means = np.zeros((19, 19))
    means[0, 0] = 1.0
    for number, vector in enumerate(VEL):
        used = [axis for axis in range(3) if vector[axis]]
        if len(used) == 1:
            axis = used[0]
            means[1 + axis, number] = 0.5
            means[7 + axis, number] = 0.5 * vector[axis]
        elif len(used) == 2:
            pair = AXIS_PAIRS.index(tuple(used))
            one, two = vector[used[0]], vector[used[1]]
            means[4 + pair, number] = 0.25
            means[10 + 2 * pair, number] = 0.25 * one
            means[11 + 2 * pair, number] = 0.25 * two
            means[16 + pair, number] = 0.25 * one * two
    combine = np.zeros((19, 19))
    entries = [
        {0: 1},
        {1: 1, 2: 1, 3: 1},
        {4: 1, 5: 1, 6: 1},
        {1: 2, 2: -1, 3: -1},
        {4: 1, 5: 1, 6: -2},
        {2: 1, 3: -1},
        {4: 1, 5: -1},
        {7: 1},
        {10: 1, 12: 1},
        {10: 1, 12: -1},
        {8: 1},
        {11: 1, 14: 1},
        {11: 1, 14: -1},
        {9: 1},
        {13: 1, 15: 1},
        {13: 1, 15: -1},
        {16: 1},
        {17: 1},
        {18: 1},
    ]
    for row_number, entry in enumerate(entries):
        for column, factor in entry.items():
            combine[row_number, column] = factor
    scale = np.array(
        [1, 1 / 3, 1 / 3, 1 / 6, 1 / 6, 0.5, 0.5]
        + [1, 0.5, 0.5] * 3
        + [1, 1, 1]
    )
    to_symmetric = combine @ means
    back = np.linalg.inv(to_symmetric)
    terms = {}
    for rate in range(19):
        part = (
            scale[:, None]
            * to_symmetric
            @ np.diag(1.0 / weights)
            @ np.outer(basis[rate], basis[rate])
            @ np.diag(weights)
            @ back
        )
        for row_number in range(19):
            for column in range(19):
                if abs(part[row_number, column]) > 1e-9:
                    terms.setdefault((row_number, column), []).append(
                        (rate, float(part[row_number, column]))
                    )
    return terms


TERMS = relaxation_terms()
ENTRY = {where: number for number, where in enumerate(sorted(TERMS))}


def to_means(value):
    mean = [None] * 19
    mean[0] = value[0]
    for axis in range(3):
        ahead, behind = value[1 + 2 * axis], value[2 + 2 * axis]
        mean[1 + axis] = 0.5 * (ahead + behind)
        mean[7 + axis] = 0.5 * (ahead - behind)
    for pair in range(3):
        pp, pm, mp, mm = value[7 + 4 * pair : 11 + 4 * pair]
        even_one, odd_one = (pp + mm), (pp - mm)
        even_two, odd_two = (pm + mp), (pm - mp)
        mean[4 + pair] = 0.25 * (even_one + even_two)
        mean[16 + pair] = 0.25 * (even_one - even_two)
        mean[10 + 2 * pair] = 0.25 * (odd_one + odd_two)
        mean[11 + 2 * pair] = 0.25 * (odd_one - odd_two)
    return mean


def from_means(mean):
    value = [None] * 19
    value[0] = mean[0]
    for axis in range(3):
        value[1 + 2 * axis] = mean[1 + axis] + mean[7 + axis]
        value[2 + 2 * axis] = mean[1 + axis] - mean[7 + axis]
    for pair in range(3):
        even_one = mean[4 + pair] + mean[16 + pair]
        even_two = mean[4 + pair] - mean[16 + pair]
        odd_one = mean[10 + 2 * pair] + mean[11 + 2 * pair]
        odd_two = mean[10 + 2 * pair] - mean[11 + 2 * pair]
        value[7 + 4 * pair] = even_one + odd_one
        value[8 + 4 * pair] = even_two + odd_two
        value[9 + 4 * pair] = even_two - odd_two
        value[10 + 4 * pair] = even_one - odd_one
    return value


def equilibrium_means(density, impulse, triple):
    half = [0.5 * part for part in triple]
    square = [impulse[axis] * half[axis] for axis in range(3)]
    rest = density - (square[0] + square[1] + square[2]) * (1.0 / 3.0)
    axes = [rest + square[axis] for axis in range(3)]
    mean = [rest] + axes
    mean += [axes[one] + square[two] for one, two in AXIS_PAIRS]
    mean += list(impulse)
    for one, two in AXIS_PAIRS:
        mean += [impulse[one], impulse[two]]
    mean += [impulse[one] * triple[two] for one, two in AXIS_PAIRS]
    return mean


def relax_means(off, coefficient):
    plus = [None] * 19
    plus[0] = off[0]
    pair_sum = off[2] + off[3]
    plus[1] = off[1] + pair_sum
    plus[3] = off[1] + off[1] - pair_sum
    plus[5] = off[2] - off[3]
    pair_sum = off[4] + off[5]
    plus[2] = pair_sum + off[6]
    plus[4] = pair_sum - (off[6] + off[6])
    plus[6] = off[4] - off[5]
    for axis, (one, two) in enumerate(((10, 12), (11, 14), (13, 15))):
        plus[7 + 3 * axis] = off[7 + axis]
        plus[8 + 3 * axis] = off[one] + off[two]
        plus[9 + 3 * axis] = off[one] - off[two]
    plus[16:19] = off[16:19]
    made = []
    for row_number in range(19):
        total = None
        for column in range(19):
            if (row_number, column) in ENTRY:
                term = coefficient(ENTRY[row_number, column]) * plus[column]
                total = term if total is None else total + term
        made.append(total)
    out = [None] * 19
    out[0] = made[0]
    lower = made[1] - made[3]
    out[1] = made[1] + (made[3] + made[3])
    out[2] = lower + made[5]
    out[3] = lower - made[5]
    upper = made[2] + made[4]
    out[4] = upper + made[6]
    out[5] = upper - made[6]
    out[6] = made[2] - (made[4] + made[4])
    for axis, (one, two) in enumerate(((10, 12), (11, 14), (13, 15))):
        out[7 + axis] = made[7 + 3 * axis]
        out[one] = made[8 + 3 * axis] + made[9 + 3 * axis]
        out[two] = made[8 + 3 * axis] - made[9 + 3 * axis]
    out[16:19] = made[16:19]
    return out


def fluid_part(value, coefficient):
    mean = to_means(value)
    ninth, third = 1.0 / 9.0, 1.0 / 3.0
    density = mean[0] * third + (
        (mean[1] + mean[2]) + (mean[3] + mean[4]) + (mean[5] + mean[6])
    ) * ninth
    impulse = [
        (mean[7 + axis] + (mean[one] + mean[two])) * third
        for axis, (one, two) in enumerate(((10, 12), (11, 14), (13, 15)))
    ]
    inverse = 1.0 / density
    triple = [part * inverse for part in impulse]
    fluid = equilibrium_means(density, impulse, triple)
    off = [mean[number] - fluid[number] for number in range(19)]
    relaxed = relax_means(off, coefficient)
    return density, [mean[number] - relaxed[number] for number in range(19)], off


def solid_part(density, kept, off, solid, solid_triple):
    wall = equilibrium_means(density, [density * part for part in solid_triple], solid_triple)
    share = 1.0 - solid
    post = []
    for number in range(19):
        odd = 7 <= number < 16
        bounced = wall[number] - off[number] if odd else wall[number] + off[number]
        post.append(share * kept[number] + solid * bounced)
    return from_means(post)


def main_kernel(
    sizes, rates_hbm, velocity_hbm, change_hbm, fractions_hbm, anchor_hbm, destination_hbm,
    populations, result,
    rates, velocity, change, fractions, anchor, destination,
    start, ahead, sent1, sent2, coef, payload, outbox, inbox, values, spread, across, solids,
    rows_out, rows_in, ends_out, ends_in,
    fetch_sem, load_sem, mail_send, mail_recv, halo_send, halo_recv,
):
    size_x, size_y, size_z, table = sizes
    tiles = size_y // 8
    me_x, me_y = lax.axis_index("gx"), lax.axis_index("gy")
    count_x, count_y = lax.axis_size("gx"), lax.axis_size("gy")

    def there(side):
        return side[1] == 0 or (me_y < count_y - 1 if side[1] > 0 else me_y > 0)

    def device(side):
        return (lax.rem(me_x + side[0] + count_x, count_x), me_y + side[1])

    def when_there(side, act):
        if side[1] == 0:
            act()
        else:
            pl.when(there(side))(act)

    inbox[...] = jnp.zeros_like(inbox)
    barrier = pltpu.get_barrier_semaphore()
    def far(side):
        return -2 * abs(side[0]) - abs(side[1])

    for side in sorted(SIDES, key=far):
        def greet(side=side):
            pl.semaphore_signal(barrier, inc=1, device_id=device(side), device_id_type=MESH)
        when_there(side, greet)

    fetches = [
        pltpu.make_async_copy(source, target, fetch_sem.at[number])
        for number, (source, target) in enumerate(
            (
                (destination_hbm, destination),
                (anchor_hbm, anchor),
                (velocity_hbm, velocity),
                (change_hbm, change),
                (fractions_hbm, fractions),
                (rates_hbm, rates),
            )
        )
    ]
    for fetch in fetches:
        fetch.start()
    load = pltpu.make_async_copy(populations, start, load_sem)
    load.start()

    payload[...] = jnp.zeros_like(payload)
    outbox[...] = jnp.zeros_like(outbox)
    for fetch in fetches:
        fetch.wait()
    place = anchor[...]
    place_x = lax.shift_right_logical(place, 13)
    place_y = lax.bitwise_and(lax.shift_right_logical(place, 8), 31)
    place_z = lax.bitwise_and(place, 255)
    moved = velocity[...] + change[...]
    payload[0:3, :] = moved
    payload[3:4, :] = place_x.astype(F32)
    payload[4:5, :] = place_y.astype(F32)
    payload[5:6, :] = place_z.astype(F32)
    for plane in range(3):
        payload[8 + 16 * plane : 17 + 16 * plane, :] = fractions[9 * plane : 9 * plane + 9, :]
    code = destination[...]
    row = lax.broadcasted_iota(jnp.int32, (64, table), 0)
    group = lax.shift_right_logical(row, 3)
    wanted = group + jnp.where(group >= 4, 1, 0)
    matches = jnp.broadcast_to(code, (64, table)) == wanted
    chosen = jnp.where(matches, 1.0, 0.0)
    earlier = jnp.where(
        lax.broadcasted_iota(jnp.int32, (table, table), 0)
        <= lax.broadcasted_iota(jnp.int32, (table, table), 1),
        1.0,
        0.0,
    ).astype(BF16)
    ranks = jnp.dot(chosen.astype(BF16), earlier, preferred_element_type=F32)
    rank_of_row = (lax.bitwise_and(row, 7) + 1).astype(F32)
    picked = jnp.where(ranks == rank_of_row, chosen, 0.0).astype(BF16)
    whole = payload[...]
    high = whole.astype(BF16)
    rest = whole - high.astype(F32)
    middle = rest.astype(BF16)
    low = (rest - middle.astype(F32)).astype(BF16)
    contract = (((1,), (1,)), ((), ()))
    packed = lax.dot_general(picked, high, contract, preferred_element_type=F32)
    packed += lax.dot_general(picked, middle, contract, preferred_element_type=F32)
    packed += lax.dot_general(picked, low, contract, preferred_element_type=F32)
    for number in range(8):
        outbox[number, :, 0:56] = packed[8 * number : 8 * number + 8, :]

    inside = jnp.logical_and(me_y > 0, me_y < count_y - 1)
    pl.when(inside)(lambda: pl.semaphore_wait(barrier, 8))
    pl.when(jnp.logical_not(inside))(lambda: pl.semaphore_wait(barrier, 5))

    def mail(number):
        return pltpu.make_async_remote_copy(
            src_ref=outbox.at[number],
            dst_ref=inbox.at[number],
            send_sem=mail_send.at[number],
            recv_sem=mail_recv.at[number],
            device_id=device(SIDES[number]),
            device_id_type=MESH,
        )

    for number in sorted(range(8), key=lambda number: far(SIDES[number])):
        when_there(SIDES[number], lambda number=number: mail(number).start())

    for where, number in ENTRY.items():
        total = None
        for rate, factor in TERMS[where]:
            term = rates[rate] * factor
            total = term if total is None else total + term
        coef[number] = jnp.full((8, 128), total, F32)

    ENDMOST, MIDDLE = (0, size_x - 1), tuple(range(1, size_x - 1))
    turned = {x: number for number, x in enumerate(ENDMOST + MIDDLE)}
    block = 4 * size_y

    def rows_of(x, c, tile):
        number = turned[x] if isinstance(x, int) else x + 1
        return pl.ds(pl.multiple_of(number * block + c * size_y + tile * 8, 8), 8)

    def prepare(many, at_y, at_z):
        along_y = lax.broadcasted_iota(jnp.int32, (size_y, many), 0).astype(F32)
        along_z = lax.broadcasted_iota(jnp.int32, (size_z, many), 0).astype(F32)
        for dz in range(3):
            across[:, dz * many : dz * many + many] = jnp.where(
                along_z == at_z + (dz - 1.0), 1.0, 0.0
            ).astype(BF16)
        return [
            jnp.where(along_y == at_y + (dy - 1.0), 1.0, 0.0).astype(BF16) for dy in range(3)
        ]

    def deposit(many, at_x, ones_y, speeds, planes, twice, xs):
        left = lax.broadcasted_iota(jnp.int32, (1, many), 1) < many // 2
        first = at_x == 1.0
        second = at_x == 2.0
        half = len(xs) * block
        for x in xs:
            near = jnp.where(first, planes[x], 0.0) if x < 3 else jnp.zeros_like(planes[0])
            if x >= 1:
                near = jnp.where(second, planes[x - 1], near)
            for c in range(4):
                part = near if c == 0 else near * speeds[c - 1]
                upper = part.astype(BF16).astype(F32)
                if twice:
                    values[0, c, x, 0:9, 0:many] = jnp.where(left, upper, part - upper)
                else:
                    values[0, c, x, 0:9, 0:many] = upper
                    values[1, c, x, 0:9, 0:many] = part - upper
        for dz in range(3):
            for s in range(1 if twice else 2):
                for number, x in enumerate(xs):
                    for c in range(4):
                        total = None
                        for dy in range(3):
                            line = values[s, c, x, 3 * dy + dz : 3 * dy + dz + 1, 0:many]
                            line = jnp.broadcast_to(line, (size_y, many)).astype(BF16)
                            term = ones_y[dy] * line
                            total = term if total is None else total + term
                        base = s * half + number * block + c * size_y
                        spread[base : base + size_y, dz * many : dz * many + many] = total
        both = lax.dot_general(
            spread[0 : half if twice else 2 * half, 0 : 3 * many],
            across[:, 0 : 3 * many],
            contract,
            preferred_element_type=F32,
        )
        return both if twice else both[0:half] + both[half:]

    staying = code == 4
    planes = [
        jnp.where(staying, payload[8 + 16 * plane : 17 + 16 * plane, :], 0.0) for plane in range(3)
    ]
    solids[...] = deposit(
        table,
        payload[3:4, :],
        prepare(table, payload[4:5, :], payload[5:6, :]),
        [payload[axis : axis + 1, :] for axis in range(3)],
        planes,
        False,
        ENDMOST + MIDDLE,
    )

    load.wait()

    @pl.loop(0, size_x * tiles)
    def _(turn):
        x, tile = turn // tiles, turn % tiles
        rows = pl.ds(pl.multiple_of(tile * 8, 8), 8)
        for h in range(2):
            lanes = slice(128 * h, 128 * h + 128)
            density, kept, off = fluid_part(
                [start[number, x, rows, lanes] for number in range(19)], lambda number: coef[number]
            )
            ahead[38, x, h, rows, :] = density
            for number in range(19):
                ahead[number, x, h, rows, :] = kept[number]
                ahead[19 + number, x, h, rows, :] = off[number]

    for number, side in enumerate(SIDES):
        back = (-side[0], -side[1])
        when_there(back, lambda number=number: mail(number).wait_recv())
    letters = inbox[...].reshape(64, 128)
    came = jnp.concatenate([letters, letters], axis=0).T
    came_y = prepare(128, came[4:5, :], came[5:6, :])

    def deposit_came(xs):
        rows = slice(turned[xs[0]] * block, (turned[xs[-1]] + 1) * block)
        solids[rows, :] += deposit(
            128,
            came[3:4, :],
            came_y,
            [came[axis : axis + 1, :] for axis in range(3)],
            [came[8 + 16 * plane : 17 + 16 * plane, :] for plane in range(3)],
            True,
            xs,
        )

    deposit_came(ENDMOST)
    lane = lax.broadcasted_iota(jnp.int32, (8, 128), 1)

    def rolled(halves, shift):
        turned = [pltpu.roll(half, shift % 128, 1) for half in halves]
        edge = lane == (0 if shift == 1 else 127)
        return [jnp.where(edge, turned[1 - h], turned[h]) for h in range(2)]

    def chunk(step, x, tile):
        posts = []
        for h in range(2):
            lanes = slice(128 * h, 128 * h + 128)
            whole_rows = [rows_of(x, c, tile) for c in range(4)]
            fields = [solids[whole_rows[c], lanes] for c in range(4)]
            if step == 0:
                own = pl.ds(pl.multiple_of(tile * 8, 8), 8)
                parts = [ahead[number, x, h, own, :] for number in range(39)]
                density, kept, off = parts[38], parts[0:19], parts[19:38]
                inverse = 3.0 / (fields[0] + 1e-06)
                solid = jnp.minimum(fields[0], 1.0)
                triple = [fields[1 + axis] * inverse for axis in range(3)]
                solids[whole_rows[0], lanes] = solid
                for axis in range(3):
                    solids[whole_rows[1 + axis], lanes] = triple[axis]
            else:
                value = [
                    sent1[
                        SLOT[number],
                        x + (1 - VEL[number][0]),
                        h,
                        pl.ds(tile * 8 + (PAD - VEL[number][1]), 8),
                        :,
                    ]
                    for number in range(19)
                ]
                solid, triple = fields[0], fields[1:]
                density, kept, off = fluid_part(value, lambda number: coef[number])
            posts.append(solid_part(density, kept, off, solid, triple))
        out = sent1 if step == 0 else sent2
        rows = pl.ds(pl.multiple_of(tile * 8 + PAD, 8), 8)
        for number in range(19):
            halves = [posts[0][number], posts[1][number]]
            if VEL[number][2]:
                halves = rolled(halves, VEL[number][2])
            for h in range(2):
                out[SLOT[number], x + 1, h, rows, :] = halves[h]

    def sweep(step, places):
        def body(turn, carry):
            chunk(step, *places(turn))
            return carry

        return body

    rims = lambda turn: (1 + turn // 2, (turn % 2) * (tiles - 1))
    inner = lambda turn: (1 + turn // (tiles - 2), 1 + turn % (tiles - 2))

    def side_of(kind, number):
        if kind == "x":
            return ((1, 0), (-1, 0))[number]
        if kind == "y":
            return ((0, 1), (0, -1))[number]
        return ((1, 1), (-1, 1), (1, -1), (-1, -1))[number]

    def halo(step, kind, number, piece=0):
        out = sent1 if step == 0 else sent2
        side = side_of(kind, number)
        if kind == "x":
            rows = pl.ds(pl.multiple_of(PAD + 8 * piece, 8), 8)
            source = out.at[pl.ds(5 * number, 5), size_x if number == 0 else 1, :, rows, :]
            target = out.at[pl.ds(5 * number, 5), 0 if number == 0 else size_x + 1, :, rows, :]
            sem = 6 + number * tiles + piece
        elif kind == "y":
            source, target = rows_out.at[step, number], rows_in.at[step, number]
            sem = number
        else:
            source, target = ends_out.at[step, number], ends_in.at[step, number]
            sem = 2 + number
        return pltpu.make_async_remote_copy(
            src_ref=source,
            dst_ref=target,
            send_sem=halo_send.at[step, sem],
            recv_sem=halo_recv.at[step, sem],
            device_id=device(side),
            device_id_type=MESH,
        )

    ROWS = [("y", 0), ("y", 1)]
    ENDS = [("e", number) for number in range(4)]
    ENDS_UP, ENDS_DOWN = ENDS[:2], ENDS[2:]

    def begin(step, halos):
        for kind, number in halos:
            when_there(
                side_of(kind, number),
                lambda kind=kind, number=number: halo(step, kind, number).start(),
            )

    def arrive(step, halos):
        for kind, number in halos:
            side = side_of(kind, number)
            when_there(
                (-side[0], -side[1]),
                lambda kind=kind, number=number: halo(step, kind, number).wait_recv(),
            )

    def face_begin(step, piece):
        for number in range(2):
            halo(step, "x", number, piece).start()

    def face_arrive(step, piece):
        for number in range(2):
            halo(step, "x", number, piece).wait_recv()

    def stage_rows(step):
        out = sent1 if step == 0 else sent2
        for number, (kinds, row) in enumerate(((UP, PAD + size_y - 1), (DOWN, PAD))):
            for order, one in enumerate(kinds):
                for x in range(size_x):
                    for h in range(2):
                        at = (order * size_x + x) * 2 + h
                        rows_out[step, number, at : at + 1, :] = out[
                            SLOT[one], x + 1, h, row : row + 1, :
                        ]

    def stage_ends(step, halos):
        out = sent1 if step == 0 else sent2
        for kind, number in halos:
            side_x, side_y = side_of(kind, number)
            one = INDEX[side_x, side_y, 0]
            row = PAD + size_y - 1 if side_y == 1 else PAD
            x = size_x if side_x == 1 else 1
            for h in range(2):
                ends_out[step, number, h : h + 1, :] = out[SLOT[one], x, h, row : row + 1, :]

    def fill_rows(step):
        out = sent1 if step == 0 else sent2
        for number, (kinds, sign) in enumerate(((UP, 1), (DOWN, -1))):
            to_row = PAD - 1 if sign == 1 else PAD + size_y
            own_tile = PAD if sign == 1 else PAD + size_y - 8
            own_row = 0 if sign == 1 else 7

            def from_neighbour(number=number, kinds=kinds, to_row=to_row):
                for order, one in enumerate(kinds):
                    for x in range(size_x):
                        for h in range(2):
                            at = (order * size_x + x) * 2 + h
                            out[SLOT[one], x + 1, h, to_row : to_row + 1, :] = rows_in[
                                step, number, at : at + 1, :
                            ]

            def from_wall(kinds=kinds, to_row=to_row, own_tile=own_tile, own_row=own_row):
                for one in kinds:
                    for x in range(size_x):
                        halves = [
                            out[SLOT[OPP[one]], x + 1, h, own_tile : own_tile + 8, :]
                            for h in range(2)
                        ]
                        if VEL[one][2]:
                            halves = rolled(halves, VEL[one][2])
                        for h in range(2):
                            out[SLOT[one], x + 1 - VEL[one][0], h, to_row : to_row + 1, :] = (
                                halves[h][own_row : own_row + 1, :]
                            )

            wall = me_y == 0 if sign == 1 else me_y == count_y - 1
            pl.when(wall)(from_wall)
            pl.when(jnp.logical_not(wall))(from_neighbour)

    def fill_ends(step):
        out = sent1 if step == 0 else sent2
        for number, (side_x, side_y) in enumerate(((1, 1), (-1, 1), (1, -1), (-1, -1))):
            one = INDEX[side_x, side_y, 0]
            to_row = PAD - 1 if side_y == 1 else PAD + size_y
            to_x = 0 if side_x == 1 else size_x + 1

            def copy_in(number=number, one=one, to_row=to_row, to_x=to_x):
                for h in range(2):
                    out[SLOT[one], to_x, h, to_row : to_row + 1, :] = ends_in[
                        step, number, h : h + 1, :
                    ]

            when_there((-side_x, -side_y), copy_in)

    def final(number, x, tiles_of):
        for h in range(2):
            for tile in tiles_of:
                result[number, x, 8 * tile : 8 * tile + 8, 128 * h : 128 * h + 128] = sent2[
                    SLOT[number],
                    x + 1 - VEL[number][0],
                    h,
                    8 * tile + PAD - VEL[number][1] : 8 * tile + PAD - VEL[number][1] + 8,
                    :,
                ]

    def finish(part):
        for number in range(19):
            for x in range(size_x):
                inside_x = 0 <= x - VEL[number][0] < size_x
                needs_row = {1: 0, -1: tiles - 1}.get(VEL[number][1])
                if part == "faces":
                    final(number, x, () if inside_x else range(tiles))
                elif inside_x:
                    final(number, x, [t for t in range(tiles) if (t == needs_row) == (part == "rows")])

    def edges(step, tile, halos=()):
        chunk(step, size_x - 1, tile)
        chunk(step, 0, tile)
        stage_ends(step, halos)
        begin(step, halos)
        face_begin(step, tile)

    edges(0, 0, ENDS_DOWN)
    edges(0, tiles - 1, ENDS_UP)
    deposit_came(MIDDLE)

    lax.fori_loop(0, 4, sweep(0, rims), 0)
    stage_rows(0)
    begin(0, ROWS)

    @pl.loop(1, tiles - 1)
    def _(turn):
        edges(0, turn)

    lax.fori_loop(0, 2 * (tiles - 2), sweep(0, inner), 0)
    lax.fori_loop(0, 2 * (tiles - 2), sweep(1, inner), 0)
    arrive(0, ROWS)
    fill_rows(0)
    arrive(0, ENDS)
    fill_ends(0)
    face_arrive(0, 0)
    face_arrive(0, 1)
    edges(1, 0, ENDS_DOWN)
    for piece in range(2, tiles):
        face_arrive(0, piece)
    edges(1, tiles - 1, ENDS_UP)
    lax.fori_loop(0, 4, sweep(1, rims), 0)
    stage_rows(1)
    begin(1, ROWS)

    @pl.loop(1, tiles - 1)
    def _(turn):
        edges(1, turn)

    finish("own")
    arrive(1, ROWS)
    fill_rows(1)
    finish("rows")
    for piece in range(tiles):
        face_arrive(1, piece)
    arrive(1, ENDS)
    fill_ends(1)
    finish("faces")
    for number, side in enumerate(SIDES):
        when_there(side, lambda number=number: mail(number).wait_send())
    for step in range(2):
        for kind, number in ROWS + ENDS:
            when_there(
                side_of(kind, number),
                lambda step=step, kind=kind, number=number: halo(step, kind, number).wait_send(),
            )
        for number in range(2):
            for piece in range(tiles):
                halo(step, "x", number, piece).wait_send()


def local(populations, relax_rates, velocity, velocity_change, fractions, anchor, destination):
    size_x, size_y, size_z = populations.shape[1:]
    table = anchor.shape[0]
    padded = (19, size_x + 2, 2, size_y + 2 * PAD, 128)
    hbm = pl.BlockSpec(memory_space=pltpu.HBM)
    rows = 5 * size_x * 2
    halos = 6 + 2 * (size_y // 8)
    return pl.pallas_call(
        functools.partial(main_kernel, (size_x, size_y, size_z, table)),
        out_shape=pltpu.VMEM(populations.shape, F32),
        in_specs=[hbm] * 7,
        out_specs=pl.BlockSpec(memory_space=pltpu.VMEM),
        scratch_shapes=[
            pltpu.SMEM((19,), F32),
            pltpu.VMEM((3, table), F32),
            pltpu.VMEM((3, table), F32),
            pltpu.VMEM((27, table), F32),
            pltpu.VMEM((1, table), jnp.int32),
            pltpu.VMEM((1, table), jnp.int32),
            pltpu.VMEM((19, size_x, size_y, size_z), F32),
            pltpu.VMEM((39, size_x, 2, size_y, 128), F32),
            pltpu.VMEM(padded, F32),
            pltpu.VMEM(padded, F32),
            pltpu.VMEM((len(ENTRY), 8, 128), F32),
            pltpu.VMEM((56, table), F32),
            pltpu.VMEM((8, 8, 128), F32),
            pltpu.VMEM((8, 8, 128), F32),
            pltpu.VMEM((2, 4, size_x, 16, table), F32),
            pltpu.VMEM((8 * size_x * size_y, 3 * table), BF16),
            pltpu.VMEM((size_z, 3 * table), BF16),
            pltpu.VMEM((4 * size_x * size_y, size_z), F32),
            pltpu.VMEM((2, 2, rows, 128), F32),
            pltpu.VMEM((2, 2, rows, 128), F32),
            pltpu.VMEM((2, 4, 2, 128), F32),
            pltpu.VMEM((2, 4, 2, 128), F32),
            pltpu.SemaphoreType.DMA((6,)),
            pltpu.SemaphoreType.DMA,
            pltpu.SemaphoreType.DMA((8,)),
            pltpu.SemaphoreType.DMA((8,)),
            pltpu.SemaphoreType.DMA((2, halos)),
            pltpu.SemaphoreType.DMA((2, halos)),
        ],
        compiler_params=pltpu.CompilerParams(
            collective_id=0, has_side_effects=True, vmem_limit_bytes=48 * 1024 * 1024
        ),
    )(
        *(
            pltpu.with_memory_space_constraint(operand, pltpu.HBM)
            for operand in (
                relax_rates,
                velocity,
                velocity_change,
                fractions,
                anchor.reshape(1, table),
                destination.reshape(1, table),
                populations,
            )
        )
    )


def solution(mesh):
    placed = (
        P(None, "gx", "gy", None),
        P(),
        P(None, ("gx", "gy")),
        P(None, ("gx", "gy")),
        P(None, ("gx", "gy")),
        P(("gx", "gy")),
        P(("gx", "gy")),
    )
    return jax.shard_map(
        local, mesh=mesh, in_specs=placed, out_specs=P(None, "gx", "gy", None), check_vma=False
    )
```

```python
import functools

import jax
import jax.numpy as jnp
import numpy as np
from jax import lax
from jax.experimental import pallas as pl
from jax.experimental.pallas import tpu as pltpu
from jax.sharding import PartitionSpec as P

CAP = 4
MESH = pl.DeviceIdType.MESH
F32 = jnp.float32
BF16 = jnp.bfloat16
AXIS_PAIRS = ((0, 1), (0, 2), (1, 2))
SIDES = ((-1, -1), (-1, 0), (-1, 1), (0, -1), (0, 1), (1, -1), (1, 0), (1, 1))
PAD = 8


def lattice():
    vectors = [(0, 0, 0)]
    for axis_one in range(3):
        for orient in (1, -1):
            vector_one = [0, 0, 0]
            vector_one[axis_one] = orient
            vectors.append(tuple(vector_one))
    for axis_one, axis_two in AXIS_PAIRS:
        for orient in (1, -1):
            for second in (1, -1):
                vector_one = [0, 0, 0]
                vector_one[axis_one] = orient
                vector_one[axis_two] = second
                vectors.append(tuple(vector_one))
    return vectors


VEL = lattice()
INDEX = {vector: number for number, vector in enumerate(VEL)}
OPP = [INDEX[tuple(-part for part in vector)] for vector in VEL]
PLACES = (
    [number for number in range(19) if VEL[number][0] == 1]
    + [number for number in range(19) if VEL[number][0] == -1]
    + [number for number in range(19) if VEL[number][0] == 0]
)
SLOT = {number: place for place, number in enumerate(PLACES)}
UP = [number for number in range(19) if VEL[number][1] == 1]
DOWN = [number for number in range(19) if VEL[number][1] == -1]


def relaxation_terms():
    speeds = np.array(VEL) * 1.0
    length = (speeds**2).sum(axis=1)
    weights = np.where(length == 0, 1.0 / 3.0, np.where(length == 1, 1.0 / 18.0, 1.0 / 36.0))
    along_x, along_y, along_z = (speeds[:, 0], speeds[:, 1], speeds[:, 2])
    rows_list = [
        np.ones(19),
        along_x,
        along_y,
        along_z,
        length,
        3 * along_x**2 - length,
        along_y**2 - along_z**2,
        along_x * along_y,
        along_y * along_z,
        along_x * along_z,
        along_x * length,
        along_y * length,
        along_z * length,
        along_x * (along_y**2 - along_z**2),
        along_y * (along_z**2 - along_x**2),
        along_z * (along_x**2 - along_y**2),
        length**2,
        (3 * along_x**2 - length) * length,
        (along_y**2 - along_z**2) * length,
    ]
    basis_rows = []
    for candidate in rows_list:
        for earlier in basis_rows:
            candidate = candidate - np.dot(candidate, earlier) * earlier
        basis_rows.append(candidate / np.sqrt(np.dot(candidate, candidate)))
    basis = np.array(basis_rows)

    means = np.zeros((19, 19))
    means[0, 0] = 1.0
    for number, vector in enumerate(VEL):
        used = [axis for axis in range(3) if vector[axis]]
        if len(used) == 1:
            axis = used[0]
            means[1 + axis, number] = 0.5
            means[7 + axis, number] = 0.5 * vector[axis]
        elif len(used) == 2:
            pair = AXIS_PAIRS.index(tuple(used))
            one, two = vector[used[0]], vector[used[1]]
            means[4 + pair, number] = 0.25
            means[10 + 2 * pair, number] = 0.25 * one
            means[11 + 2 * pair, number] = 0.25 * two
            means[16 + pair, number] = 0.25 * one * two
    combine = np.zeros((19, 19))
    entries = [
        {0: 1},
        {1: 1, 2: 1, 3: 1},
        {4: 1, 5: 1, 6: 1},
        {1: 2, 2: -1, 3: -1},
        {4: 1, 5: 1, 6: -2},
        {2: 1, 3: -1},
        {4: 1, 5: -1},
        {7: 1},
        {10: 1, 12: 1},
        {10: 1, 12: -1},
        {8: 1},
        {11: 1, 14: 1},
        {11: 1, 14: -1},
        {9: 1},
        {13: 1, 15: 1},
        {13: 1, 15: -1},
        {16: 1},
        {17: 1},
        {18: 1},
    ]
    for row_number, entry in enumerate(entries):
        for column, factor in entry.items():
            combine[row_number, column] = factor
    scale = np.array(
        [1, 1 / 3, 1 / 3, 1 / 6, 1 / 6, 0.5, 0.5]
        + [1, 0.5, 0.5] * 3
        + [1, 1, 1]
    )
    to_symmetric = combine @ means
    back = np.linalg.inv(to_symmetric)
    terms = {}
    for rate in range(19):
        part = (
            scale[:, None]
            * to_symmetric
            @ np.diag(1.0 / weights)
            @ np.outer(basis[rate], basis[rate])
            @ np.diag(weights)
            @ back
        )
        for row_number in range(19):
            for column in range(19):
                if abs(part[row_number, column]) > 1e-9:
                    terms.setdefault((row_number, column), []).append(
                        (rate, float(part[row_number, column]))
                    )
    return terms


TERMS = relaxation_terms()
ENTRY = {where: number for number, where in enumerate(sorted(TERMS))}


def to_means(value):
    mean = [None] * 19
    mean[0] = value[0]
    for axis in range(3):
        ahead, behind = value[1 + 2 * axis], value[2 + 2 * axis]
        mean[1 + axis] = 0.5 * (ahead + behind)
        mean[7 + axis] = 0.5 * (ahead - behind)
    for pair in range(3):
        pp, pm, mp, mm = value[7 + 4 * pair : 11 + 4 * pair]
        even_one, odd_one = (pp + mm), (pp - mm)
        even_two, odd_two = (pm + mp), (pm - mp)
        mean[4 + pair] = 0.25 * (even_one + even_two)
        mean[16 + pair] = 0.25 * (even_one - even_two)
        mean[10 + 2 * pair] = 0.25 * (odd_one + odd_two)
        mean[11 + 2 * pair] = 0.25 * (odd_one - odd_two)
    return mean


def from_means(mean):
    value = [None] * 19
    value[0] = mean[0]
    for axis in range(3):
        value[1 + 2 * axis] = mean[1 + axis] + mean[7 + axis]
        value[2 + 2 * axis] = mean[1 + axis] - mean[7 + axis]
    for pair in range(3):
        even_one = mean[4 + pair] + mean[16 + pair]
        even_two = mean[4 + pair] - mean[16 + pair]
        odd_one = mean[10 + 2 * pair] + mean[11 + 2 * pair]
        odd_two = mean[10 + 2 * pair] - mean[11 + 2 * pair]
        value[7 + 4 * pair] = even_one + odd_one
        value[8 + 4 * pair] = even_two + odd_two
        value[9 + 4 * pair] = even_two - odd_two
        value[10 + 4 * pair] = even_one - odd_one
    return value


def equilibrium_means(density, impulse, triple):
    half = [0.5 * part for part in triple]
    square = [impulse[axis] * half[axis] for axis in range(3)]
    rest = density - (square[0] + square[1] + square[2]) * (1.0 / 3.0)
    axes = [rest + square[axis] for axis in range(3)]
    mean = [rest] + axes
    mean += [axes[one] + square[two] for one, two in AXIS_PAIRS]
    mean += list(impulse)
    for one, two in AXIS_PAIRS:
        mean += [impulse[one], impulse[two]]
    mean += [impulse[one] * triple[two] for one, two in AXIS_PAIRS]
    return mean


def relax_means(off, coefficient):
    plus = [None] * 19
    plus[0] = off[0]
    pair_sum = off[2] + off[3]
    plus[1] = off[1] + pair_sum
    plus[3] = off[1] + off[1] - pair_sum
    plus[5] = off[2] - off[3]
    pair_sum = off[4] + off[5]
    plus[2] = pair_sum + off[6]
    plus[4] = pair_sum - (off[6] + off[6])
    plus[6] = off[4] - off[5]
    for axis, (one, two) in enumerate(((10, 12), (11, 14), (13, 15))):
        plus[7 + 3 * axis] = off[7 + axis]
        plus[8 + 3 * axis] = off[one] + off[two]
        plus[9 + 3 * axis] = off[one] - off[two]
    plus[16:19] = off[16:19]
    made = []
    for row_number in range(19):
        total = None
        for column in range(19):
            if (row_number, column) in ENTRY:
                term = coefficient(ENTRY[row_number, column]) * plus[column]
                total = term if total is None else total + term
        made.append(total)
    out = [None] * 19
    out[0] = made[0]
    lower = made[1] - made[3]
    out[1] = made[1] + (made[3] + made[3])
    out[2] = lower + made[5]
    out[3] = lower - made[5]
    upper = made[2] + made[4]
    out[4] = upper + made[6]
    out[5] = upper - made[6]
    out[6] = made[2] - (made[4] + made[4])
    for axis, (one, two) in enumerate(((10, 12), (11, 14), (13, 15))):
        out[7 + axis] = made[7 + 3 * axis]
        out[one] = made[8 + 3 * axis] + made[9 + 3 * axis]
        out[two] = made[8 + 3 * axis] - made[9 + 3 * axis]
    out[16:19] = made[16:19]
    return out


def fluid_part(value, coefficient):
    mean = to_means(value)
    ninth, third = 1.0 / 9.0, 1.0 / 3.0
    density = mean[0] * third + (
        (mean[1] + mean[2]) + (mean[3] + mean[4]) + (mean[5] + mean[6])
    ) * ninth
    impulse = [
        (mean[7 + axis] + (mean[one] + mean[two])) * third
        for axis, (one, two) in enumerate(((10, 12), (11, 14), (13, 15)))
    ]
    inverse = 1.0 / density
    triple = [part * inverse for part in impulse]
    fluid = equilibrium_means(density, impulse, triple)
    off = [mean[number] - fluid[number] for number in range(19)]
    relaxed = relax_means(off, coefficient)
    return density, [mean[number] - relaxed[number] for number in range(19)], off


def solid_part(density, kept, off, solid, solid_triple):
    wall = equilibrium_means(density, [density * part for part in solid_triple], solid_triple)
    share = 1.0 - solid
    post = []
    for number in range(19):
        odd = 7 <= number < 16
        bounced = wall[number] - off[number] if odd else wall[number] + off[number]
        post.append(share * kept[number] + solid * bounced)
    return from_means(post)


def main_kernel(
    sizes, rates_hbm, velocity_hbm, change_hbm, fractions_hbm, anchor_hbm, destination_hbm,
    populations, result,
    rates, velocity, change, fractions, anchor, destination,
    start, ahead, sent1, sent2, coef, payload, outbox, inbox, values, spread, across, solids,
    rows_out, rows_in, ends_out, ends_in,
    fetch_sem, load_sem, mail_send, mail_recv, halo_send, halo_recv,
):
    size_x, size_y, size_z, table = sizes
    tiles = size_y // 8
    me_x, me_y = lax.axis_index("gx"), lax.axis_index("gy")
    count_x, count_y = lax.axis_size("gx"), lax.axis_size("gy")

    def there(side):
        return side[1] == 0 or (me_y < count_y - 1 if side[1] > 0 else me_y > 0)

    def device(side):
        return (lax.rem(me_x + side[0] + count_x, count_x), me_y + side[1])

    def when_there(side, act):
        if side[1] == 0:
            act()
        else:
            pl.when(there(side))(act)

    inbox[...] = jnp.zeros_like(inbox)
    barrier = pltpu.get_barrier_semaphore()
    def far(side):
        return -2 * abs(side[0]) - abs(side[1])

    for side in sorted(SIDES, key=far):
        def greet(side=side):
            pl.semaphore_signal(barrier, inc=1, device_id=device(side), device_id_type=MESH)
        when_there(side, greet)

    fetches = [
        pltpu.make_async_copy(source, target, fetch_sem.at[number])
        for number, (source, target) in enumerate(
            (
                (destination_hbm, destination),
                (anchor_hbm, anchor),
                (velocity_hbm, velocity),
                (change_hbm, change),
                (fractions_hbm, fractions),
                (rates_hbm, rates),
            )
        )
    ]
    for fetch in fetches:
        fetch.start()
    load = pltpu.make_async_copy(populations, start, load_sem)
    load.start()

    payload[...] = jnp.zeros_like(payload)
    outbox[...] = jnp.zeros_like(outbox)
    for fetch in fetches:
        fetch.wait()
    place = anchor[...]
    place_x = lax.shift_right_logical(place, 13)
    place_y = lax.bitwise_and(lax.shift_right_logical(place, 8), 31)
    place_z = lax.bitwise_and(place, 255)
    moved = velocity[...] + change[...]
    payload[0:3, :] = moved
    payload[3:4, :] = place_x.astype(F32)
    payload[4:5, :] = place_y.astype(F32)
    payload[5:6, :] = place_z.astype(F32)
    for plane in range(3):
        payload[8 + 16 * plane : 17 + 16 * plane, :] = fractions[9 * plane : 9 * plane + 9, :]
    code = destination[...]
    row = lax.broadcasted_iota(jnp.int32, (64, table), 0)
    group = lax.shift_right_logical(row, 3)
    wanted = group + jnp.where(group >= 4, 1, 0)
    matches = jnp.broadcast_to(code, (64, table)) == wanted
    chosen = jnp.where(matches, 1.0, 0.0)
    earlier = jnp.where(
        lax.broadcasted_iota(jnp.int32, (table, table), 0)
        <= lax.broadcasted_iota(jnp.int32, (table, table), 1),
        1.0,
        0.0,
    ).astype(BF16)
    ranks = jnp.dot(chosen.astype(BF16), earlier, preferred_element_type=F32)
    rank_of_row = (lax.bitwise_and(row, 7) + 1).astype(F32)
    picked = jnp.where(ranks == rank_of_row, chosen, 0.0).astype(BF16)
    whole = payload[...]
    high = whole.astype(BF16)
    rest = whole - high.astype(F32)
    middle = rest.astype(BF16)
    low = (rest - middle.astype(F32)).astype(BF16)
    contract = (((1,), (1,)), ((), ()))
    packed = lax.dot_general(picked, high, contract, preferred_element_type=F32)
    packed += lax.dot_general(picked, middle, contract, preferred_element_type=F32)
    packed += lax.dot_general(picked, low, contract, preferred_element_type=F32)
    for number in range(8):
        outbox[number, :, 0:56] = packed[8 * number : 8 * number + 8, :]

    inside = jnp.logical_and(me_y > 0, me_y < count_y - 1)
    pl.when(inside)(lambda: pl.semaphore_wait(barrier, 8))
    pl.when(jnp.logical_not(inside))(lambda: pl.semaphore_wait(barrier, 5))

    def mail(number):
        return pltpu.make_async_remote_copy(
            src_ref=outbox.at[number],
            dst_ref=inbox.at[number],
            send_sem=mail_send.at[number],
            recv_sem=mail_recv.at[number],
            device_id=device(SIDES[number]),
            device_id_type=MESH,
        )

    for number in sorted(range(8), key=lambda number: far(SIDES[number])):
        when_there(SIDES[number], lambda number=number: mail(number).start())

    for where, number in ENTRY.items():
        total = None
        for rate, factor in TERMS[where]:
            term = rates[rate] * factor
            total = term if total is None else total + term
        coef[number] = jnp.full((8, 128), total, F32)

    ENDMOST, MIDDLE = (0, size_x - 1), tuple(range(1, size_x - 1))
    turned = {x: number for number, x in enumerate(ENDMOST + MIDDLE)}
    block = 4 * size_y

    def rows_of(x, c, tile):
        number = turned[x] if isinstance(x, int) else x + 1
        return pl.ds(pl.multiple_of(number * block + c * size_y + tile * 8, 8), 8)

    def prepare(many, at_y, at_z):
        along_y = lax.broadcasted_iota(jnp.int32, (size_y, many), 0).astype(F32)
        along_z = lax.broadcasted_iota(jnp.int32, (size_z, many), 0).astype(F32)
        for dz in range(3):
            across[:, dz * many : dz * many + many] = jnp.where(
                along_z == at_z + (dz - 1.0), 1.0, 0.0
            ).astype(BF16)
        return [
            jnp.where(along_y == at_y + (dy - 1.0), 1.0, 0.0).astype(BF16) for dy in range(3)
        ]

    def deposit(many, at_x, ones_y, speeds, planes, twice, xs):
        left = lax.broadcasted_iota(jnp.int32, (1, many), 1) < many // 2
        first = at_x == 1.0
        second = at_x == 2.0
        half = len(xs) * block
        for x in xs:
            near = jnp.where(first, planes[x], 0.0) if x < 3 else jnp.zeros_like(planes[0])
            if x >= 1:
                near = jnp.where(second, planes[x - 1], near)
            for c in range(4):
                part = near if c == 0 else near * speeds[c - 1]
                upper = part.astype(BF16).astype(F32)
                if twice:
                    values[0, c, x, 0:9, 0:many] = jnp.where(left, upper, part - upper)
                else:
                    values[0, c, x, 0:9, 0:many] = upper
                    values[1, c, x, 0:9, 0:many] = part - upper
        for dz in range(3):
            for s in range(1 if twice else 2):
                for number, x in enumerate(xs):
                    for c in range(4):
                        total = None
                        for dy in range(3):
                            line = values[s, c, x, 3 * dy + dz : 3 * dy + dz + 1, 0:many]
                            line = jnp.broadcast_to(line, (size_y, many)).astype(BF16)
                            term = ones_y[dy] * line
                            total = term if total is None else total + term
                        base = s * half + number * block + c * size_y
                        spread[base : base + size_y, dz * many : dz * many + many] = total
        both = lax.dot_general(
            spread[0 : half if twice else 2 * half, 0 : 3 * many],
            across[:, 0 : 3 * many],
            contract,
            preferred_element_type=F32,
        )
        return both if twice else both[0:half] + both[half:]

    staying = code == 4
    planes = [
        jnp.where(staying, payload[8 + 16 * plane : 17 + 16 * plane, :], 0.0) for plane in range(3)
    ]
    solids[...] = deposit(
        table,
        payload[3:4, :],
        prepare(table, payload[4:5, :], payload[5:6, :]),
        [payload[axis : axis + 1, :] for axis in range(3)],
        planes,
        False,
        ENDMOST + MIDDLE,
    )

    load.wait()

    @pl.loop(0, size_x * tiles)
    def _(turn):
        x, tile = turn // tiles, turn % tiles
        rows = pl.ds(pl.multiple_of(tile * 8, 8), 8)
        for h in range(2):
            lanes = slice(128 * h, 128 * h + 128)
            density, kept, off = fluid_part(
                [start[number, x, rows, lanes] for number in range(19)], lambda number: coef[number]
            )
            ahead[38, x, h, rows, :] = density
            for number in range(19):
                ahead[number, x, h, rows, :] = kept[number]
                ahead[19 + number, x, h, rows, :] = off[number]

    for number, side in enumerate(SIDES):
        back = (-side[0], -side[1])
        when_there(back, lambda number=number: mail(number).wait_recv())
    letters = inbox[...].reshape(64, 128)
    came = jnp.concatenate([letters, letters], axis=0).T
    came_y = prepare(128, came[4:5, :], came[5:6, :])

    def deposit_came(xs):
        rows = slice(turned[xs[0]] * block, (turned[xs[-1]] + 1) * block)
        solids[rows, :] += deposit(
            128,
            came[3:4, :],
            came_y,
            [came[axis : axis + 1, :] for axis in range(3)],
            [came[8 + 16 * plane : 17 + 16 * plane, :] for plane in range(3)],
            True,
            xs,
        )

    deposit_came(ENDMOST)
    lane = lax.broadcasted_iota(jnp.int32, (8, 128), 1)

    def rolled(halves, shift):
        turned = [pltpu.roll(half, shift % 128, 1) for half in halves]
        edge = lane == (0 if shift == 1 else 127)
        return [jnp.where(edge, turned[1 - h], turned[h]) for h in range(2)]

    def chunk(step, x, tile):
        out = sent1 if step == 0 else sent2
        rows = pl.ds(pl.multiple_of(tile * 8 + PAD, 8), 8)
        for h in range(2):
            lanes = slice(128 * h, 128 * h + 128)
            whole_rows = [rows_of(x, c, tile) for c in range(4)]
            fields = [solids[whole_rows[c], lanes] for c in range(4)]
            if step == 0:
                own = pl.ds(pl.multiple_of(tile * 8, 8), 8)
                parts = [ahead[number, x, h, own, :] for number in range(39)]
                density, kept, off = parts[38], parts[0:19], parts[19:38]
                inverse = 3.0 / (fields[0] + 1e-06)
                solid = jnp.minimum(fields[0], 1.0)
                triple = [fields[1 + axis] * inverse for axis in range(3)]
                solids[whole_rows[0], lanes] = solid
                for axis in range(3):
                    solids[whole_rows[1 + axis], lanes] = triple[axis]
            else:
                value = [
                    sent1[
                        SLOT[number],
                        x + (1 - VEL[number][0]),
                        h,
                        pl.ds(tile * 8 + (PAD - VEL[number][1]), 8),
                        :,
                    ]
                    for number in range(19)
                ]
                solid, triple = fields[0], fields[1:]
                density, kept, off = fluid_part(value, lambda number: coef[number])
            post = solid_part(density, kept, off, solid, triple)
            for number in range(19):
                shift = VEL[number][2]
                if shift:
                    turned_post = pltpu.roll(post[number], shift % 128, 1)
                    edge = lane == (0 if shift == 1 else 127)
                    pltpu.store(
                        out.at[SLOT[number], x + 1, h, rows, :], turned_post, mask=jnp.logical_not(edge)
                    )
                    pltpu.store(
                        out.at[SLOT[number], x + 1, 1 - h, rows, :], turned_post, mask=edge
                    )
                else:
                    out[SLOT[number], x + 1, h, rows, :] = post[number]

    def sweep(step, places):
        def body(turn, carry):
            chunk(step, *places(turn))
            return carry

        return body

    rims = lambda turn: (1 + turn // 2, (turn % 2) * (tiles - 1))
    inner = lambda turn: (1 + turn // (tiles - 2), 1 + turn % (tiles - 2))

    def side_of(kind, number):
        if kind == "x":
            return ((1, 0), (-1, 0))[number]
        if kind == "y":
            return ((0, 1), (0, -1))[number]
        return ((1, 1), (-1, 1), (1, -1), (-1, -1))[number]

    def halo(step, kind, number, piece=0):
        out = sent1 if step == 0 else sent2
        side = side_of(kind, number)
        if kind == "x":
            rows = pl.ds(pl.multiple_of(PAD + 8 * piece, 8), 8)
            source = out.at[pl.ds(5 * number, 5), size_x if number == 0 else 1, :, rows, :]
            target = out.at[pl.ds(5 * number, 5), 0 if number == 0 else size_x + 1, :, rows, :]
            sem = 6 + number * tiles + piece
        elif kind == "y":
            source, target = rows_out.at[step, number], rows_in.at[step, number]
            sem = number
        else:
            source, target = ends_out.at[step, number], ends_in.at[step, number]
            sem = 2 + number
        return pltpu.make_async_remote_copy(
            src_ref=source,
            dst_ref=target,
            send_sem=halo_send.at[step, sem],
            recv_sem=halo_recv.at[step, sem],
            device_id=device(side),
            device_id_type=MESH,
        )

    ROWS = [("y", 0), ("y", 1)]
    ENDS = [("e", number) for number in range(4)]
    ENDS_UP, ENDS_DOWN = ENDS[:2], ENDS[2:]

    def begin(step, halos):
        for kind, number in halos:
            when_there(
                side_of(kind, number),
                lambda kind=kind, number=number: halo(step, kind, number).start(),
            )

    def arrive(step, halos):
        for kind, number in halos:
            side = side_of(kind, number)
            when_there(
                (-side[0], -side[1]),
                lambda kind=kind, number=number: halo(step, kind, number).wait_recv(),
            )

    def face_begin(step, piece):
        for number in range(2):
            halo(step, "x", number, piece).start()

    def face_arrive(step, piece):
        for number in range(2):
            halo(step, "x", number, piece).wait_recv()

    def stage_rows(step):
        out = sent1 if step == 0 else sent2
        for number, (kinds, row) in enumerate(((UP, PAD + size_y - 1), (DOWN, PAD))):
            for order, one in enumerate(kinds):
                for x in range(size_x):
                    for h in range(2):
                        at = (order * size_x + x) * 2 + h
                        rows_out[step, number, at : at + 1, :] = out[
                            SLOT[one], x + 1, h, row : row + 1, :
                        ]

    def stage_ends(step, halos):
        out = sent1 if step == 0 else sent2
        for kind, number in halos:
            side_x, side_y = side_of(kind, number)
            one = INDEX[side_x, side_y, 0]
            row = PAD + size_y - 1 if side_y == 1 else PAD
            x = size_x if side_x == 1 else 1
            for h in range(2):
                ends_out[step, number, h : h + 1, :] = out[SLOT[one], x, h, row : row + 1, :]

    def fill_rows(step):
        out = sent1 if step == 0 else sent2
        for number, (kinds, sign) in enumerate(((UP, 1), (DOWN, -1))):
            to_row = PAD - 1 if sign == 1 else PAD + size_y
            own_tile = PAD if sign == 1 else PAD + size_y - 8
            own_row = 0 if sign == 1 else 7

            def from_neighbour(number=number, kinds=kinds, to_row=to_row):
                for order, one in enumerate(kinds):
                    for x in range(size_x):
                        for h in range(2):
                            at = (order * size_x + x) * 2 + h
                            out[SLOT[one], x + 1, h, to_row : to_row + 1, :] = rows_in[
                                step, number, at : at + 1, :
                            ]

            def from_wall(kinds=kinds, to_row=to_row, own_tile=own_tile, own_row=own_row):
                for one in kinds:
                    for x in range(size_x):
                        halves = [
                            out[SLOT[OPP[one]], x + 1, h, own_tile : own_tile + 8, :]
                            for h in range(2)
                        ]
                        if VEL[one][2]:
                            halves = rolled(halves, VEL[one][2])
                        for h in range(2):
                            out[SLOT[one], x + 1 - VEL[one][0], h, to_row : to_row + 1, :] = (
                                halves[h][own_row : own_row + 1, :]
                            )

            wall = me_y == 0 if sign == 1 else me_y == count_y - 1
            pl.when(wall)(from_wall)
            pl.when(jnp.logical_not(wall))(from_neighbour)

    def fill_ends(step):
        out = sent1 if step == 0 else sent2
        for number, (side_x, side_y) in enumerate(((1, 1), (-1, 1), (1, -1), (-1, -1))):
            one = INDEX[side_x, side_y, 0]
            to_row = PAD - 1 if side_y == 1 else PAD + size_y
            to_x = 0 if side_x == 1 else size_x + 1

            def copy_in(number=number, one=one, to_row=to_row, to_x=to_x):
                for h in range(2):
                    out[SLOT[one], to_x, h, to_row : to_row + 1, :] = ends_in[
                        step, number, h : h + 1, :
                    ]

            when_there((-side_x, -side_y), copy_in)

    def final(number, x, tiles_of):
        for h in range(2):
            for tile in tiles_of:
                result[number, x, 8 * tile : 8 * tile + 8, 128 * h : 128 * h + 128] = sent2[
                    SLOT[number],
                    x + 1 - VEL[number][0],
                    h,
                    8 * tile + PAD - VEL[number][1] : 8 * tile + PAD - VEL[number][1] + 8,
                    :,
                ]

    def finish(part):
        for number in range(19):
            for x in range(size_x):
                inside_x = 0 <= x - VEL[number][0] < size_x
                needs_row = {1: 0, -1: tiles - 1}.get(VEL[number][1])
                if part == "faces":
                    final(number, x, () if inside_x else range(tiles))
                elif inside_x:
                    final(number, x, [t for t in range(tiles) if (t == needs_row) == (part == "rows")])

    def edges(step, tile, halos=()):
        chunk(step, size_x - 1, tile)
        chunk(step, 0, tile)
        stage_ends(step, halos)
        begin(step, halos)
        face_begin(step, tile)

    edges(0, 0, ENDS_DOWN)
    edges(0, tiles - 1, ENDS_UP)
    deposit_came(MIDDLE)

    lax.fori_loop(0, 4, sweep(0, rims), 0)
    stage_rows(0)
    begin(0, ROWS)

    @pl.loop(1, tiles - 1)
    def _(turn):
        edges(0, turn)

    lax.fori_loop(0, 2 * (tiles - 2), sweep(0, inner), 0)
    lax.fori_loop(0, 2 * (tiles - 2), sweep(1, inner), 0)
    arrive(0, ROWS)
    fill_rows(0)
    arrive(0, ENDS)
    fill_ends(0)
    face_arrive(0, 0)
    face_arrive(0, 1)
    edges(1, 0, ENDS_DOWN)
    for piece in range(2, tiles):
        face_arrive(0, piece)
    edges(1, tiles - 1, ENDS_UP)
    lax.fori_loop(0, 4, sweep(1, rims), 0)
    stage_rows(1)
    begin(1, ROWS)

    @pl.loop(1, tiles - 1)
    def _(turn):
        edges(1, turn)

    finish("own")
    arrive(1, ROWS)
    fill_rows(1)
    finish("rows")
    for piece in range(tiles):
        face_arrive(1, piece)
    arrive(1, ENDS)
    fill_ends(1)
    finish("faces")
    for number, side in enumerate(SIDES):
        when_there(side, lambda number=number: mail(number).wait_send())
    for step in range(2):
        for kind, number in ROWS + ENDS:
            when_there(
                side_of(kind, number),
                lambda step=step, kind=kind, number=number: halo(step, kind, number).wait_send(),
            )
        for number in range(2):
            for piece in range(tiles):
                halo(step, "x", number, piece).wait_send()


def local(populations, relax_rates, velocity, velocity_change, fractions, anchor, destination):
    size_x, size_y, size_z = populations.shape[1:]
    table = anchor.shape[0]
    padded = (19, size_x + 2, 2, size_y + 2 * PAD, 128)
    hbm = pl.BlockSpec(memory_space=pltpu.HBM)
    rows = 5 * size_x * 2
    halos = 6 + 2 * (size_y // 8)
    return pl.pallas_call(
        functools.partial(main_kernel, (size_x, size_y, size_z, table)),
        out_shape=pltpu.VMEM(populations.shape, F32),
        in_specs=[hbm] * 7,
        out_specs=pl.BlockSpec(memory_space=pltpu.VMEM),
        scratch_shapes=[
            pltpu.SMEM((19,), F32),
            pltpu.VMEM((3, table), F32),
            pltpu.VMEM((3, table), F32),
            pltpu.VMEM((27, table), F32),
            pltpu.VMEM((1, table), jnp.int32),
            pltpu.VMEM((1, table), jnp.int32),
            pltpu.VMEM((19, size_x, size_y, size_z), F32),
            pltpu.VMEM((39, size_x, 2, size_y, 128), F32),
            pltpu.VMEM(padded, F32),
            pltpu.VMEM(padded, F32),
            pltpu.VMEM((len(ENTRY), 8, 128), F32),
            pltpu.VMEM((56, table), F32),
            pltpu.VMEM((8, 8, 128), F32),
            pltpu.VMEM((8, 8, 128), F32),
            pltpu.VMEM((2, 4, size_x, 16, table), F32),
            pltpu.VMEM((8 * size_x * size_y, 3 * table), BF16),
            pltpu.VMEM((size_z, 3 * table), BF16),
            pltpu.VMEM((4 * size_x * size_y, size_z), F32),
            pltpu.VMEM((2, 2, rows, 128), F32),
            pltpu.VMEM((2, 2, rows, 128), F32),
            pltpu.VMEM((2, 4, 2, 128), F32),
            pltpu.VMEM((2, 4, 2, 128), F32),
            pltpu.SemaphoreType.DMA((6,)),
            pltpu.SemaphoreType.DMA,
            pltpu.SemaphoreType.DMA((8,)),
            pltpu.SemaphoreType.DMA((8,)),
            pltpu.SemaphoreType.DMA((2, halos)),
            pltpu.SemaphoreType.DMA((2, halos)),
        ],
        compiler_params=pltpu.CompilerParams(
            collective_id=0, has_side_effects=True, vmem_limit_bytes=48 * 1024 * 1024
        ),
    )(
        *(
            pltpu.with_memory_space_constraint(operand, pltpu.HBM)
            for operand in (
                relax_rates,
                velocity,
                velocity_change,
                fractions,
                anchor.reshape(1, table),
                destination.reshape(1, table),
                populations,
            )
        )
    )


def solution(mesh):
    placed = (
        P(None, "gx", "gy", None),
        P(),
        P(None, ("gx", "gy")),
        P(None, ("gx", "gy")),
        P(None, ("gx", "gy")),
        P(("gx", "gy")),
        P(("gx", "gy")),
    )
    return jax.shard_map(
        local, mesh=mesh, in_specs=placed, out_specs=P(None, "gx", "gy", None), check_vma=False
    )
```

```python
import functools

import jax
import jax.numpy as jnp
import numpy as np
from jax import lax
from jax.experimental import pallas as pl
from jax.experimental.pallas import tpu as pltpu
from jax.sharding import PartitionSpec as P

CAP = 4
MESH = pl.DeviceIdType.MESH
F32 = jnp.float32
BF16 = jnp.bfloat16
AXIS_PAIRS = ((0, 1), (0, 2), (1, 2))
SIDES = ((-1, -1), (-1, 0), (-1, 1), (0, -1), (0, 1), (1, -1), (1, 0), (1, 1))
PAD = 8


def lattice():
    vectors = [(0, 0, 0)]
    for axis_one in range(3):
        for orient in (1, -1):
            vector_one = [0, 0, 0]
            vector_one[axis_one] = orient
            vectors.append(tuple(vector_one))
    for axis_one, axis_two in AXIS_PAIRS:
        for orient in (1, -1):
            for second in (1, -1):
                vector_one = [0, 0, 0]
                vector_one[axis_one] = orient
                vector_one[axis_two] = second
                vectors.append(tuple(vector_one))
    return vectors


VEL = lattice()
INDEX = {vector: number for number, vector in enumerate(VEL)}
OPP = [INDEX[tuple(-part for part in vector)] for vector in VEL]
PLACES = (
    [number for number in range(19) if VEL[number][0] == 1]
    + [number for number in range(19) if VEL[number][0] == -1]
    + [number for number in range(19) if VEL[number][0] == 0]
)
SLOT = {number: place for place, number in enumerate(PLACES)}
UP = [number for number in range(19) if VEL[number][1] == 1]
DOWN = [number for number in range(19) if VEL[number][1] == -1]


def relaxation_terms():
    speeds = np.array(VEL) * 1.0
    length = (speeds**2).sum(axis=1)
    weights = np.where(length == 0, 1.0 / 3.0, np.where(length == 1, 1.0 / 18.0, 1.0 / 36.0))
    along_x, along_y, along_z = (speeds[:, 0], speeds[:, 1], speeds[:, 2])
    rows_list = [
        np.ones(19),
        along_x,
        along_y,
        along_z,
        length,
        3 * along_x**2 - length,
        along_y**2 - along_z**2,
        along_x * along_y,
        along_y * along_z,
        along_x * along_z,
        along_x * length,
        along_y * length,
        along_z * length,
        along_x * (along_y**2 - along_z**2),
        along_y * (along_z**2 - along_x**2),
        along_z * (along_x**2 - along_y**2),
        length**2,
        (3 * along_x**2 - length) * length,
        (along_y**2 - along_z**2) * length,
    ]
    basis_rows = []
    for candidate in rows_list:
        for earlier in basis_rows:
            candidate = candidate - np.dot(candidate, earlier) * earlier
        basis_rows.append(candidate / np.sqrt(np.dot(candidate, candidate)))
    basis = np.array(basis_rows)

    means = np.zeros((19, 19))
    means[0, 0] = 1.0
    for number, vector in enumerate(VEL):
        used = [axis for axis in range(3) if vector[axis]]
        if len(used) == 1:
            axis = used[0]
            means[1 + axis, number] = 0.5
            means[7 + axis, number] = 0.5 * vector[axis]
        elif len(used) == 2:
            pair = AXIS_PAIRS.index(tuple(used))
            one, two = vector[used[0]], vector[used[1]]
            means[4 + pair, number] = 0.25
            means[10 + 2 * pair, number] = 0.25 * one
            means[11 + 2 * pair, number] = 0.25 * two
            means[16 + pair, number] = 0.25 * one * two
    combine = np.zeros((19, 19))
    entries = [
        {0: 1},
        {1: 1, 2: 1, 3: 1},
        {4: 1, 5: 1, 6: 1},
        {1: 2, 2: -1, 3: -1},
        {4: 1, 5: 1, 6: -2},
        {2: 1, 3: -1},
        {4: 1, 5: -1},
        {7: 1},
        {10: 1, 12: 1},
        {10: 1, 12: -1},
        {8: 1},
        {11: 1, 14: 1},
        {11: 1, 14: -1},
        {9: 1},
        {13: 1, 15: 1},
        {13: 1, 15: -1},
        {16: 1},
        {17: 1},
        {18: 1},
    ]
    for row_number, entry in enumerate(entries):
        for column, factor in entry.items():
            combine[row_number, column] = factor
    scale = np.array(
        [1, 1 / 3, 1 / 3, 1 / 6, 1 / 6, 0.5, 0.5]
        + [1, 0.5, 0.5] * 3
        + [1, 1, 1]
    )
    to_symmetric = combine @ means
    back = np.linalg.inv(to_symmetric)
    terms = {}
    for rate in range(19):
        part = (
            scale[:, None]
            * to_symmetric
            @ np.diag(1.0 / weights)
            @ np.outer(basis[rate], basis[rate])
            @ np.diag(weights)
            @ back
        )
        for row_number in range(19):
            for column in range(19):
                if abs(part[row_number, column]) > 1e-9:
                    terms.setdefault((row_number, column), []).append(
                        (rate, float(part[row_number, column]))
                    )
    return terms


TERMS = relaxation_terms()
ENTRY = {where: number for number, where in enumerate(sorted(TERMS))}


def to_means(value):
    mean = [None] * 19
    mean[0] = value[0]
    for axis in range(3):
        ahead, behind = value[1 + 2 * axis], value[2 + 2 * axis]
        mean[1 + axis] = 0.5 * (ahead + behind)
        mean[7 + axis] = 0.5 * (ahead - behind)
    for pair in range(3):
        pp, pm, mp, mm = value[7 + 4 * pair : 11 + 4 * pair]
        even_one, odd_one = (pp + mm), (pp - mm)
        even_two, odd_two = (pm + mp), (pm - mp)
        mean[4 + pair] = 0.25 * (even_one + even_two)
        mean[16 + pair] = 0.25 * (even_one - even_two)
        mean[10 + 2 * pair] = 0.25 * (odd_one + odd_two)
        mean[11 + 2 * pair] = 0.25 * (odd_one - odd_two)
    return mean


def from_means(mean):
    value = [None] * 19
    value[0] = mean[0]
    for axis in range(3):
        value[1 + 2 * axis] = mean[1 + axis] + mean[7 + axis]
        value[2 + 2 * axis] = mean[1 + axis] - mean[7 + axis]
    for pair in range(3):
        even_one = mean[4 + pair] + mean[16 + pair]
        even_two = mean[4 + pair] - mean[16 + pair]
        odd_one = mean[10 + 2 * pair] + mean[11 + 2 * pair]
        odd_two = mean[10 + 2 * pair] - mean[11 + 2 * pair]
        value[7 + 4 * pair] = even_one + odd_one
        value[8 + 4 * pair] = even_two + odd_two
        value[9 + 4 * pair] = even_two - odd_two
        value[10 + 4 * pair] = even_one - odd_one
    return value


def equilibrium_means(density, impulse, triple):
    half = [0.5 * part for part in triple]
    square = [impulse[axis] * half[axis] for axis in range(3)]
    rest = density - (square[0] + square[1] + square[2]) * (1.0 / 3.0)
    axes = [rest + square[axis] for axis in range(3)]
    mean = [rest] + axes
    mean += [axes[one] + square[two] for one, two in AXIS_PAIRS]
    mean += list(impulse)
    for one, two in AXIS_PAIRS:
        mean += [impulse[one], impulse[two]]
    mean += [impulse[one] * triple[two] for one, two in AXIS_PAIRS]
    return mean


def relax_means(off, coefficient):
    plus = [None] * 19
    plus[0] = off[0]
    pair_sum = off[2] + off[3]
    plus[1] = off[1] + pair_sum
    plus[3] = off[1] + off[1] - pair_sum
    plus[5] = off[2] - off[3]
    pair_sum = off[4] + off[5]
    plus[2] = pair_sum + off[6]
    plus[4] = pair_sum - (off[6] + off[6])
    plus[6] = off[4] - off[5]
    for axis, (one, two) in enumerate(((10, 12), (11, 14), (13, 15))):
        plus[7 + 3 * axis] = off[7 + axis]
        plus[8 + 3 * axis] = off[one] + off[two]
        plus[9 + 3 * axis] = off[one] - off[two]
    plus[16:19] = off[16:19]
    made = []
    for row_number in range(19):
        total = None
        for column in range(19):
            if (row_number, column) in ENTRY:
                term = coefficient(ENTRY[row_number, column]) * plus[column]
                total = term if total is None else total + term
        made.append(total)
    out = [None] * 19
    out[0] = made[0]
    lower = made[1] - made[3]
    out[1] = made[1] + (made[3] + made[3])
    out[2] = lower + made[5]
    out[3] = lower - made[5]
    upper = made[2] + made[4]
    out[4] = upper + made[6]
    out[5] = upper - made[6]
    out[6] = made[2] - (made[4] + made[4])
    for axis, (one, two) in enumerate(((10, 12), (11, 14), (13, 15))):
        out[7 + axis] = made[7 + 3 * axis]
        out[one] = made[8 + 3 * axis] + made[9 + 3 * axis]
        out[two] = made[8 + 3 * axis] - made[9 + 3 * axis]
    out[16:19] = made[16:19]
    return out


def fluid_part(value, coefficient):
    mean = to_means(value)
    ninth, third = 1.0 / 9.0, 1.0 / 3.0
    density = mean[0] * third + (
        (mean[1] + mean[2]) + (mean[3] + mean[4]) + (mean[5] + mean[6])
    ) * ninth
    impulse = [
        (mean[7 + axis] + (mean[one] + mean[two])) * third
        for axis, (one, two) in enumerate(((10, 12), (11, 14), (13, 15)))
    ]
    inverse = 1.0 / density
    triple = [part * inverse for part in impulse]
    fluid = equilibrium_means(density, impulse, triple)
    off = [mean[number] - fluid[number] for number in range(19)]
    relaxed = relax_means(off, coefficient)
    return density, [mean[number] - relaxed[number] for number in range(19)], off


def solid_part(density, kept, off, solid, solid_triple):
    wall = equilibrium_means(density, [density * part for part in solid_triple], solid_triple)
    share = 1.0 - solid
    post = []
    for number in range(19):
        odd = 7 <= number < 16
        bounced = wall[number] - off[number] if odd else wall[number] + off[number]
        post.append(share * kept[number] + solid * bounced)
    return from_means(post)


def main_kernel(
    sizes, rates_hbm, velocity_hbm, change_hbm, fractions_hbm, anchor_hbm, destination_hbm,
    populations, result,
    rates, velocity, change, fractions, anchor, destination,
    start, ahead, sent1, sent2, coef, payload, outbox, inbox, values, spread, across, solids,
    rows_out, rows_in, ends_out, ends_in,
    fetch_sem, load_sem, mail_send, mail_recv, halo_send, halo_recv,
):
    size_x, size_y, size_z, table = sizes
    tiles = size_y // 8
    me_x, me_y = lax.axis_index("gx"), lax.axis_index("gy")
    count_x, count_y = lax.axis_size("gx"), lax.axis_size("gy")

    def there(side):
        return side[1] == 0 or (me_y < count_y - 1 if side[1] > 0 else me_y > 0)

    def device(side):
        return (lax.rem(me_x + side[0] + count_x, count_x), me_y + side[1])

    def when_there(side, act):
        if side[1] == 0:
            act()
        else:
            pl.when(there(side))(act)

    inbox[...] = jnp.zeros_like(inbox)
    barrier = pltpu.get_barrier_semaphore()
    def far(side):
        return -2 * abs(side[0]) - abs(side[1])

    for side in sorted(SIDES, key=far):
        def greet(side=side):
            pl.semaphore_signal(barrier, inc=1, device_id=device(side), device_id_type=MESH)
        when_there(side, greet)

    fetches = [
        pltpu.make_async_copy(source, target, fetch_sem.at[number])
        for number, (source, target) in enumerate(
            (
                (destination_hbm, destination),
                (anchor_hbm, anchor),
                (velocity_hbm, velocity),
                (change_hbm, change),
                (fractions_hbm, fractions),
                (rates_hbm, rates),
            )
        )
    ]
    for fetch in fetches:
        fetch.start()
    load = pltpu.make_async_copy(populations, start, load_sem)
    load.start()

    payload[...] = jnp.zeros_like(payload)
    outbox[...] = jnp.zeros_like(outbox)
    for fetch in fetches:
        fetch.wait()
    place = anchor[...]
    place_x = lax.shift_right_logical(place, 13)
    place_y = lax.bitwise_and(lax.shift_right_logical(place, 8), 31)
    place_z = lax.bitwise_and(place, 255)
    moved = velocity[...] + change[...]
    payload[0:3, :] = moved
    payload[3:4, :] = place_x.astype(F32)
    payload[4:5, :] = place_y.astype(F32)
    payload[5:6, :] = place_z.astype(F32)
    for plane in range(3):
        payload[8 + 16 * plane : 17 + 16 * plane, :] = fractions[9 * plane : 9 * plane + 9, :]
    code = destination[...]
    row = lax.broadcasted_iota(jnp.int32, (64, table), 0)
    group = lax.shift_right_logical(row, 3)
    wanted = group + jnp.where(group >= 4, 1, 0)
    matches = jnp.broadcast_to(code, (64, table)) == wanted
    chosen = jnp.where(matches, 1.0, 0.0)
    earlier = jnp.where(
        lax.broadcasted_iota(jnp.int32, (table, table), 0)
        <= lax.broadcasted_iota(jnp.int32, (table, table), 1),
        1.0,
        0.0,
    ).astype(BF16)
    ranks = jnp.dot(chosen.astype(BF16), earlier, preferred_element_type=F32)
    rank_of_row = (lax.bitwise_and(row, 7) + 1).astype(F32)
    picked = jnp.where(ranks == rank_of_row, chosen, 0.0).astype(BF16)
    whole = payload[...]
    high = whole.astype(BF16)
    rest = whole - high.astype(F32)
    middle = rest.astype(BF16)
    low = (rest - middle.astype(F32)).astype(BF16)
    contract = (((1,), (1,)), ((), ()))
    packed = lax.dot_general(picked, high, contract, preferred_element_type=F32)
    packed += lax.dot_general(picked, middle, contract, preferred_element_type=F32)
    packed += lax.dot_general(picked, low, contract, preferred_element_type=F32)
    for number in range(8):
        outbox[number, :, 0:56] = packed[8 * number : 8 * number + 8, :]

    inside = jnp.logical_and(me_y > 0, me_y < count_y - 1)
    pl.when(inside)(lambda: pl.semaphore_wait(barrier, 8))
    pl.when(jnp.logical_not(inside))(lambda: pl.semaphore_wait(barrier, 5))

    def mail(number):
        return pltpu.make_async_remote_copy(
            src_ref=outbox.at[number],
            dst_ref=inbox.at[number],
            send_sem=mail_send.at[number],
            recv_sem=mail_recv.at[number],
            device_id=device(SIDES[number]),
            device_id_type=MESH,
        )

    for number in sorted(range(8), key=lambda number: far(SIDES[number])):
        when_there(SIDES[number], lambda number=number: mail(number).start())

    for where, number in ENTRY.items():
        total = None
        for rate, factor in TERMS[where]:
            term = rates[rate] * factor
            total = term if total is None else total + term
        coef[number] = jnp.full((8, 128), total, F32)

    ENDMOST, MIDDLE = (0, size_x - 1), tuple(range(1, size_x - 1))
    turned = {x: number for number, x in enumerate(ENDMOST + MIDDLE)}
    block = 4 * size_y

    def rows_of(x, c, tile):
        number = turned[x] if isinstance(x, int) else x + 1
        return pl.ds(pl.multiple_of(number * block + c * size_y + tile * 8, 8), 8)

    def prepare(many, at_y, at_z):
        along_y = lax.broadcasted_iota(jnp.int32, (size_y, many), 0).astype(F32)
        along_z = lax.broadcasted_iota(jnp.int32, (size_z, many), 0).astype(F32)
        for dz in range(3):
            across[:, dz * many : dz * many + many] = jnp.where(
                along_z == at_z + (dz - 1.0), 1.0, 0.0
            ).astype(BF16)
        return [
            jnp.where(along_y == at_y + (dy - 1.0), 1.0, 0.0).astype(BF16) for dy in range(3)
        ]

    def deposit(many, at_x, ones_y, speeds, planes, twice, xs):
        left = lax.broadcasted_iota(jnp.int32, (1, many), 1) < many // 2
        first = at_x == 1.0
        second = at_x == 2.0
        half = len(xs) * block
        for x in xs:
            near = jnp.where(first, planes[x], 0.0) if x < 3 else jnp.zeros_like(planes[0])
            if x >= 1:
                near = jnp.where(second, planes[x - 1], near)
            for c in range(4):
                part = near if c == 0 else near * speeds[c - 1]
                upper = part.astype(BF16).astype(F32)
                if twice:
                    values[0, c, x, 0:9, 0:many] = jnp.where(left, upper, part - upper)
                else:
                    values[0, c, x, 0:9, 0:many] = upper
                    values[1, c, x, 0:9, 0:many] = part - upper
        for dz in range(3):
            for s in range(1 if twice else 2):
                for number, x in enumerate(xs):
                    for c in range(4):
                        total = None
                        for dy in range(3):
                            line = values[s, c, x, 3 * dy + dz : 3 * dy + dz + 1, 0:many]
                            line = jnp.broadcast_to(line, (size_y, many)).astype(BF16)
                            term = ones_y[dy] * line
                            total = term if total is None else total + term
                        base = s * half + number * block + c * size_y
                        spread[base : base + size_y, dz * many : dz * many + many] = total
        both = lax.dot_general(
            spread[0 : half if twice else 2 * half, 0 : 3 * many],
            across[:, 0 : 3 * many],
            contract,
            preferred_element_type=F32,
        )
        return both if twice else both[0:half] + both[half:]

    staying = code == 4
    planes = [
        jnp.where(staying, payload[8 + 16 * plane : 17 + 16 * plane, :], 0.0) for plane in range(3)
    ]
    solids[...] = deposit(
        table,
        payload[3:4, :],
        prepare(table, payload[4:5, :], payload[5:6, :]),
        [payload[axis : axis + 1, :] for axis in range(3)],
        planes,
        False,
        ENDMOST + MIDDLE,
    )

    load.wait()

    @pl.loop(0, size_x * tiles)
    def _(turn):
        x, tile = turn // tiles, turn % tiles
        rows = pl.ds(pl.multiple_of(tile * 8, 8), 8)
        for h in range(2):
            lanes = slice(128 * h, 128 * h + 128)
            density, kept, off = fluid_part(
                [start[number, x, rows, lanes] for number in range(19)], lambda number: coef[number]
            )
            ahead[38, x, h, rows, :] = density
            for number in range(19):
                ahead[number, x, h, rows, :] = kept[number]
                ahead[19 + number, x, h, rows, :] = off[number]

    for number, side in enumerate(SIDES):
        back = (-side[0], -side[1])
        when_there(back, lambda number=number: mail(number).wait_recv())
    letters = inbox[...].reshape(64, 128)
    came = jnp.concatenate([letters, letters], axis=0).T
    came_y = prepare(128, came[4:5, :], came[5:6, :])

    def deposit_came(xs):
        rows = slice(turned[xs[0]] * block, (turned[xs[-1]] + 1) * block)
        solids[rows, :] += deposit(
            128,
            came[3:4, :],
            came_y,
            [came[axis : axis + 1, :] for axis in range(3)],
            [came[8 + 16 * plane : 17 + 16 * plane, :] for plane in range(3)],
            True,
            xs,
        )

    deposit_came(ENDMOST)
    lane = lax.broadcasted_iota(jnp.int32, (8, 128), 1)

    def rolled(halves, shift):
        turned = [pltpu.roll(half, shift % 128, 1) for half in halves]
        edge = lane == (0 if shift == 1 else 127)
        return [jnp.where(edge, turned[1 - h], turned[h]) for h in range(2)]

    def chunk(step, x, tile):
        out = sent1 if step == 0 else sent2
        rows = pl.ds(pl.multiple_of(tile * 8 + PAD, 8), 8)
        for h in range(2):
            lanes = slice(128 * h, 128 * h + 128)
            whole_rows = [rows_of(x, c, tile) for c in range(4)]
            fields = [solids[whole_rows[c], lanes] for c in range(4)]
            if step == 0:
                own = pl.ds(pl.multiple_of(tile * 8, 8), 8)
                parts = [ahead[number, x, h, own, :] for number in range(39)]
                density, kept, off = parts[38], parts[0:19], parts[19:38]
                inverse = 3.0 / (fields[0] + 1e-06)
                solid = jnp.minimum(fields[0], 1.0)
                triple = [fields[1 + axis] * inverse for axis in range(3)]
                solids[whole_rows[0], lanes] = solid
                for axis in range(3):
                    solids[whole_rows[1 + axis], lanes] = triple[axis]
            else:
                value = [
                    sent1[
                        SLOT[number],
                        x + (1 - VEL[number][0]),
                        h,
                        pl.ds(tile * 8 + (PAD - VEL[number][1]), 8),
                        :,
                    ]
                    for number in range(19)
                ]
                solid, triple = fields[0], fields[1:]
                density, kept, off = fluid_part(value, lambda number: coef[number])
            post = solid_part(density, kept, off, solid, triple)
            for number in range(19):
                shift = VEL[number][2]
                if shift:
                    turned_post = pltpu.roll(post[number], shift % 128, 1)
                    edge = lane == (0 if shift == 1 else 127)
                    pltpu.store(
                        out.at[SLOT[number], x + 1, h, rows, :], turned_post, mask=jnp.logical_not(edge)
                    )
                    pltpu.store(
                        out.at[SLOT[number], x + 1, 1 - h, rows, :], turned_post, mask=edge
                    )
                else:
                    out[SLOT[number], x + 1, h, rows, :] = post[number]

    def sweep(step, places):
        def body(turn, carry):
            chunk(step, *places(turn))
            return carry

        return body

    rims = lambda turn: (1 + turn // 2, (turn % 2) * (tiles - 1))
    inner = lambda turn: (1 + turn // (tiles - 2), 1 + turn % (tiles - 2))

    def side_of(kind, number):
        if kind == "x":
            return ((1, 0), (-1, 0))[number]
        if kind == "y":
            return ((0, 1), (0, -1))[number]
        return ((1, 1), (-1, 1), (1, -1), (-1, -1))[number]

    def halo(step, kind, number, piece=0):
        out = sent1 if step == 0 else sent2
        side = side_of(kind, number)
        if kind == "x":
            rows = pl.ds(pl.multiple_of(PAD + 8 * piece, 8), 8)
            source = out.at[pl.ds(5 * number, 5), size_x if number == 0 else 1, :, rows, :]
            target = out.at[pl.ds(5 * number, 5), 0 if number == 0 else size_x + 1, :, rows, :]
            sem = 6 + number * tiles + piece
        elif kind == "y":
            source, target = rows_out.at[step, number], rows_in.at[step, number]
            sem = number
        else:
            source, target = ends_out.at[step, number], ends_in.at[step, number]
            sem = 2 + number
        return pltpu.make_async_remote_copy(
            src_ref=source,
            dst_ref=target,
            send_sem=halo_send.at[step, sem],
            recv_sem=halo_recv.at[step, sem],
            device_id=device(side),
            device_id_type=MESH,
        )

    ROWS = [("y", 0), ("y", 1)]
    ENDS = [("e", number) for number in range(4)]
    ENDS_UP, ENDS_DOWN = ENDS[:2], ENDS[2:]

    def begin(step, halos):
        for kind, number in halos:
            when_there(
                side_of(kind, number),
                lambda kind=kind, number=number: halo(step, kind, number).start(),
            )

    def arrive(step, halos):
        for kind, number in halos:
            side = side_of(kind, number)
            when_there(
                (-side[0], -side[1]),
                lambda kind=kind, number=number: halo(step, kind, number).wait_recv(),
            )

    def face_arrive(step, piece):
        for number in range(2):
            halo(step, "x", number, piece).wait_recv()

    def stage_rows(step):
        out = sent1 if step == 0 else sent2
        for number, (kinds, row) in enumerate(((UP, PAD + size_y - 1), (DOWN, PAD))):
            for order, one in enumerate(kinds):
                for x in range(size_x):
                    for h in range(2):
                        at = (order * size_x + x) * 2 + h
                        rows_out[step, number, at : at + 1, :] = out[
                            SLOT[one], x + 1, h, row : row + 1, :
                        ]

    def stage_ends(step, halos):
        out = sent1 if step == 0 else sent2
        for kind, number in halos:
            side_x, side_y = side_of(kind, number)
            one = INDEX[side_x, side_y, 0]
            row = PAD + size_y - 1 if side_y == 1 else PAD
            x = size_x if side_x == 1 else 1
            for h in range(2):
                ends_out[step, number, h : h + 1, :] = out[SLOT[one], x, h, row : row + 1, :]

    def fill_rows(step):
        out = sent1 if step == 0 else sent2
        for number, (kinds, sign) in enumerate(((UP, 1), (DOWN, -1))):
            to_row = PAD - 1 if sign == 1 else PAD + size_y
            own_tile = PAD if sign == 1 else PAD + size_y - 8
            own_row = 0 if sign == 1 else 7

            def from_neighbour(number=number, kinds=kinds, to_row=to_row):
                for order, one in enumerate(kinds):
                    for x in range(size_x):
                        for h in range(2):
                            at = (order * size_x + x) * 2 + h
                            out[SLOT[one], x + 1, h, to_row : to_row + 1, :] = rows_in[
                                step, number, at : at + 1, :
                            ]

            def from_wall(kinds=kinds, to_row=to_row, own_tile=own_tile, own_row=own_row):
                for one in kinds:
                    for x in range(size_x):
                        halves = [
                            out[SLOT[OPP[one]], x + 1, h, own_tile : own_tile + 8, :]
                            for h in range(2)
                        ]
                        if VEL[one][2]:
                            halves = rolled(halves, VEL[one][2])
                        for h in range(2):
                            out[SLOT[one], x + 1 - VEL[one][0], h, to_row : to_row + 1, :] = (
                                halves[h][own_row : own_row + 1, :]
                            )

            wall = me_y == 0 if sign == 1 else me_y == count_y - 1
            pl.when(wall)(from_wall)
            pl.when(jnp.logical_not(wall))(from_neighbour)

    def fill_ends(step):
        out = sent1 if step == 0 else sent2
        for number, (side_x, side_y) in enumerate(((1, 1), (-1, 1), (1, -1), (-1, -1))):
            one = INDEX[side_x, side_y, 0]
            to_row = PAD - 1 if side_y == 1 else PAD + size_y
            to_x = 0 if side_x == 1 else size_x + 1

            def copy_in(number=number, one=one, to_row=to_row, to_x=to_x):
                for h in range(2):
                    out[SLOT[one], to_x, h, to_row : to_row + 1, :] = ends_in[
                        step, number, h : h + 1, :
                    ]

            when_there((-side_x, -side_y), copy_in)

    def final(number, x, tiles_of):
        for h in range(2):
            for tile in tiles_of:
                result[number, x, 8 * tile : 8 * tile + 8, 128 * h : 128 * h + 128] = sent2[
                    SLOT[number],
                    x + 1 - VEL[number][0],
                    h,
                    8 * tile + PAD - VEL[number][1] : 8 * tile + PAD - VEL[number][1] + 8,
                    :,
                ]

    def finish(part):
        for number in range(19):
            for x in range(size_x):
                inside_x = 0 <= x - VEL[number][0] < size_x
                needs_row = {1: 0, -1: tiles - 1}.get(VEL[number][1])
                if part == "faces":
                    final(number, x, () if inside_x else range(tiles))
                elif inside_x:
                    final(number, x, [t for t in range(tiles) if (t == needs_row) == (part == "rows")])

    def edges(step, tile, halos=()):
        chunk(step, size_x - 1, tile)
        halo(step, "x", 0, tile).start()
        chunk(step, 0, tile)
        stage_ends(step, halos)
        begin(step, halos)
        halo(step, "x", 1, tile).start()

    edges(0, 0, ENDS_DOWN)
    edges(0, tiles - 1, ENDS_UP)
    deposit_came(MIDDLE)

    lax.fori_loop(0, 4, sweep(0, rims), 0)
    stage_rows(0)
    begin(0, ROWS)

    @pl.loop(1, tiles - 1)
    def _(turn):
        edges(0, turn)

    lax.fori_loop(0, 2 * (tiles - 2), sweep(0, inner), 0)
    lax.fori_loop(0, 2 * (tiles - 2), sweep(1, inner), 0)
    arrive(0, ROWS)
    fill_rows(0)
    arrive(0, ENDS)
    fill_ends(0)
    face_arrive(0, 0)
    face_arrive(0, 1)
    edges(1, 0, ENDS_DOWN)
    for piece in range(2, tiles):
        face_arrive(0, piece)
    edges(1, tiles - 1, ENDS_UP)
    lax.fori_loop(0, 4, sweep(1, rims), 0)
    stage_rows(1)
    begin(1, ROWS)

    @pl.loop(1, tiles - 1)
    def _(turn):
        edges(1, turn)

    finish("own")
    arrive(1, ROWS)
    fill_rows(1)
    finish("rows")
    for piece in range(tiles):
        face_arrive(1, piece)
    arrive(1, ENDS)
    fill_ends(1)
    finish("faces")
    for number, side in enumerate(SIDES):
        when_there(side, lambda number=number: mail(number).wait_send())
    for step in range(2):
        for kind, number in ROWS + ENDS:
            when_there(
                side_of(kind, number),
                lambda step=step, kind=kind, number=number: halo(step, kind, number).wait_send(),
            )
        for number in range(2):
            for piece in range(tiles):
                halo(step, "x", number, piece).wait_send()


def local(populations, relax_rates, velocity, velocity_change, fractions, anchor, destination):
    size_x, size_y, size_z = populations.shape[1:]
    table = anchor.shape[0]
    padded = (19, size_x + 2, 2, size_y + 2 * PAD, 128)
    hbm = pl.BlockSpec(memory_space=pltpu.HBM)
    rows = 5 * size_x * 2
    halos = 6 + 2 * (size_y // 8)
    return pl.pallas_call(
        functools.partial(main_kernel, (size_x, size_y, size_z, table)),
        out_shape=pltpu.VMEM(populations.shape, F32),
        in_specs=[hbm] * 7,
        out_specs=pl.BlockSpec(memory_space=pltpu.VMEM),
        scratch_shapes=[
            pltpu.SMEM((19,), F32),
            pltpu.VMEM((3, table), F32),
            pltpu.VMEM((3, table), F32),
            pltpu.VMEM((27, table), F32),
            pltpu.VMEM((1, table), jnp.int32),
            pltpu.VMEM((1, table), jnp.int32),
            pltpu.VMEM((19, size_x, size_y, size_z), F32),
            pltpu.VMEM((39, size_x, 2, size_y, 128), F32),
            pltpu.VMEM(padded, F32),
            pltpu.VMEM(padded, F32),
            pltpu.VMEM((len(ENTRY), 8, 128), F32),
            pltpu.VMEM((56, table), F32),
            pltpu.VMEM((8, 8, 128), F32),
            pltpu.VMEM((8, 8, 128), F32),
            pltpu.VMEM((2, 4, size_x, 16, table), F32),
            pltpu.VMEM((8 * size_x * size_y, 3 * table), BF16),
            pltpu.VMEM((size_z, 3 * table), BF16),
            pltpu.VMEM((4 * size_x * size_y, size_z), F32),
            pltpu.VMEM((2, 2, rows, 128), F32),
            pltpu.VMEM((2, 2, rows, 128), F32),
            pltpu.VMEM((2, 4, 2, 128), F32),
            pltpu.VMEM((2, 4, 2, 128), F32),
            pltpu.SemaphoreType.DMA((6,)),
            pltpu.SemaphoreType.DMA,
            pltpu.SemaphoreType.DMA((8,)),
            pltpu.SemaphoreType.DMA((8,)),
            pltpu.SemaphoreType.DMA((2, halos)),
            pltpu.SemaphoreType.DMA((2, halos)),
        ],
        compiler_params=pltpu.CompilerParams(
            collective_id=0, has_side_effects=True, vmem_limit_bytes=48 * 1024 * 1024
        ),
    )(
        *(
            pltpu.with_memory_space_constraint(operand, pltpu.HBM)
            for operand in (
                relax_rates,
                velocity,
                velocity_change,
                fractions,
                anchor.reshape(1, table),
                destination.reshape(1, table),
                populations,
            )
        )
    )


def solution(mesh):
    placed = (
        P(None, "gx", "gy", None),
        P(),
        P(None, ("gx", "gy")),
        P(None, ("gx", "gy")),
        P(None, ("gx", "gy")),
        P(("gx", "gy")),
        P(("gx", "gy")),
    )
    return jax.shard_map(
        local, mesh=mesh, in_specs=placed, out_specs=P(None, "gx", "gy", None), check_vma=False
    )
```

```python
import functools

import jax
import jax.numpy as jnp
import numpy as np
from jax import lax
from jax.experimental import pallas as pl
from jax.experimental.pallas import tpu as pltpu
from jax.sharding import PartitionSpec as P

CAP = 4
MESH = pl.DeviceIdType.MESH
F32 = jnp.float32
BF16 = jnp.bfloat16
AXIS_PAIRS = ((0, 1), (0, 2), (1, 2))
SIDES = ((-1, -1), (-1, 0), (-1, 1), (0, -1), (0, 1), (1, -1), (1, 0), (1, 1))
PAD = 8


def lattice():
    vectors = [(0, 0, 0)]
    for axis_one in range(3):
        for orient in (1, -1):
            vector_one = [0, 0, 0]
            vector_one[axis_one] = orient
            vectors.append(tuple(vector_one))
    for axis_one, axis_two in AXIS_PAIRS:
        for orient in (1, -1):
            for second in (1, -1):
                vector_one = [0, 0, 0]
                vector_one[axis_one] = orient
                vector_one[axis_two] = second
                vectors.append(tuple(vector_one))
    return vectors


VEL = lattice()
INDEX = {vector: number for number, vector in enumerate(VEL)}
OPP = [INDEX[tuple(-part for part in vector)] for vector in VEL]
PLACES = (
    [number for number in range(19) if VEL[number][0] == 1]
    + [number for number in range(19) if VEL[number][0] == -1]
    + [number for number in range(19) if VEL[number][0] == 0]
)
SLOT = {number: place for place, number in enumerate(PLACES)}
UP = [number for number in range(19) if VEL[number][1] == 1]
DOWN = [number for number in range(19) if VEL[number][1] == -1]


def relaxation_terms():
    speeds = np.array(VEL) * 1.0
    length = (speeds**2).sum(axis=1)
    weights = np.where(length == 0, 1.0 / 3.0, np.where(length == 1, 1.0 / 18.0, 1.0 / 36.0))
    along_x, along_y, along_z = (speeds[:, 0], speeds[:, 1], speeds[:, 2])
    rows_list = [
        np.ones(19),
        along_x,
        along_y,
        along_z,
        length,
        3 * along_x**2 - length,
        along_y**2 - along_z**2,
        along_x * along_y,
        along_y * along_z,
        along_x * along_z,
        along_x * length,
        along_y * length,
        along_z * length,
        along_x * (along_y**2 - along_z**2),
        along_y * (along_z**2 - along_x**2),
        along_z * (along_x**2 - along_y**2),
        length**2,
        (3 * along_x**2 - length) * length,
        (along_y**2 - along_z**2) * length,
    ]
    basis_rows = []
    for candidate in rows_list:
        for earlier in basis_rows:
            candidate = candidate - np.dot(candidate, earlier) * earlier
        basis_rows.append(candidate / np.sqrt(np.dot(candidate, candidate)))
    basis = np.array(basis_rows)

    means = np.zeros((19, 19))
    means[0, 0] = 1.0
    for number, vector in enumerate(VEL):
        used = [axis for axis in range(3) if vector[axis]]
        if len(used) == 1:
            axis = used[0]
            means[1 + axis, number] = 0.5
            means[7 + axis, number] = 0.5 * vector[axis]
        elif len(used) == 2:
            pair = AXIS_PAIRS.index(tuple(used))
            one, two = vector[used[0]], vector[used[1]]
            means[4 + pair, number] = 0.25
            means[10 + 2 * pair, number] = 0.25 * one
            means[11 + 2 * pair, number] = 0.25 * two
            means[16 + pair, number] = 0.25 * one * two
    combine = np.zeros((19, 19))
    entries = [
        {0: 1},
        {1: 1, 2: 1, 3: 1},
        {4: 1, 5: 1, 6: 1},
        {1: 2, 2: -1, 3: -1},
        {4: 1, 5: 1, 6: -2},
        {2: 1, 3: -1},
        {4: 1, 5: -1},
        {7: 1},
        {10: 1, 12: 1},
        {10: 1, 12: -1},
        {8: 1},
        {11: 1, 14: 1},
        {11: 1, 14: -1},
        {9: 1},
        {13: 1, 15: 1},
        {13: 1, 15: -1},
        {16: 1},
        {17: 1},
        {18: 1},
    ]
    for row_number, entry in enumerate(entries):
        for column, factor in entry.items():
            combine[row_number, column] = factor
    scale = np.array(
        [1, 1 / 3, 1 / 3, 1 / 6, 1 / 6, 0.5, 0.5]
        + [1, 0.5, 0.5] * 3
        + [1, 1, 1]
    )
    to_symmetric = combine @ means
    back = np.linalg.inv(to_symmetric)
    terms = {}
    for rate in range(19):
        part = (
            scale[:, None]
            * to_symmetric
            @ np.diag(1.0 / weights)
            @ np.outer(basis[rate], basis[rate])
            @ np.diag(weights)
            @ back
        )
        for row_number in range(19):
            for column in range(19):
                if abs(part[row_number, column]) > 1e-9:
                    terms.setdefault((row_number, column), []).append(
                        (rate, float(part[row_number, column]))
                    )
    return terms


TERMS = relaxation_terms()
ENTRY = {where: number for number, where in enumerate(sorted(TERMS))}


def to_means(value):
    mean = [None] * 19
    mean[0] = value[0]
    for axis in range(3):
        ahead, behind = value[1 + 2 * axis], value[2 + 2 * axis]
        mean[1 + axis] = 0.5 * (ahead + behind)
        mean[7 + axis] = 0.5 * (ahead - behind)
    for pair in range(3):
        pp, pm, mp, mm = value[7 + 4 * pair : 11 + 4 * pair]
        even_one, odd_one = (pp + mm), (pp - mm)
        even_two, odd_two = (pm + mp), (pm - mp)
        mean[4 + pair] = 0.25 * (even_one + even_two)
        mean[16 + pair] = 0.25 * (even_one - even_two)
        mean[10 + 2 * pair] = 0.25 * (odd_one + odd_two)
        mean[11 + 2 * pair] = 0.25 * (odd_one - odd_two)
    return mean


def from_means(mean):
    value = [None] * 19
    value[0] = mean[0]
    for axis in range(3):
        value[1 + 2 * axis] = mean[1 + axis] + mean[7 + axis]
        value[2 + 2 * axis] = mean[1 + axis] - mean[7 + axis]
    for pair in range(3):
        even_one = mean[4 + pair] + mean[16 + pair]
        even_two = mean[4 + pair] - mean[16 + pair]
        odd_one = mean[10 + 2 * pair] + mean[11 + 2 * pair]
        odd_two = mean[10 + 2 * pair] - mean[11 + 2 * pair]
        value[7 + 4 * pair] = even_one + odd_one
        value[8 + 4 * pair] = even_two + odd_two
        value[9 + 4 * pair] = even_two - odd_two
        value[10 + 4 * pair] = even_one - odd_one
    return value


def equilibrium_means(density, impulse, triple):
    half = [0.5 * part for part in triple]
    square = [impulse[axis] * half[axis] for axis in range(3)]
    rest = density - (square[0] + square[1] + square[2]) * (1.0 / 3.0)
    axes = [rest + square[axis] for axis in range(3)]
    mean = [rest] + axes
    mean += [axes[one] + square[two] for one, two in AXIS_PAIRS]
    mean += list(impulse)
    for one, two in AXIS_PAIRS:
        mean += [impulse[one], impulse[two]]
    mean += [impulse[one] * triple[two] for one, two in AXIS_PAIRS]
    return mean


def relax_means(off, coefficient):
    plus = [None] * 19
    plus[0] = off[0]
    pair_sum = off[2] + off[3]
    plus[1] = off[1] + pair_sum
    plus[3] = off[1] + off[1] - pair_sum
    plus[5] = off[2] - off[3]
    pair_sum = off[4] + off[5]
    plus[2] = pair_sum + off[6]
    plus[4] = pair_sum - (off[6] + off[6])
    plus[6] = off[4] - off[5]
    for axis, (one, two) in enumerate(((10, 12), (11, 14), (13, 15))):
        plus[7 + 3 * axis] = off[7 + axis]
        plus[8 + 3 * axis] = off[one] + off[two]
        plus[9 + 3 * axis] = off[one] - off[two]
    plus[16:19] = off[16:19]
    made = []
    for row_number in range(19):
        total = None
        for column in range(19):
            if (row_number, column) in ENTRY:
                term = coefficient(ENTRY[row_number, column]) * plus[column]
                total = term if total is None else total + term
        made.append(total)
    out = [None] * 19
    out[0] = made[0]
    lower = made[1] - made[3]
    out[1] = made[1] + (made[3] + made[3])
    out[2] = lower + made[5]
    out[3] = lower - made[5]
    upper = made[2] + made[4]
    out[4] = upper + made[6]
    out[5] = upper - made[6]
    out[6] = made[2] - (made[4] + made[4])
    for axis, (one, two) in enumerate(((10, 12), (11, 14), (13, 15))):
        out[7 + axis] = made[7 + 3 * axis]
        out[one] = made[8 + 3 * axis] + made[9 + 3 * axis]
        out[two] = made[8 + 3 * axis] - made[9 + 3 * axis]
    out[16:19] = made[16:19]
    return out


def fluid_part(value, coefficient):
    mean = to_means(value)
    ninth, third = 1.0 / 9.0, 1.0 / 3.0
    density = mean[0] * third + (
        (mean[1] + mean[2]) + (mean[3] + mean[4]) + (mean[5] + mean[6])
    ) * ninth
    impulse = [
        (mean[7 + axis] + (mean[one] + mean[two])) * third
        for axis, (one, two) in enumerate(((10, 12), (11, 14), (13, 15)))
    ]
    inverse = 1.0 / density
    triple = [part * inverse for part in impulse]
    fluid = equilibrium_means(density, impulse, triple)
    off = [mean[number] - fluid[number] for number in range(19)]
    relaxed = relax_means(off, coefficient)
    return density, [mean[number] - relaxed[number] for number in range(19)], off


def solid_part(density, kept, off, solid, solid_triple):
    wall = equilibrium_means(density, [density * part for part in solid_triple], solid_triple)
    share = 1.0 - solid
    post = []
    for number in range(19):
        odd = 7 <= number < 16
        bounced = wall[number] - off[number] if odd else wall[number] + off[number]
        post.append(share * kept[number] + solid * bounced)
    return from_means(post)


def main_kernel(
    sizes, rates_hbm, velocity_hbm, change_hbm, fractions_hbm, anchor_hbm, destination_hbm,
    populations, result,
    rates, velocity, change, fractions, anchor, destination,
    start, ahead, sent1, sent2, coef, payload, outbox, inbox, values, spread, across, solids,
    rows_out, rows_in, ends_out, ends_in,
    fetch_sem, load_sem, mail_send, mail_recv, halo_send, halo_recv,
):
    size_x, size_y, size_z, table = sizes
    tiles = size_y // 8
    me_x, me_y = lax.axis_index("gx"), lax.axis_index("gy")
    count_x, count_y = lax.axis_size("gx"), lax.axis_size("gy")

    def there(side):
        return side[1] == 0 or (me_y < count_y - 1 if side[1] > 0 else me_y > 0)

    def device(side):
        return (lax.rem(me_x + side[0] + count_x, count_x), me_y + side[1])

    def when_there(side, act):
        if side[1] == 0:
            act()
        else:
            pl.when(there(side))(act)

    inbox[...] = jnp.zeros_like(inbox)
    barrier = pltpu.get_barrier_semaphore()
    def far(side):
        return -2 * abs(side[0]) - abs(side[1])

    for side in sorted(SIDES, key=far):
        def greet(side=side):
            pl.semaphore_signal(barrier, inc=1, device_id=device(side), device_id_type=MESH)
        when_there(side, greet)

    fetches = [
        pltpu.make_async_copy(source, target, fetch_sem.at[number])
        for number, (source, target) in enumerate(
            (
                (destination_hbm, destination),
                (anchor_hbm, anchor),
                (velocity_hbm, velocity),
                (change_hbm, change),
                (fractions_hbm, fractions),
                (rates_hbm, rates),
            )
        )
    ]
    for fetch in fetches:
        fetch.start()

    payload[...] = jnp.zeros_like(payload)
    outbox[...] = jnp.zeros_like(outbox)
    for fetch in fetches:
        fetch.wait()
    load = pltpu.make_async_copy(populations, start, load_sem)
    load.start()
    place = anchor[...]
    place_x = lax.shift_right_logical(place, 13)
    place_y = lax.bitwise_and(lax.shift_right_logical(place, 8), 31)
    place_z = lax.bitwise_and(place, 255)
    moved = velocity[...] + change[...]
    payload[0:3, :] = moved
    payload[3:4, :] = place_x.astype(F32)
    payload[4:5, :] = place_y.astype(F32)
    payload[5:6, :] = place_z.astype(F32)
    for plane in range(3):
        payload[8 + 16 * plane : 17 + 16 * plane, :] = fractions[9 * plane : 9 * plane + 9, :]
    code = destination[...]
    row = lax.broadcasted_iota(jnp.int32, (64, table), 0)
    group = lax.shift_right_logical(row, 3)
    wanted = group + jnp.where(group >= 4, 1, 0)
    matches = jnp.broadcast_to(code, (64, table)) == wanted
    chosen = jnp.where(matches, 1.0, 0.0)
    earlier = jnp.where(
        lax.broadcasted_iota(jnp.int32, (table, table), 0)
        <= lax.broadcasted_iota(jnp.int32, (table, table), 1),
        1.0,
        0.0,
    ).astype(BF16)
    ranks = jnp.dot(chosen.astype(BF16), earlier, preferred_element_type=F32)
    rank_of_row = (lax.bitwise_and(row, 7) + 1).astype(F32)
    picked = jnp.where(ranks == rank_of_row, chosen, 0.0).astype(BF16)
    whole = payload[...]
    high = whole.astype(BF16)
    rest = whole - high.astype(F32)
    middle = rest.astype(BF16)
    low = (rest - middle.astype(F32)).astype(BF16)
    contract = (((1,), (1,)), ((), ()))
    packed = lax.dot_general(picked, high, contract, preferred_element_type=F32)
    packed += lax.dot_general(picked, middle, contract, preferred_element_type=F32)
    packed += lax.dot_general(picked, low, contract, preferred_element_type=F32)
    for number in range(8):
        outbox[number, :, 0:56] = packed[8 * number : 8 * number + 8, :]

    inside = jnp.logical_and(me_y > 0, me_y < count_y - 1)
    pl.when(inside)(lambda: pl.semaphore_wait(barrier, 8))
    pl.when(jnp.logical_not(inside))(lambda: pl.semaphore_wait(barrier, 5))

    def mail(number):
        return pltpu.make_async_remote_copy(
            src_ref=outbox.at[number],
            dst_ref=inbox.at[number],
            send_sem=mail_send.at[number],
            recv_sem=mail_recv.at[number],
            device_id=device(SIDES[number]),
            device_id_type=MESH,
        )

    for number in sorted(range(8), key=lambda number: far(SIDES[number])):
        when_there(SIDES[number], lambda number=number: mail(number).start())

    for where, number in ENTRY.items():
        total = None
        for rate, factor in TERMS[where]:
            term = rates[rate] * factor
            total = term if total is None else total + term
        coef[number] = jnp.full((8, 128), total, F32)

    ENDMOST, MIDDLE = (0, size_x - 1), tuple(range(1, size_x - 1))
    turned = {x: number for number, x in enumerate(ENDMOST + MIDDLE)}
    block = 4 * size_y

    def rows_of(x, c, tile):
        number = turned[x] if isinstance(x, int) else x + 1
        return pl.ds(pl.multiple_of(number * block + c * size_y + tile * 8, 8), 8)

    def prepare(many, at_y, at_z):
        along_y = lax.broadcasted_iota(jnp.int32, (size_y, many), 0).astype(F32)
        along_z = lax.broadcasted_iota(jnp.int32, (size_z, many), 0).astype(F32)
        for dz in range(3):
            across[:, dz * many : dz * many + many] = jnp.where(
                along_z == at_z + (dz - 1.0), 1.0, 0.0
            ).astype(BF16)
        return [
            jnp.where(along_y == at_y + (dy - 1.0), 1.0, 0.0).astype(BF16) for dy in range(3)
        ]

    def deposit(many, at_x, ones_y, speeds, planes, twice, xs):
        left = lax.broadcasted_iota(jnp.int32, (1, many), 1) < many // 2
        first = at_x == 1.0
        second = at_x == 2.0
        half = len(xs) * block
        for x in xs:
            near = jnp.where(first, planes[x], 0.0) if x < 3 else jnp.zeros_like(planes[0])
            if x >= 1:
                near = jnp.where(second, planes[x - 1], near)
            for c in range(4):
                part = near if c == 0 else near * speeds[c - 1]
                upper = part.astype(BF16).astype(F32)
                if twice:
                    values[0, c, x, 0:9, 0:many] = jnp.where(left, upper, part - upper)
                else:
                    values[0, c, x, 0:9, 0:many] = upper
                    values[1, c, x, 0:9, 0:many] = part - upper
        for dz in range(3):
            for s in range(1 if twice else 2):
                for number, x in enumerate(xs):
                    for c in range(4):
                        total = None
                        for dy in range(3):
                            line = values[s, c, x, 3 * dy + dz : 3 * dy + dz + 1, 0:many]
                            line = jnp.broadcast_to(line, (size_y, many)).astype(BF16)
                            term = ones_y[dy] * line
                            total = term if total is None else total + term
                        base = s * half + number * block + c * size_y
                        spread[base : base + size_y, dz * many : dz * many + many] = total
        both = lax.dot_general(
            spread[0 : half if twice else 2 * half, 0 : 3 * many],
            across[:, 0 : 3 * many],
            contract,
            preferred_element_type=F32,
        )
        return both if twice else both[0:half] + both[half:]

    staying = code == 4
    planes = [
        jnp.where(staying, payload[8 + 16 * plane : 17 + 16 * plane, :], 0.0) for plane in range(3)
    ]
    solids[...] = deposit(
        table,
        payload[3:4, :],
        prepare(table, payload[4:5, :], payload[5:6, :]),
        [payload[axis : axis + 1, :] for axis in range(3)],
        planes,
        False,
        ENDMOST + MIDDLE,
    )

    load.wait()

    @pl.loop(0, size_x * tiles)
    def _(turn):
        x, tile = turn // tiles, turn % tiles
        rows = pl.ds(pl.multiple_of(tile * 8, 8), 8)
        for h in range(2):
            lanes = slice(128 * h, 128 * h + 128)
            density, kept, off = fluid_part(
                [start[number, x, rows, lanes] for number in range(19)], lambda number: coef[number]
            )
            ahead[38, x, h, rows, :] = density
            for number in range(19):
                ahead[number, x, h, rows, :] = kept[number]
                ahead[19 + number, x, h, rows, :] = off[number]

    for number, side in enumerate(SIDES):
        back = (-side[0], -side[1])
        when_there(back, lambda number=number: mail(number).wait_recv())
    letters = inbox[...].reshape(64, 128)
    came = jnp.concatenate([letters, letters], axis=0).T
    came_y = prepare(128, came[4:5, :], came[5:6, :])

    def deposit_came(xs):
        rows = slice(turned[xs[0]] * block, (turned[xs[-1]] + 1) * block)
        solids[rows, :] += deposit(
            128,
            came[3:4, :],
            came_y,
            [came[axis : axis + 1, :] for axis in range(3)],
            [came[8 + 16 * plane : 17 + 16 * plane, :] for plane in range(3)],
            True,
            xs,
        )

    deposit_came(ENDMOST)
    lane = lax.broadcasted_iota(jnp.int32, (8, 128), 1)

    def rolled(halves, shift):
        turned = [pltpu.roll(half, shift % 128, 1) for half in halves]
        edge = lane == (0 if shift == 1 else 127)
        return [jnp.where(edge, turned[1 - h], turned[h]) for h in range(2)]

    def chunk(step, x, tile):
        out = sent1 if step == 0 else sent2
        rows = pl.ds(pl.multiple_of(tile * 8 + PAD, 8), 8)
        for h in range(2):
            lanes = slice(128 * h, 128 * h + 128)
            whole_rows = [rows_of(x, c, tile) for c in range(4)]
            fields = [solids[whole_rows[c], lanes] for c in range(4)]
            if step == 0:
                own = pl.ds(pl.multiple_of(tile * 8, 8), 8)
                parts = [ahead[number, x, h, own, :] for number in range(39)]
                density, kept, off = parts[38], parts[0:19], parts[19:38]
                inverse = 3.0 / (fields[0] + 1e-06)
                solid = jnp.minimum(fields[0], 1.0)
                triple = [fields[1 + axis] * inverse for axis in range(3)]
                solids[whole_rows[0], lanes] = solid
                for axis in range(3):
                    solids[whole_rows[1 + axis], lanes] = triple[axis]
            else:
                value = [
                    sent1[
                        SLOT[number],
                        x + (1 - VEL[number][0]),
                        h,
                        pl.ds(tile * 8 + (PAD - VEL[number][1]), 8),
                        :,
                    ]
                    for number in range(19)
                ]
                solid, triple = fields[0], fields[1:]
                density, kept, off = fluid_part(value, lambda number: coef[number])
            post = solid_part(density, kept, off, solid, triple)
            for number in range(19):
                shift = VEL[number][2]
                if shift:
                    turned_post = pltpu.roll(post[number], shift % 128, 1)
                    edge = lane == (0 if shift == 1 else 127)
                    pltpu.store(
                        out.at[SLOT[number], x + 1, h, rows, :], turned_post, mask=jnp.logical_not(edge)
                    )
                    pltpu.store(
                        out.at[SLOT[number], x + 1, 1 - h, rows, :], turned_post, mask=edge
                    )
                else:
                    out[SLOT[number], x + 1, h, rows, :] = post[number]

    def sweep(step, places):
        def body(turn, carry):
            chunk(step, *places(turn))
            return carry

        return body

    rims = lambda turn: (1 + turn // 2, (turn % 2) * (tiles - 1))
    inner = lambda turn: (1 + turn // (tiles - 2), 1 + turn % (tiles - 2))

    def side_of(kind, number):
        if kind == "x":
            return ((1, 0), (-1, 0))[number]
        if kind == "y":
            return ((0, 1), (0, -1))[number]
        return ((1, 1), (-1, 1), (1, -1), (-1, -1))[number]

    def halo(step, kind, number, piece=0):
        out = sent1 if step == 0 else sent2
        side = side_of(kind, number)
        if kind == "x":
            rows = pl.ds(pl.multiple_of(PAD + 8 * piece, 8), 8)
            source = out.at[pl.ds(5 * number, 5), size_x if number == 0 else 1, :, rows, :]
            target = out.at[pl.ds(5 * number, 5), 0 if number == 0 else size_x + 1, :, rows, :]
            sem = 6 + number * tiles + piece
        elif kind == "y":
            source, target = rows_out.at[step, number], rows_in.at[step, number]
            sem = number
        else:
            source, target = ends_out.at[step, number], ends_in.at[step, number]
            sem = 2 + number
        return pltpu.make_async_remote_copy(
            src_ref=source,
            dst_ref=target,
            send_sem=halo_send.at[step, sem],
            recv_sem=halo_recv.at[step, sem],
            device_id=device(side),
            device_id_type=MESH,
        )

    ROWS = [("y", 0), ("y", 1)]
    ENDS = [("e", number) for number in range(4)]
    ENDS_UP, ENDS_DOWN = ENDS[:2], ENDS[2:]

    def begin(step, halos):
        for kind, number in halos:
            when_there(
                side_of(kind, number),
                lambda kind=kind, number=number: halo(step, kind, number).start(),
            )

    def arrive(step, halos):
        for kind, number in halos:
            side = side_of(kind, number)
            when_there(
                (-side[0], -side[1]),
                lambda kind=kind, number=number: halo(step, kind, number).wait_recv(),
            )

    def face_begin(step, piece):
        for number in range(2):
            halo(step, "x", number, piece).start()

    def face_arrive(step, piece):
        for number in range(2):
            halo(step, "x", number, piece).wait_recv()

    def stage_rows(step):
        out = sent1 if step == 0 else sent2
        for number, (kinds, row) in enumerate(((UP, PAD + size_y - 1), (DOWN, PAD))):
            for order, one in enumerate(kinds):
                for x in range(size_x):
                    for h in range(2):
                        at = (order * size_x + x) * 2 + h
                        rows_out[step, number, at : at + 1, :] = out[
                            SLOT[one], x + 1, h, row : row + 1, :
                        ]

    def stage_ends(step, halos):
        out = sent1 if step == 0 else sent2
        for kind, number in halos:
            side_x, side_y = side_of(kind, number)
            one = INDEX[side_x, side_y, 0]
            row = PAD + size_y - 1 if side_y == 1 else PAD
            x = size_x if side_x == 1 else 1
            for h in range(2):
                ends_out[step, number, h : h + 1, :] = out[SLOT[one], x, h, row : row + 1, :]

    def fill_rows(step):
        out = sent1 if step == 0 else sent2
        for number, (kinds, sign) in enumerate(((UP, 1), (DOWN, -1))):
            to_row = PAD - 1 if sign == 1 else PAD + size_y
            own_tile = PAD if sign == 1 else PAD + size_y - 8
            own_row = 0 if sign == 1 else 7

            def from_neighbour(number=number, kinds=kinds, to_row=to_row):
                for order, one in enumerate(kinds):
                    for x in range(size_x):
                        for h in range(2):
                            at = (order * size_x + x) * 2 + h
                            out[SLOT[one], x + 1, h, to_row : to_row + 1, :] = rows_in[
                                step, number, at : at + 1, :
                            ]

            def from_wall(kinds=kinds, to_row=to_row, own_tile=own_tile, own_row=own_row):
                for one in kinds:
                    for x in range(size_x):
                        halves = [
                            out[SLOT[OPP[one]], x + 1, h, own_tile : own_tile + 8, :]
                            for h in range(2)
                        ]
                        if VEL[one][2]:
                            halves = rolled(halves, VEL[one][2])
                        for h in range(2):
                            out[SLOT[one], x + 1 - VEL[one][0], h, to_row : to_row + 1, :] = (
                                halves[h][own_row : own_row + 1, :]
                            )

            wall = me_y == 0 if sign == 1 else me_y == count_y - 1
            pl.when(wall)(from_wall)
            pl.when(jnp.logical_not(wall))(from_neighbour)

    def fill_ends(step):
        out = sent1 if step == 0 else sent2
        for number, (side_x, side_y) in enumerate(((1, 1), (-1, 1), (1, -1), (-1, -1))):
            one = INDEX[side_x, side_y, 0]
            to_row = PAD - 1 if side_y == 1 else PAD + size_y
            to_x = 0 if side_x == 1 else size_x + 1

            def copy_in(number=number, one=one, to_row=to_row, to_x=to_x):
                for h in range(2):
                    out[SLOT[one], to_x, h, to_row : to_row + 1, :] = ends_in[
                        step, number, h : h + 1, :
                    ]

            when_there((-side_x, -side_y), copy_in)

    def final(number, x, tiles_of):
        for h in range(2):
            for tile in tiles_of:
                result[number, x, 8 * tile : 8 * tile + 8, 128 * h : 128 * h + 128] = sent2[
                    SLOT[number],
                    x + 1 - VEL[number][0],
                    h,
                    8 * tile + PAD - VEL[number][1] : 8 * tile + PAD - VEL[number][1] + 8,
                    :,
                ]

    def finish(part):
        for number in range(19):
            for x in range(size_x):
                inside_x = 0 <= x - VEL[number][0] < size_x
                needs_row = {1: 0, -1: tiles - 1}.get(VEL[number][1])
                if part == "faces":
                    final(number, x, () if inside_x else range(tiles))
                elif inside_x:
                    final(number, x, [t for t in range(tiles) if (t == needs_row) == (part == "rows")])

    def edges(step, tile, halos=()):
        chunk(step, size_x - 1, tile)
        chunk(step, 0, tile)
        stage_ends(step, halos)
        begin(step, halos)
        face_begin(step, tile)

    edges(0, 0, ENDS_DOWN)
    edges(0, tiles - 1, ENDS_UP)
    deposit_came(MIDDLE)

    lax.fori_loop(0, 4, sweep(0, rims), 0)
    stage_rows(0)
    begin(0, ROWS)

    @pl.loop(1, tiles - 1)
    def _(turn):
        edges(0, turn)

    lax.fori_loop(0, 2 * (tiles - 2), sweep(0, inner), 0)
    lax.fori_loop(0, 2 * (tiles - 2), sweep(1, inner), 0)
    arrive(0, ROWS)
    fill_rows(0)
    arrive(0, ENDS)
    fill_ends(0)
    face_arrive(0, 0)
    face_arrive(0, 1)
    edges(1, 0, ENDS_DOWN)
    for piece in range(2, tiles):
        face_arrive(0, piece)
    edges(1, tiles - 1, ENDS_UP)
    lax.fori_loop(0, 4, sweep(1, rims), 0)
    stage_rows(1)
    begin(1, ROWS)

    @pl.loop(1, tiles - 1)
    def _(turn):
        edges(1, turn)

    finish("own")
    arrive(1, ROWS)
    fill_rows(1)
    finish("rows")
    for piece in range(tiles):
        face_arrive(1, piece)
    arrive(1, ENDS)
    fill_ends(1)
    finish("faces")
    for number, side in enumerate(SIDES):
        when_there(side, lambda number=number: mail(number).wait_send())
    for step in range(2):
        for kind, number in ROWS + ENDS:
            when_there(
                side_of(kind, number),
                lambda step=step, kind=kind, number=number: halo(step, kind, number).wait_send(),
            )
        for number in range(2):
            for piece in range(tiles):
                halo(step, "x", number, piece).wait_send()


def local(populations, relax_rates, velocity, velocity_change, fractions, anchor, destination):
    size_x, size_y, size_z = populations.shape[1:]
    table = anchor.shape[0]
    padded = (19, size_x + 2, 2, size_y + 2 * PAD, 128)
    hbm = pl.BlockSpec(memory_space=pltpu.HBM)
    rows = 5 * size_x * 2
    halos = 6 + 2 * (size_y // 8)
    return pl.pallas_call(
        functools.partial(main_kernel, (size_x, size_y, size_z, table)),
        out_shape=pltpu.VMEM(populations.shape, F32),
        in_specs=[hbm] * 7,
        out_specs=pl.BlockSpec(memory_space=pltpu.VMEM),
        scratch_shapes=[
            pltpu.SMEM((19,), F32),
            pltpu.VMEM((3, table), F32),
            pltpu.VMEM((3, table), F32),
            pltpu.VMEM((27, table), F32),
            pltpu.VMEM((1, table), jnp.int32),
            pltpu.VMEM((1, table), jnp.int32),
            pltpu.VMEM((19, size_x, size_y, size_z), F32),
            pltpu.VMEM((39, size_x, 2, size_y, 128), F32),
            pltpu.VMEM(padded, F32),
            pltpu.VMEM(padded, F32),
            pltpu.VMEM((len(ENTRY), 8, 128), F32),
            pltpu.VMEM((56, table), F32),
            pltpu.VMEM((8, 8, 128), F32),
            pltpu.VMEM((8, 8, 128), F32),
            pltpu.VMEM((2, 4, size_x, 16, table), F32),
            pltpu.VMEM((8 * size_x * size_y, 3 * table), BF16),
            pltpu.VMEM((size_z, 3 * table), BF16),
            pltpu.VMEM((4 * size_x * size_y, size_z), F32),
            pltpu.VMEM((2, 2, rows, 128), F32),
            pltpu.VMEM((2, 2, rows, 128), F32),
            pltpu.VMEM((2, 4, 2, 128), F32),
            pltpu.VMEM((2, 4, 2, 128), F32),
            pltpu.SemaphoreType.DMA((6,)),
            pltpu.SemaphoreType.DMA,
            pltpu.SemaphoreType.DMA((8,)),
            pltpu.SemaphoreType.DMA((8,)),
            pltpu.SemaphoreType.DMA((2, halos)),
            pltpu.SemaphoreType.DMA((2, halos)),
        ],
        compiler_params=pltpu.CompilerParams(
            collective_id=0, has_side_effects=True, vmem_limit_bytes=48 * 1024 * 1024
        ),
    )(
        *(
            pltpu.with_memory_space_constraint(operand, pltpu.HBM)
            for operand in (
                relax_rates,
                velocity,
                velocity_change,
                fractions,
                anchor.reshape(1, table),
                destination.reshape(1, table),
                populations,
            )
        )
    )


def solution(mesh):
    placed = (
        P(None, "gx", "gy", None),
        P(),
        P(None, ("gx", "gy")),
        P(None, ("gx", "gy")),
        P(None, ("gx", "gy")),
        P(("gx", "gy")),
        P(("gx", "gy")),
    )
    return jax.shard_map(
        local, mesh=mesh, in_specs=placed, out_specs=P(None, "gx", "gy", None), check_vma=False
    )
```
